512 devices in a mesh: grp: 16 (over y, x), tok: 32 (over z, core).
Axes of the slice: x: 4, y: 4, z: 16, core: 2. Of those that a mesh axis runs over, the one named last changes fastest.
Arguments:
- hidden_in: bfloat16 [16, 4096, 1024], P('grp', 'tok'), may hold values from -6 to 6
- lengths: int32 [16, 3], P('grp'), may hold values from 1 to 3072, 4096 in all within a row
- prefix_cache: bfloat16 [16, 512, 512], P('grp', 'tok'), may hold values from -2600 to 2600
- routes: int32 [16, 4096, 8], P('grp', 'tok'), may hold values from 0 to 31, all different within a row; in each aligned block of 128 rows (0 to 127, 128 to 255, ..., all dimensions but the last counted through in order) at most 40 rows name the same one
- gates: float32 [16, 4096, 8], P('grp', 'tok'), may hold values from 0.05 to 0.4
- attn_gain: float32 [1024], replicated, may hold values from 0.1 to 1.9
- w_qkv: bfloat16 [1024, 1024], P('grp', 'tok'), may hold values from -0.75 to 0.75
- w_out: bfloat16 [512, 1024], P('grp', 'tok'), may hold values from -0.25 to 0.25
- moe_gain: float32 [1024], replicated, may hold values from 0.1 to 1.9
- expert_gate_up: bfloat16 [32, 1024, 1024], P('tok', 'grp'), may hold values from -0.1875 to 0.1875
- expert_down: bfloat16 [32, 512, 1024], P('tok', 'grp'), may hold values from -0.25 to 0.25
Outputs:
- hidden_out: bfloat16 [16, 4096, 1024], P('grp', 'tok')
- suffix_cache: bfloat16 [16, 4096, 512], P('grp', 'tok')
The draws below stay inside these ranges and needn't reach their ends.
Inputs may be any that keep to these rules, and one draw needn't show every extreme that they name: Each group's 3 lengths sum to 4096; no request is longer than 3072 tokens, and some request of every draw has exactly 3072. `routes`: each token names 8 different experts. Among the 128 tokens of one device no expert is named more than 40 times, a bound that some block reaches.
All inputs are finite; a program needn't handle non-finite values.
Results may differ from the reference program's by a relative error of at most 0.02.
Values may be sent and summed in bfloat16 or wider, within the bound.
A program may use at most 128 MiB of HBM per device.

```python
import math
import jax
import jax.numpy as jnp
import numpy as np
from jax import lax

D = 1024
HEADS = 8
KV_HEADS = 4
HEAD_DIM = 64
FF = 512
EXPERTS = 32
TOP = 8
REQS = 3
TOK_DEV = 128
GROUPS = 16
TOK_GRP = 4096
PREFIX = 512
MAXLEN = 3072
CAP = 40
N_TOK = 32


def draw_prefix_cache(key, part):
    base_key = jax.random.fold_in(key, 0)
    key_width = KV_HEADS * HEAD_DIM
    shape_full = (GROUPS, PREFIX, 2 * key_width)
    cache = 4.0 * jnp.clip(jax.random.normal(base_key, shape_full, jnp.float32), -6.0, 6.0)
    return cache.astype(jnp.bfloat16)


def steps_of(key, dims, shards, smallest, high):
    def one(dim, parts):
        heights = jax.random.uniform(jax.random.fold_in(jax.random.fold_in(key, 6), dim), (parts,), jnp.float32, smallest / len(shards), high / len(shards))
        return jnp.repeat(jnp.exp(heights), dims[dim] // parts).reshape((-1,) + (1,) * (len(dims) - dim - 1))

    level = one(*shards[0])
    for cut in shards[1:]:
        level = level * one(*cut)
    return level


def profile(number_of, total, limit, lean):
    loads = [(1 << 20) // math.isqrt(standing ** lean) + 1 for standing in range(2, number_of + 1)]
    spare, counts = total - limit - (number_of - 1), [1] * (number_of - 1)
    while spare > 0:
        free = [i for i in range(number_of - 1) if counts[i] < limit]
        pool, left = sum([loads[i] for i in free]), spare
        for i in free:
            addition = min(limit - counts[i], max(1, left * loads[i] // pool), spare)
            counts[i] = counts[i] + addition
            spare = spare - addition
    return np.array([limit] + counts)


def ragged_sizes(rng, number_of, total, reach, slope):
    if number_of == 2:
        one = jax.random.randint(rng, (), max(1, total - reach), min(reach, total - 1) + 1)
        return jnp.stack([one, total - one])
    sizes = jnp.asarray(profile(number_of, total, reach, slope), jnp.int32)
    couples = (number_of - 1) // 2
    source_of, taker = sizes[1:1 + 2 * couples:2], sizes[2:2 + 2 * couples:2]
    room = jnp.minimum(source_of - 1, reach - taker)
    moved = jax.random.randint(jax.random.fold_in(rng, 1), (couples,), 0, 1 << 20) % (room + 1)
    sizes = sizes.at[1:1 + 2 * couples:2].set(source_of - moved).at[2:2 + 2 * couples:2].set(taker + moved)
    return sizes[jax.random.permutation(jax.random.fold_in(rng, 2), number_of)]


def assign_block(key, own, number, rows, number_of, top, limit, slope):
    order = jax.random.permutation(key, number_of)
    crowded, ordinary = shares(number_of, rows * top, limit, slope, True), shares(number_of, rows * top, limit, slope, False)
    places = jnp.arange(number_of)

    def named(sizes, rotation):
        used = int((sizes > 0).sum())
        fixed = max(1, used // 4)
        shifted = fixed + (places - fixed + rotation * (used - fixed)) % max(1, number_of - fixed)
        return jnp.zeros((number_of,), jnp.int32).at[order[jnp.where(places < fixed, places, shifted)]].set(jnp.asarray(sizes, jnp.int32))

    sizes = jnp.where(number % 4 == 0, named(crowded, number // 4), named(ordinary, number - number // 4 - 1))
    mixed = jax.random.permutation(jax.random.fold_in(own, 3), number_of)
    source_of, receiver = mixed[0:number_of // 2 * 2:2], mixed[1:number_of // 2 * 2:2]
    slack = jnp.minimum(sizes[source_of] - 1, limit - sizes[receiver]) // 2
    slack = jnp.where((source_of == order[0]) | (receiver == order[0]) | (sizes[receiver] == 0), 0, jnp.maximum(slack, 0))
    shifted = jax.random.randint(jax.random.fold_in(own, 4), (number_of // 2,), 0, 1 << 20) % (slack + 1)
    sizes = sizes.at[source_of].add(-shifted).at[receiver].add(shifted)
    labels = jnp.searchsorted(jnp.cumsum(sizes), jnp.arange(rows * top), side="right").astype(jnp.int32)
    grid = labels.reshape(top, rows).T
    grid = grid[jax.random.permutation(jax.random.fold_in(own, 1), rows)]
    rotation = jax.random.randint(jax.random.fold_in(own, 2), (rows, 1), 0, top)
    return jnp.take_along_axis(grid, (jnp.arange(top)[None, :] + rotation) % top, axis=1)


def shares(count, total, bound, skew, full):
    loads = [(1 << 20) // math.isqrt(rank ** skew) + 1 for rank in range(1, count + 1)]
    largest = bound if full else min(bound, max(-(-total // count), total * loads[0] // sum(loads)))
    least = 1 if total - largest >= count - 1 else 0
    counts, spare = [largest] + [least] * (count - 1), total - largest - least * (count - 1)
    while spare > 0:
        free = [i for i in range(1, count) if counts[i] < largest] or [i for i in range(1, count) if counts[i] < bound]
        whole, budget = sum([loads[i] for i in free]), spare
        for i in free:
            addition = min(bound - counts[i], max(1, budget * loads[i] // whole), spare)
            counts[i] = counts[i] + addition
            spare = spare - addition
    return np.array(counts)


def bell_draw(own_key, extent, scale, most, shards=(), kind=jnp.bfloat16):
    values = scale * jax.random.normal(own_key, extent, jnp.float32)
    if shards:
        values = values * steps_of(own_key, extent, shards, -0.22, 0.18)
    return jnp.clip(values, -most, most).astype(kind)


def setup_inputs(seed: int = 0) -> dict:
    keys = jax.random.split(jax.random.key(seed), 12)
    hidden_in = bell_draw(keys[0], (GROUPS, TOK_GRP, D), 1.0, 6.0, ((0, 16), (1, 32)))
    lengths = jax.vmap(lambda own: ragged_sizes(own, REQS, TOK_GRP, MAXLEN, 2))(jax.random.split(keys[1], GROUPS)).reshape((GROUPS, REQS)).astype(jnp.int32)
    prefix_cache = draw_prefix_cache(jax.random.fold_in(keys[11], 71), 0)
    routes_keys = jax.random.split(jax.random.fold_in(keys[3], 1), GROUPS * TOK_GRP // TOK_DEV)
    routes_turns = jax.random.permutation(jax.random.fold_in(keys[3], 3), GROUPS * TOK_GRP // TOK_DEV)
    routes = jax.vmap(lambda own, number: assign_block(jax.random.fold_in(keys[3], 2), own, number, TOK_DEV, EXPERTS, TOP, CAP, 1))(routes_keys, routes_turns).reshape((GROUPS, TOK_GRP, TOP))
    gates = jnp.clip(jnp.exp(math.log(0.4) - 2.0794415 * jax.random.uniform(keys[4], (GROUPS, TOK_GRP, TOP), jnp.float32) ** steps_of(keys[4], (GROUPS, TOK_GRP, TOP), ((0, 16), (1, 32)), -0.2, 0.2)), 0.05, 0.4)
    attn_gain = jnp.clip(1.0 + 0.18 * jax.random.normal(keys[5], (D,), jnp.float32), 0.1, 1.9)
    w_qkv = bell_draw(keys[6], (D, (HEADS + 2 * KV_HEADS) * HEAD_DIM), (D // 16) ** -0.5, 0.75, ((0, 16), (1, 32)))
    w_out = bell_draw(keys[7], (HEADS * HEAD_DIM, D), (HEADS * HEAD_DIM) ** -0.5, 0.25, ((0, 16), (1, 32)))
    moe_gain = jnp.clip(1.0 + 0.18 * jax.random.normal(keys[8], (D,), jnp.float32), 0.1, 1.9)
    expert_gate_up = bell_draw(keys[9], (EXPERTS, D, 2 * FF), D ** -0.5, 0.1875, ((0, 32), (1, 16)))
    expert_down = bell_draw(keys[10], (EXPERTS, FF, D), FF ** -0.5, 0.25, ((0, 32), (1, 16)))
    return {"hidden_in": hidden_in, "lengths": lengths, "prefix_cache": prefix_cache, "routes": routes, "gates": gates, "attn_gain": attn_gain, "w_qkv": w_qkv, "w_out": w_out, "moe_gain": moe_gain, "expert_gate_up": expert_gate_up, "expert_down": expert_down}


epsilon = 1e-05
score_scale = 0.015625
rope_base = 10000.0
big_negative = -1e+30

def rms_scale(values, gain):
    values = values.astype(jnp.float32)
    mean_square = lax.optimization_barrier(jnp.mean(values * values, axis=-1, keepdims=True))
    return values * lax.rsqrt(mean_square + epsilon) * gain.astype(jnp.float32)

def request_layout(group_lengths, token_index):
    ends = jnp.cumsum(group_lengths).astype(jnp.int32)
    starts = ends - group_lengths
    segment = lax.optimization_barrier(jnp.sum((token_index[:, None] >= ends[None, :]).astype(jnp.int32), axis=1))
    match = segment[:, None] == jnp.arange(group_lengths.shape[0], dtype=jnp.int32)[None, :]
    offset = token_index - lax.optimization_barrier(jnp.sum(jnp.where(match, starts[None, :], 0), axis=1))
    return (segment, offset.astype(jnp.int32))

def rotate(values, position):
    half_width = values.shape[-1] // 2
    frequency = rope_base ** (-jnp.arange(half_width, dtype=jnp.float32) * 2.0 / values.shape[-1])
    angle = position.astype(jnp.float32)[:, None] * frequency[None, :]
    cosine = jnp.cos(angle)[:, None, :]
    sine = jnp.sin(angle)[:, None, :]
    first = values[..., :half_width]
    second = values[..., half_width:]
    return jnp.concatenate([first * cosine - second * sine, second * cosine + first * sine], axis=-1)

def rounded_f32(values):
    return lax.optimization_barrier(values.astype(jnp.bfloat16)).astype(jnp.float32)

def group_attention(tokens_here, group_lengths, prefix, attn_gain, w_qkv, w_out, moe_gain):
    tok_count = tokens_here.shape[0]
    key_width = KV_HEADS * HEAD_DIM
    query_width = HEADS * HEAD_DIM
    group_share = HEADS // KV_HEADS
    token_index = jnp.arange(tok_count, dtype=jnp.int32)
    segment, offset = request_layout(group_lengths, token_index)
    position = PREFIX + offset
    normed = rms_scale(tokens_here, attn_gain).astype(jnp.bfloat16)
    projected = jnp.dot(normed, w_qkv, preferred_element_type=jnp.float32)
    query = rotate(projected[:, :query_width].reshape(tok_count, HEADS, HEAD_DIM), position).astype(jnp.bfloat16)
    keys_new = rotate(projected[:, query_width:query_width + key_width].reshape(tok_count, KV_HEADS, HEAD_DIM), position).astype(jnp.bfloat16)
    values_new = projected[:, query_width + key_width:].astype(jnp.bfloat16)
    cache = jnp.concatenate([keys_new.reshape(tok_count, key_width), values_new], axis=1)
    prefix_keys = prefix[:, :key_width].reshape(-1, KV_HEADS, HEAD_DIM).astype(jnp.float32)
    prefix_values = prefix[:, key_width:].reshape(-1, KV_HEADS, HEAD_DIM).astype(jnp.float32)
    suffix_keys = keys_new.astype(jnp.float32)
    suffix_values = values_new.reshape(tok_count, KV_HEADS, HEAD_DIM).astype(jnp.float32)
    block_rows = min(512, tok_count)

    def one_block(first_row):
        block_query = lax.dynamic_slice_in_dim(query, first_row, block_rows, 0).astype(jnp.float32)
        block_query = block_query.reshape(block_rows, KV_HEADS, group_share, HEAD_DIM)
        row_index = lax.dynamic_slice_in_dim(token_index, first_row, block_rows, 0)
        row_segment = lax.dynamic_slice_in_dim(segment, first_row, block_rows, 0)
        allowed = (token_index[None, :] <= row_index[:, None]) & (segment[None, :] == row_segment[:, None])
        mask = allowed[:, None, None, :]
        prefix_scores = jnp.einsum('qkgd,pkd->qkgp', block_query, prefix_keys) * score_scale
        suffix_scores = jnp.einsum('qkgd,tkd->qkgt', block_query, suffix_keys) * score_scale
        best = jnp.maximum(lax.optimization_barrier(jnp.max(prefix_scores, axis=-1)), lax.optimization_barrier(jnp.max(jnp.where(mask, suffix_scores, big_negative), axis=-1)))
        prefix_probs = jnp.exp(prefix_scores - best[..., None])
        suffix_probs = jnp.where(mask, jnp.exp(suffix_scores - best[..., None]), 0.0)
        total = lax.optimization_barrier(jnp.sum(prefix_probs, axis=-1)) + lax.optimization_barrier(jnp.sum(suffix_probs, axis=-1))
        mixed = jnp.einsum('qkgp,pkd->qkgd', rounded_f32(prefix_probs), prefix_values)
        mixed = mixed + jnp.einsum('qkgt,tkd->qkgd', rounded_f32(suffix_probs), suffix_values)
        return (mixed / total[..., None]).reshape(block_rows, query_width).astype(jnp.bfloat16)
    block_starts = jnp.arange(tok_count // block_rows, dtype=jnp.int32) * block_rows
    attended = lax.map(one_block, block_starts).reshape(tok_count, query_width)
    after_attention = tokens_here.astype(jnp.float32) + jnp.dot(attended, w_out, preferred_element_type=jnp.float32)
    moe_in = rms_scale(after_attention, moe_gain).astype(jnp.bfloat16)
    return (after_attention, moe_in, cache)

def expert_apply(expert_rows, gate_up, down):
    hidden_pair = jnp.dot(expert_rows, gate_up, preferred_element_type=jnp.float32)
    activated = (jax.nn.silu(hidden_pair[:, :FF]) * hidden_pair[:, FF:]).astype(jnp.bfloat16)
    return jnp.dot(activated, down, preferred_element_type=jnp.float32).astype(jnp.bfloat16)

def reference(hidden_in, lengths, prefix_cache, routes, gates, attn_gain, w_qkv, w_out, moe_gain, expert_gate_up, expert_down):

    def one_group(group_items):
        tokens_here, group_lengths, prefix = group_items
        return group_attention(tokens_here, group_lengths, prefix, attn_gain, w_qkv, w_out, moe_gain)
    after_attention, moe_in, cache = lax.map(one_group, (hidden_in, lengths, prefix_cache))
    model_width = hidden_in.shape[2]
    flat_moe = moe_in.reshape(-1, model_width)
    flat_routes = routes.reshape(-1).astype(jnp.int32)
    flat_gates = gates.reshape(-1)
    slot_total = GROUPS * N_TOK * CAP

    def one_expert(running, expert_id):
        named = flat_routes == expert_id
        named_count = jnp.sum(named.astype(jnp.int32))
        picked = jnp.nonzero(named, size=slot_total, fill_value=0)[0].astype(jnp.int32)
        valid = jnp.arange(slot_total, dtype=jnp.int32) < named_count
        source_token = picked // TOP
        expert_rows = flat_moe[source_token]
        gate_up = lax.dynamic_index_in_dim(expert_gate_up, expert_id, 0, keepdims=False)
        down = lax.dynamic_index_in_dim(expert_down, expert_id, 0, keepdims=False)
        result = expert_apply(expert_rows, gate_up, down).astype(jnp.float32)
        weight = jnp.where(valid, flat_gates[picked], 0.0)
        return (running.at[source_token].add(weight[:, None] * result), None)
    start_sum = jnp.zeros(flat_moe.shape, jnp.float32)
    moe_out, unused = lax.scan(one_expert, start_sum, jnp.arange(EXPERTS, dtype=jnp.int32))
    hidden_out = (after_attention + moe_out.reshape(after_attention.shape)).astype(jnp.bfloat16)
    return (hidden_out, cache)
```

```python
import jax
import jax.numpy as jnp
from jax import lax
from jax.sharding import PartitionSpec as P

HEADS = 8
KV_HEADS = 4
HEAD_DIM = 64
FF = 512
EXPERTS = 32
TOP = 8
CAP = 40


epsilon = 1e-05
score_scale = 0.015625
rope_base = 10000.0
big_negative = -1e30


def rms_scale(values, gain):
    values = values.astype(jnp.float32)
    mean_square = jnp.mean(values * values, axis=-1, keepdims=True)
    return values * lax.rsqrt(mean_square + epsilon) * gain


def request_layout(group_lengths, token_index):
    ends = jnp.cumsum(group_lengths)
    starts = ends - group_lengths
    segment = jnp.sum((token_index[:, None] >= ends[None, :]).astype(jnp.int32), axis=1)
    match = segment[:, None] == jnp.arange(group_lengths.shape[0], dtype=jnp.int32)[None, :]
    offset = token_index - jnp.sum(jnp.where(match, starts[None, :], 0), axis=1)
    return (segment, offset)


def rotate(values, position):
    half_width = values.shape[-1] // 2
    frequency = rope_base ** (-jnp.arange(half_width, dtype=jnp.float32) * 2.0 / values.shape[-1])
    angle = position.astype(jnp.float32)[:, None] * frequency[None, :]
    cosine = jnp.cos(angle)[:, None, :]
    sine = jnp.sin(angle)[:, None, :]
    first = values[..., :half_width]
    second = values[..., half_width:]
    return jnp.concatenate(
        [first * cosine - second * sine, second * cosine + first * sine], axis=-1
    )


def gather_small(blocks):
    flat = jnp.concatenate([b.reshape(-1) for b in blocks])
    gathered = lax.all_gather(flat[None], "tok", axis=0, tiled=True)
    pieces, start = [], 0
    for b in blocks:
        size = b.size
        pieces.append(gathered[:, start : start + size].reshape((-1,) + b.shape[1:]))
        start += size
    return pieces


def gather_rows(by_columns):
    return lax.all_gather(by_columns[None], "grp", axis=0, tiled=True)


def attend(carry, grouped, keys_values, allowed):
    best, total, mixed = carry
    key_count = keys_values.shape[0]
    key_width = KV_HEADS * HEAD_DIM
    key_heads = keys_values[:, :key_width].reshape(key_count, KV_HEADS, HEAD_DIM).transpose(1, 0, 2)
    value_heads = (
        keys_values[:, key_width:].reshape(key_count, KV_HEADS, HEAD_DIM).transpose(1, 0, 2)
    )
    scores = (
        jnp.einsum("kqd,knd->kqn", grouped, key_heads, preferred_element_type=jnp.float32)
        * score_scale
    )
    if allowed is not None:
        row_count = grouped.shape[1]
        share = row_count // allowed.shape[0]
        mask = jnp.broadcast_to(allowed[:, None, :], (allowed.shape[0], share, key_count)).reshape(
            row_count, key_count
        )
        scores = jnp.where(mask[None], scores, big_negative)
    new_best = jnp.maximum(best, jnp.max(scores, axis=-1))
    factor = jnp.exp(best - new_best)
    probs = jnp.exp(scores - new_best[..., None])
    total = total * factor + jnp.sum(probs, axis=-1)
    mixed = mixed * factor[..., None] + jnp.einsum(
        "kqn,knd->kqd", probs.astype(jnp.bfloat16), value_heads, preferred_element_type=jnp.float32
    )
    return (new_best, total, mixed)


def local(
    hidden_in,
    lengths,
    prefix_cache,
    routes,
    gates,
    attn_gain,
    w_qkv,
    w_out,
    moe_gain,
    expert_gate_up,
    expert_down,
):
    tokens_here = hidden_in[0]
    tok_count = tokens_here.shape[0]
    axis_count = lax.axis_size("tok")
    device_place = lax.axis_index("tok")
    group_lengths = lengths[0]
    token_index = device_place * tok_count + jnp.arange(tok_count, dtype=jnp.int32)
    segment, offset = request_layout(group_lengths, token_index)
    position = prefix_cache.shape[1] * axis_count + offset
    query_width = HEADS * HEAD_DIM
    key_width = KV_HEADS * HEAD_DIM
    group_share = HEADS // KV_HEADS
    normed = rms_scale(tokens_here, attn_gain).astype(jnp.bfloat16)
    qkv_columns, out_columns, prefix_all = gather_small([w_qkv.T, w_out.T, prefix_cache[0]])
    qkv_weight = gather_rows(qkv_columns)
    projected = jnp.einsum(
        "ngr,gcr->nc",
        normed.reshape(tok_count, qkv_weight.shape[0], qkv_weight.shape[2]),
        qkv_weight,
        preferred_element_type=jnp.float32,
    )
    query = rotate(projected[:, :query_width].reshape(tok_count, HEADS, HEAD_DIM), position).astype(
        jnp.bfloat16
    )
    keys_new = rotate(
        projected[:, query_width : query_width + key_width].reshape(tok_count, KV_HEADS, HEAD_DIM),
        position,
    ).astype(jnp.bfloat16)
    values_new = projected[:, query_width + key_width :].astype(jnp.bfloat16)
    suffix_cache = jnp.concatenate([keys_new.reshape(tok_count, key_width), values_new], axis=1)
    row_count = tok_count * group_share
    grouped = (
        query.reshape(tok_count, KV_HEADS, group_share, HEAD_DIM)
        .transpose(1, 0, 2, 3)
        .reshape(KV_HEADS, row_count, HEAD_DIM)
    )
    start_carry = (
        jnp.full((KV_HEADS, row_count), big_negative, jnp.float32),
        jnp.zeros((KV_HEADS, row_count), jnp.float32),
        jnp.zeros((KV_HEADS, row_count, HEAD_DIM), jnp.float32),
    )
    carry = attend(
        start_carry, grouped, prefix_all, None
    )
    piece = lax.all_gather(suffix_cache, "tok", axis=0, tiled=True)
    key_index = jnp.arange(piece.shape[0], dtype=jnp.int32)
    key_segment, key_offset = request_layout(group_lengths, key_index)
    earlier = key_index[None, :] <= token_index[:, None]
    same_request = key_segment[None, :] == segment[:, None]
    carry = attend(carry, grouped, piece, earlier & same_request & (key_index[None, :] >= 0))
    best, total, mixed = carry
    attended = (mixed / total[..., None]).reshape(KV_HEADS, tok_count, group_share, HEAD_DIM)
    attended = attended.transpose(1, 0, 2, 3).reshape(tok_count, query_width).astype(jnp.bfloat16)
    out_weight = gather_rows(out_columns)
    projected_out = jnp.einsum(
        "ngr,gcr->nc",
        attended.reshape(tok_count, out_weight.shape[0], out_weight.shape[2]),
        out_weight,
        preferred_element_type=jnp.float32,
    )
    after_attention = tokens_here.astype(jnp.float32) + projected_out
    moe_in = rms_scale(after_attention, moe_gain).astype(jnp.bfloat16)
    model_width = moe_in.shape[1]
    flat_routes = routes[0].reshape(-1)
    onehot = (flat_routes[:, None] == jnp.arange(EXPERTS, dtype=jnp.int32)[None, :]).astype(
        jnp.int32
    )
    slot_rank = jnp.sum(jnp.cumsum(onehot, axis=0) * onehot, axis=1) - 1
    slot_index = flat_routes * CAP + slot_rank
    source_token = jnp.arange(flat_routes.shape[0], dtype=jnp.int32) // TOP
    outgoing = (
        jnp.zeros((EXPERTS * CAP, model_width), jnp.bfloat16)
        .at[slot_index]
        .set(moe_in[source_token])
    )
    arrived = lax.all_to_all(
        outgoing.reshape(EXPERTS, CAP, model_width), "tok", split_axis=0, concat_axis=0, tiled=True
    ).reshape(1, EXPERTS * CAP, model_width)
    sliced = arrived
    hidden_pair = jnp.einsum(
        "erd,edf->erf",
        sliced,
        lax.all_gather(expert_gate_up, "grp", axis=1, tiled=True),
        preferred_element_type=jnp.float32,
    )
    activated = (jax.nn.silu(hidden_pair[..., :FF]) * hidden_pair[..., FF:]).astype(jnp.bfloat16)
    sliced = activated
    expert_result = jnp.einsum(
        "erf,efd->erd",
        sliced,
        lax.all_gather(expert_down, "grp", axis=1, tiled=True),
        preferred_element_type=jnp.float32,
    ).astype(jnp.bfloat16)
    returned = lax.all_to_all(
        expert_result.reshape(EXPERTS, CAP, model_width), "tok", split_axis=0, concat_axis=0, tiled=True
    ).reshape(EXPERTS * CAP, -1)
    weighted = returned[slot_index].astype(jnp.float32) * gates[0].reshape(-1)[:, None]
    moe_out = jnp.sum(weighted.reshape(tok_count, TOP, -1), axis=1)
    hidden_out = (after_attention + moe_out).astype(jnp.bfloat16)
    return (hidden_out[None], suffix_cache[None])


def solution(mesh):
    return jax.shard_map(
        local,
        mesh=mesh,
        in_specs=(
            P("grp", "tok", None),
            P("grp", None),
            P("grp", "tok", None),
            P("grp", "tok", None),
            P("grp", "tok", None),
            P(),
            P("grp", "tok"),
            P("grp", "tok"),
            P(),
            P("tok", "grp", None),
            P("tok", "grp", None),
        ),
        out_specs=(P("grp", "tok", None), P("grp", "tok", None)),
        check_vma=False,
    )
```

```python
import jax
import jax.numpy as jnp
from jax import lax
from jax.sharding import PartitionSpec as P

HEADS = 8
KV_HEADS = 4
HEAD_DIM = 64
FF = 512
EXPERTS = 32
TOP = 8
CAP = 40


epsilon = 1e-05
score_scale = 0.015625
rope_base = 10000.0
big_negative = -1e30


def rms_scale(values, gain):
    values = values.astype(jnp.float32)
    mean_square = jnp.mean(values * values, axis=-1, keepdims=True)
    return values * lax.rsqrt(mean_square + epsilon) * gain


def request_layout(group_lengths, token_index):
    ends = jnp.cumsum(group_lengths)
    starts = ends - group_lengths
    segment = jnp.sum((token_index[:, None] >= ends[None, :]).astype(jnp.int32), axis=1)
    match = segment[:, None] == jnp.arange(group_lengths.shape[0], dtype=jnp.int32)[None, :]
    offset = token_index - jnp.sum(jnp.where(match, starts[None, :], 0), axis=1)
    return (segment, offset)


def rotate(values, position):
    half_width = values.shape[-1] // 2
    frequency = rope_base ** (-jnp.arange(half_width, dtype=jnp.float32) * 2.0 / values.shape[-1])
    angle = position.astype(jnp.float32)[:, None] * frequency[None, :]
    cosine = jnp.cos(angle)[:, None, :]
    sine = jnp.sin(angle)[:, None, :]
    first = values[..., :half_width]
    second = values[..., half_width:]
    return jnp.concatenate(
        [first * cosine - second * sine, second * cosine + first * sine], axis=-1
    )


def gather_small(blocks):
    flat = jnp.concatenate([b.reshape(-1) for b in blocks])
    gathered = lax.all_gather(flat[None], "tok", axis=0, tiled=True)
    pieces, start = [], 0
    for b in blocks:
        size = b.size
        pieces.append(gathered[:, start : start + size].reshape((-1,) + b.shape[1:]))
        start += size
    return pieces


def gather_rows(by_columns):
    return lax.all_gather(by_columns[None], "grp", axis=0, tiled=True)


def expert_weight_slices(gate_up, down):
    grp_count = lax.axis_size("grp")
    tok_count = lax.axis_size("tok")
    per = tok_count // grp_count
    pairs = []
    for g in range(grp_count):
        for e in range(tok_count):
            pairs.append((g * tok_count + e, (e // per) * tok_count + per * g + e % per))
    block = jnp.concatenate([gate_up[0], down[0]], axis=0)
    return lax.ppermute(block, ("grp", "tok"), pairs)


def expert_weights_full(block, after):
    block, _ = lax.optimization_barrier((block, after))
    grp_count = lax.axis_size("grp")
    tok_count = lax.axis_size("tok")
    gathered = lax.all_gather(block, "tok", axis=0, tiled=True)
    return gathered.reshape(grp_count, tok_count // grp_count, block.shape[0], block.shape[1])


def attend(carry, grouped, keys_values, allowed):
    best, total, mixed = carry
    key_count = keys_values.shape[0]
    key_width = KV_HEADS * HEAD_DIM
    key_heads = keys_values[:, :key_width].reshape(key_count, KV_HEADS, HEAD_DIM).transpose(1, 0, 2)
    value_heads = (
        keys_values[:, key_width:].reshape(key_count, KV_HEADS, HEAD_DIM).transpose(1, 0, 2)
    )
    scores = (
        jnp.einsum("kqd,knd->kqn", grouped, key_heads, preferred_element_type=jnp.float32)
        * score_scale
    )
    if allowed is not None:
        row_count = grouped.shape[1]
        share = row_count // allowed.shape[0]
        mask = jnp.broadcast_to(allowed[:, None, :], (allowed.shape[0], share, key_count)).reshape(
            row_count, key_count
        )
        scores = jnp.where(mask[None], scores, big_negative)
    new_best = jnp.maximum(best, jnp.max(scores, axis=-1))
    factor = jnp.exp(best - new_best)
    probs = jnp.exp(scores - new_best[..., None])
    total = total * factor + jnp.sum(probs, axis=-1)
    mixed = mixed * factor[..., None] + jnp.einsum(
        "kqn,knd->kqd", probs.astype(jnp.bfloat16), value_heads, preferred_element_type=jnp.float32
    )
    return (new_best, total, mixed)


def local(
    hidden_in,
    lengths,
    prefix_cache,
    routes,
    gates,
    attn_gain,
    w_qkv,
    w_out,
    moe_gain,
    expert_gate_up,
    expert_down,
):
    tokens_here = hidden_in[0]
    tok_count = tokens_here.shape[0]
    axis_count = lax.axis_size("tok")
    device_place = lax.axis_index("tok")
    group_lengths = lengths[0]
    token_index = device_place * tok_count + jnp.arange(tok_count, dtype=jnp.int32)
    segment, offset = request_layout(group_lengths, token_index)
    position = prefix_cache.shape[1] * axis_count + offset
    query_width = HEADS * HEAD_DIM
    key_width = KV_HEADS * HEAD_DIM
    group_share = HEADS // KV_HEADS
    normed = rms_scale(tokens_here, attn_gain).astype(jnp.bfloat16)
    qkv_columns, out_columns, prefix_all = gather_small([w_qkv.T, w_out.T, prefix_cache[0]])
    packed_rows = gather_rows(jnp.concatenate([qkv_columns, out_columns], axis=1))
    qkv_width = qkv_columns.shape[1]
    qkv_weight = packed_rows[:, :, :qkv_width]
    out_weight = packed_rows[:, :, qkv_width:]
    expert_weights = expert_weight_slices(expert_gate_up, expert_down)
    projected = jnp.einsum(
        "ngr,gcr->nc",
        normed.reshape(tok_count, qkv_weight.shape[0], qkv_weight.shape[2]),
        qkv_weight,
        preferred_element_type=jnp.float32,
    )
    query = rotate(projected[:, :query_width].reshape(tok_count, HEADS, HEAD_DIM), position).astype(
        jnp.bfloat16
    )
    keys_new = rotate(
        projected[:, query_width : query_width + key_width].reshape(tok_count, KV_HEADS, HEAD_DIM),
        position,
    ).astype(jnp.bfloat16)
    values_new = projected[:, query_width + key_width :].astype(jnp.bfloat16)
    suffix_cache = jnp.concatenate([keys_new.reshape(tok_count, key_width), values_new], axis=1)
    row_count = tok_count * group_share
    grouped = (
        query.reshape(tok_count, KV_HEADS, group_share, HEAD_DIM)
        .transpose(1, 0, 2, 3)
        .reshape(KV_HEADS, row_count, HEAD_DIM)
    )
    start_carry = (
        jnp.full((KV_HEADS, row_count), big_negative, jnp.float32),
        jnp.zeros((KV_HEADS, row_count), jnp.float32),
        jnp.zeros((KV_HEADS, row_count, HEAD_DIM), jnp.float32),
    )
    carry = attend(
        start_carry, grouped, prefix_all, None
    )
    piece = lax.all_gather(suffix_cache, "tok", axis=0, tiled=True)
    key_index = jnp.arange(piece.shape[0], dtype=jnp.int32)
    key_segment, key_offset = request_layout(group_lengths, key_index)
    earlier = key_index[None, :] <= token_index[:, None]
    same_request = key_segment[None, :] == segment[:, None]
    carry = attend(carry, grouped, piece, earlier & same_request & (key_index[None, :] >= 0))
    best, total, mixed = carry
    attended = (mixed / total[..., None]).reshape(KV_HEADS, tok_count, group_share, HEAD_DIM)
    attended = attended.transpose(1, 0, 2, 3).reshape(tok_count, query_width).astype(jnp.bfloat16)
    projected_out = jnp.einsum(
        "ngr,gcr->nc",
        attended.reshape(tok_count, out_weight.shape[0], out_weight.shape[2]),
        out_weight,
        preferred_element_type=jnp.float32,
    )
    after_attention = tokens_here.astype(jnp.float32) + projected_out
    moe_in = rms_scale(after_attention, moe_gain).astype(jnp.bfloat16)
    model_width = moe_in.shape[1]
    flat_routes = routes[0].reshape(-1)
    onehot = (flat_routes[:, None] == jnp.arange(EXPERTS, dtype=jnp.int32)[None, :]).astype(
        jnp.int32
    )
    slot_rank = jnp.sum(jnp.cumsum(onehot, axis=0) * onehot, axis=1) - 1
    slot_index = flat_routes * CAP + slot_rank
    source_token = jnp.arange(flat_routes.shape[0], dtype=jnp.int32) // TOP
    outgoing = (
        jnp.zeros((EXPERTS * CAP, model_width), jnp.bfloat16)
        .at[slot_index]
        .set(moe_in[source_token])
    )
    grp_count = lax.axis_size("grp")
    local_experts = EXPERTS // grp_count
    full = expert_weights_full(expert_weights, piece)
    gate_rows = expert_gate_up.shape[1]
    arrived = lax.all_to_all(
        outgoing.reshape(grp_count, local_experts * CAP, model_width),
        "grp",
        split_axis=0,
        concat_axis=0,
        tiled=True,
    )
    arrived = arrived.reshape(grp_count, local_experts, CAP, model_width).transpose(1, 0, 2, 3)
    arrived = arrived.reshape(local_experts, grp_count * CAP, model_width)
    gate_up_w = full[:, :, :gate_rows].transpose(1, 0, 2, 3).reshape(local_experts, -1, model_width)
    down_w = full[:, :, gate_rows:].transpose(1, 0, 2, 3).reshape(local_experts, -1, model_width)
    hidden_pair = jnp.einsum("erd,edf->erf", arrived, gate_up_w, preferred_element_type=jnp.float32)
    activated = (jax.nn.silu(hidden_pair[..., :FF]) * hidden_pair[..., FF:]).astype(jnp.bfloat16)
    expert_result = jnp.einsum(
        "erf,efd->erd", activated, down_w, preferred_element_type=jnp.float32
    ).astype(jnp.bfloat16)
    expert_result = expert_result.reshape(local_experts, grp_count, CAP, model_width).transpose(1, 0, 2, 3)
    returned = lax.all_to_all(
        expert_result.reshape(grp_count, local_experts * CAP, model_width),
        "grp",
        split_axis=0,
        concat_axis=0,
        tiled=True,
    ).reshape(EXPERTS * CAP, -1)
    weighted = returned[slot_index].astype(jnp.float32) * gates[0].reshape(-1)[:, None]
    moe_out = jnp.sum(weighted.reshape(tok_count, TOP, -1), axis=1)
    hidden_out = (after_attention + moe_out).astype(jnp.bfloat16)
    return (hidden_out[None], suffix_cache[None])


def solution(mesh):
    return jax.shard_map(
        local,
        mesh=mesh,
        in_specs=(
            P("grp", "tok", None),
            P("grp", None),
            P("grp", "tok", None),
            P("grp", "tok", None),
            P("grp", "tok", None),
            P(),
            P("grp", "tok"),
            P("grp", "tok"),
            P(),
            P("tok", "grp", None),
            P("tok", "grp", None),
        ),
        out_specs=(P("grp", "tok", None), P("grp", "tok", None)),
        check_vma=False,
    )
```

```python
import jax
import jax.numpy as jnp
from jax import lax
from jax.sharding import PartitionSpec as P
from jax.experimental import pallas as pl
from jax.experimental.pallas import tpu as pltpu

HEADS = 8
KV_HEADS = 4
HEAD_DIM = 64
FF = 512
EXPERTS = 32
TOP = 8
CAP = 40


epsilon = 1e-05
score_scale = 0.015625
rope_base = 10000.0
big_negative = -1e30


def rms_scale(values, gain):
    values = values.astype(jnp.float32)
    mean_square = jnp.mean(values * values, axis=-1, keepdims=True)
    return values * lax.rsqrt(mean_square + epsilon) * gain


def request_layout(group_lengths, token_index):
    ends = jnp.cumsum(group_lengths)
    starts = ends - group_lengths
    segment = jnp.sum((token_index[:, None] >= ends[None, :]).astype(jnp.int32), axis=1)
    match = segment[:, None] == jnp.arange(group_lengths.shape[0], dtype=jnp.int32)[None, :]
    offset = token_index - jnp.sum(jnp.where(match, starts[None, :], 0), axis=1)
    return (segment, offset)


def rotate(values, position):
    half_width = values.shape[-1] // 2
    frequency = rope_base ** (-jnp.arange(half_width, dtype=jnp.float32) * 2.0 / values.shape[-1])
    angle = position.astype(jnp.float32)[:, None] * frequency[None, :]
    cosine = jnp.cos(angle)[:, None, :]
    sine = jnp.sin(angle)[:, None, :]
    first = values[..., :half_width]
    second = values[..., half_width:]
    return jnp.concatenate(
        [first * cosine - second * sine, second * cosine + first * sine], axis=-1
    )


def ring_gather(block, collective_id):
    tok_count = lax.axis_size("tok")
    rows, width = block.shape
    chips = tok_count // 2
    ahead = chips // 2
    behind = chips - 1 - ahead
    mesh_ids = pl.DeviceIdType.MESH

    def kernel(x_ref, out_ref, local_sem, send_r, send_l, send_p, recv):
        me = lax.axis_index("tok")
        grp = lax.axis_index("grp")
        z = me // 2
        core = me % 2
        right = ((z + 1) % chips) * 2 + core
        left = ((z + chips - 1) % chips) * 2 + core
        peer = z * 2 + (1 - core)
        barrier = pltpu.get_barrier_semaphore()
        for other in (right, left, peer):
            pl.semaphore_signal(barrier, 1, device_id=(grp, other), device_id_type=mesh_ids)
        pl.semaphore_wait(barrier, 3)

        def remote(src, slot, sem, target):
            return pltpu.make_async_remote_copy(
                src_ref=src,
                dst_ref=out_ref.at[slot],
                send_sem=sem,
                recv_sem=recv.at[slot],
                device_id=(grp, target),
                device_id_type=mesh_ids,
            )

        own = pltpu.make_async_copy(x_ref, out_ref.at[me], local_sem.at[0])
        own.start()
        sends = [
            remote(x_ref, me, send_p.at[0], peer),
            remote(x_ref, me, send_r.at[0], right),
            remote(x_ref, me, send_l.at[0], left),
        ]
        for c in sends:
            c.start()
        peer_count = 1
        for s in range(1, ahead + 1):
            for sign, limit, sem, target in ((-1, ahead, send_r, right), (1, behind, send_l, left)):
                if s > limit:
                    continue
                slot = ((z + chips + sign * s) % chips) * 2 + core
                remote(out_ref.at[slot], slot, sem.at[0], target).wait_recv()
                if s < limit:
                    c = remote(out_ref.at[slot], slot, sem.at[s], target)
                    c.start()
                    sends.append(c)
                c = remote(out_ref.at[slot], slot, send_p.at[peer_count], peer)
                c.start()
                sends.append(c)
                peer_count += 1
        for other_z in range(chips):
            slot = other_z * 2 + (1 - core)
            remote(out_ref.at[slot], slot, send_p.at[0], peer).wait_recv()
        own.wait()
        for c in sends:
            c.wait_send()

    block_bytes = rows * width * block.dtype.itemsize
    return pl.pallas_call(
        kernel,
        out_shape=jax.ShapeDtypeStruct((tok_count, rows, width), block.dtype),
        in_specs=[pl.BlockSpec(memory_space=pltpu.VMEM)],
        out_specs=pl.BlockSpec(memory_space=pltpu.VMEM),
        scratch_shapes=[
            pltpu.SemaphoreType.DMA((1,)),
            pltpu.SemaphoreType.DMA((ahead,)),
            pltpu.SemaphoreType.DMA((ahead,)),
            pltpu.SemaphoreType.DMA((chips,)),
            pltpu.SemaphoreType.DMA((tok_count,)),
        ],
        compiler_params=pltpu.CompilerParams(collective_id=collective_id, has_side_effects=True),
        cost_estimate=pl.CostEstimate(
            flops=0, transcendentals=0, bytes_accessed=2 * tok_count * block_bytes
        ),
    )(block)


def gather_small(blocks):
    flat = jnp.concatenate([b.reshape(-1) for b in blocks])
    width = 512
    padded_rows = -(-flat.shape[0] // (16 * width)) * 16
    flat = jnp.pad(flat, (0, padded_rows * width - flat.shape[0]))
    gathered = ring_gather(flat.reshape(padded_rows, width), 1)
    gathered = gathered.reshape(gathered.shape[0], -1)
    pieces, start = [], 0
    for b in blocks:
        size = b.size
        pieces.append(gathered[:, start : start + size].reshape((-1,) + b.shape[1:]))
        start += size
    return pieces


def gather_rows(by_columns):
    return lax.all_gather(by_columns[None], "grp", axis=0, tiled=True)


def expert_weight_slices(gate_up, down):
    grp_count = lax.axis_size("grp")
    tok_count = lax.axis_size("tok")
    per = tok_count // grp_count
    pairs = []
    for g in range(grp_count):
        for e in range(tok_count):
            pairs.append((g * tok_count + e, (e // per) * tok_count + per * g + e % per))
    block = jnp.concatenate([gate_up[0], down[0]], axis=0)
    return lax.ppermute(block, ("grp", "tok"), pairs)


def expert_weights_full(block, after):
    block, _ = lax.optimization_barrier((block, after))
    grp_count = lax.axis_size("grp")
    tok_count = lax.axis_size("tok")
    gathered = lax.all_gather(block, "tok", axis=0, tiled=True)
    return gathered.reshape(grp_count, tok_count // grp_count, block.shape[0], block.shape[1])


def attend(carry, grouped, keys_values, allowed):
    best, total, mixed = carry
    key_count = keys_values.shape[0]
    key_width = KV_HEADS * HEAD_DIM
    key_heads = keys_values[:, :key_width].reshape(key_count, KV_HEADS, HEAD_DIM).transpose(1, 0, 2)
    value_heads = (
        keys_values[:, key_width:].reshape(key_count, KV_HEADS, HEAD_DIM).transpose(1, 0, 2)
    )
    scores = (
        jnp.einsum("kqd,knd->kqn", grouped, key_heads, preferred_element_type=jnp.float32)
        * score_scale
    )
    if allowed is not None:
        row_count = grouped.shape[1]
        share = row_count // allowed.shape[0]
        mask = jnp.broadcast_to(allowed[:, None, :], (allowed.shape[0], share, key_count)).reshape(
            row_count, key_count
        )
        scores = jnp.where(mask[None], scores, big_negative)
    new_best = jnp.maximum(best, jnp.max(scores, axis=-1))
    factor = jnp.exp(best - new_best)
    probs = jnp.exp(scores - new_best[..., None])
    total = total * factor + jnp.sum(probs, axis=-1)
    mixed = mixed * factor[..., None] + jnp.einsum(
        "kqn,knd->kqd", probs.astype(jnp.bfloat16), value_heads, preferred_element_type=jnp.float32
    )
    return (new_best, total, mixed)


def local(
    hidden_in,
    lengths,
    prefix_cache,
    routes,
    gates,
    attn_gain,
    w_qkv,
    w_out,
    moe_gain,
    expert_gate_up,
    expert_down,
):
    tokens_here = hidden_in[0]
    tok_count = tokens_here.shape[0]
    axis_count = lax.axis_size("tok")
    device_place = lax.axis_index("tok")
    group_lengths = lengths[0]
    token_index = device_place * tok_count + jnp.arange(tok_count, dtype=jnp.int32)
    segment, offset = request_layout(group_lengths, token_index)
    position = prefix_cache.shape[1] * axis_count + offset
    query_width = HEADS * HEAD_DIM
    key_width = KV_HEADS * HEAD_DIM
    group_share = HEADS // KV_HEADS
    normed = rms_scale(tokens_here, attn_gain).astype(jnp.bfloat16)
    qkv_columns, out_columns = gather_small([w_qkv.T, w_out.T])
    packed_rows = gather_rows(jnp.concatenate([qkv_columns, out_columns], axis=1))
    qkv_width = qkv_columns.shape[1]
    qkv_weight = packed_rows[:, :, :qkv_width]
    out_weight = packed_rows[:, :, qkv_width:]
    expert_weights = expert_weight_slices(expert_gate_up, expert_down)
    projected = jnp.einsum(
        "ngr,gcr->nc",
        normed.reshape(tok_count, qkv_weight.shape[0], qkv_weight.shape[2]),
        qkv_weight,
        preferred_element_type=jnp.float32,
    )
    query = rotate(projected[:, :query_width].reshape(tok_count, HEADS, HEAD_DIM), position).astype(
        jnp.bfloat16
    )
    keys_new = rotate(
        projected[:, query_width : query_width + key_width].reshape(tok_count, KV_HEADS, HEAD_DIM),
        position,
    ).astype(jnp.bfloat16)
    values_new = projected[:, query_width + key_width :].astype(jnp.bfloat16)
    suffix_cache = jnp.concatenate([keys_new.reshape(tok_count, key_width), values_new], axis=1)
    row_count = tok_count * group_share
    grouped = (
        query.reshape(tok_count, KV_HEADS, group_share, HEAD_DIM)
        .transpose(1, 0, 2, 3)
        .reshape(KV_HEADS, row_count, HEAD_DIM)
    )
    start_carry = (
        jnp.full((KV_HEADS, row_count), big_negative, jnp.float32),
        jnp.zeros((KV_HEADS, row_count), jnp.float32),
        jnp.zeros((KV_HEADS, row_count, HEAD_DIM), jnp.float32),
    )
    both = ring_gather(jnp.concatenate([suffix_cache, prefix_cache[0]], axis=0), 0)
    piece = both[:, :tok_count].reshape(-1, both.shape[2])
    prefix_all = both[:, tok_count:].reshape(-1, both.shape[2])
    carry = attend(start_carry, grouped, prefix_all, None)
    key_index = jnp.arange(piece.shape[0], dtype=jnp.int32)
    key_segment, key_offset = request_layout(group_lengths, key_index)
    earlier = key_index[None, :] <= token_index[:, None]
    same_request = key_segment[None, :] == segment[:, None]
    carry = attend(carry, grouped, piece, earlier & same_request & (key_index[None, :] >= 0))
    best, total, mixed = carry
    attended = (mixed / total[..., None]).reshape(KV_HEADS, tok_count, group_share, HEAD_DIM)
    attended = attended.transpose(1, 0, 2, 3).reshape(tok_count, query_width).astype(jnp.bfloat16)
    projected_out = jnp.einsum(
        "ngr,gcr->nc",
        attended.reshape(tok_count, out_weight.shape[0], out_weight.shape[2]),
        out_weight,
        preferred_element_type=jnp.float32,
    )
    after_attention = tokens_here.astype(jnp.float32) + projected_out
    moe_in = rms_scale(after_attention, moe_gain).astype(jnp.bfloat16)
    model_width = moe_in.shape[1]
    flat_routes = routes[0].reshape(-1)
    onehot = (flat_routes[:, None] == jnp.arange(EXPERTS, dtype=jnp.int32)[None, :]).astype(
        jnp.int32
    )
    slot_rank = jnp.sum(jnp.cumsum(onehot, axis=0) * onehot, axis=1) - 1
    slot_index = flat_routes * CAP + slot_rank
    source_token = jnp.arange(flat_routes.shape[0], dtype=jnp.int32) // TOP
    outgoing = (
        jnp.zeros((EXPERTS * CAP, model_width), jnp.bfloat16)
        .at[slot_index]
        .set(moe_in[source_token])
    )
    grp_count = lax.axis_size("grp")
    local_experts = EXPERTS // grp_count
    full = expert_weights_full(expert_weights, piece)
    gate_rows = expert_gate_up.shape[1]
    arrived = lax.all_to_all(
        outgoing.reshape(grp_count, local_experts * CAP, model_width),
        "grp",
        split_axis=0,
        concat_axis=0,
        tiled=True,
    )
    arrived = arrived.reshape(grp_count, local_experts, CAP, model_width).transpose(1, 0, 2, 3)
    arrived = arrived.reshape(local_experts, grp_count * CAP, model_width)
    gate_up_w = full[:, :, :gate_rows].transpose(1, 0, 2, 3).reshape(local_experts, -1, model_width)
    down_w = full[:, :, gate_rows:].transpose(1, 0, 2, 3).reshape(local_experts, -1, model_width)
    hidden_pair = jnp.einsum("erd,edf->erf", arrived, gate_up_w, preferred_element_type=jnp.float32)
    activated = (jax.nn.silu(hidden_pair[..., :FF]) * hidden_pair[..., FF:]).astype(jnp.bfloat16)
    expert_result = jnp.einsum(
        "erf,efd->erd", activated, down_w, preferred_element_type=jnp.float32
    ).astype(jnp.bfloat16)
    expert_result = expert_result.reshape(local_experts, grp_count, CAP, model_width).transpose(1, 0, 2, 3)
    returned = lax.all_to_all(
        expert_result.reshape(grp_count, local_experts * CAP, model_width),
        "grp",
        split_axis=0,
        concat_axis=0,
        tiled=True,
    ).reshape(EXPERTS * CAP, -1)
    weighted = returned[slot_index].astype(jnp.float32) * gates[0].reshape(-1)[:, None]
    moe_out = jnp.sum(weighted.reshape(tok_count, TOP, -1), axis=1)
    hidden_out = (after_attention + moe_out).astype(jnp.bfloat16)
    return (hidden_out[None], suffix_cache[None])


def solution(mesh):
    return jax.shard_map(
        local,
        mesh=mesh,
        in_specs=(
            P("grp", "tok", None),
            P("grp", None),
            P("grp", "tok", None),
            P("grp", "tok", None),
            P("grp", "tok", None),
            P(),
            P("grp", "tok"),
            P("grp", "tok"),
            P(),
            P("tok", "grp", None),
            P("tok", "grp", None),
        ),
        out_specs=(P("grp", "tok", None), P("grp", "tok", None)),
        check_vma=False,
    )
```

```python
import jax
import jax.numpy as jnp
from jax import lax
from jax.sharding import PartitionSpec as P
from jax.experimental import pallas as pl
from jax.experimental.pallas import tpu as pltpu

HEADS = 8
KV_HEADS = 4
HEAD_DIM = 64
FF = 512
EXPERTS = 32
TOP = 8
CAP = 40


epsilon = 1e-05
score_scale = 0.015625
rope_base = 10000.0
big_negative = -1e30


def rms_scale(values, gain):
    values = values.astype(jnp.float32)
    mean_square = jnp.mean(values * values, axis=-1, keepdims=True)
    return values * lax.rsqrt(mean_square + epsilon) * gain


def request_layout(group_lengths, token_index):
    ends = jnp.cumsum(group_lengths)
    starts = ends - group_lengths
    segment = jnp.sum((token_index[:, None] >= ends[None, :]).astype(jnp.int32), axis=1)
    match = segment[:, None] == jnp.arange(group_lengths.shape[0], dtype=jnp.int32)[None, :]
    offset = token_index - jnp.sum(jnp.where(match, starts[None, :], 0), axis=1)
    return (segment, offset)


def rotate(values, position):
    half_width = values.shape[-1] // 2
    frequency = rope_base ** (-jnp.arange(half_width, dtype=jnp.float32) * 2.0 / values.shape[-1])
    angle = position.astype(jnp.float32)[:, None] * frequency[None, :]
    cosine = jnp.cos(angle)[:, None, :]
    sine = jnp.sin(angle)[:, None, :]
    first = values[..., :half_width]
    second = values[..., half_width:]
    return jnp.concatenate(
        [first * cosine - second * sine, second * cosine + first * sine], axis=-1
    )


def ring_gather(block, collective_id):
    tok_count = lax.axis_size("tok")
    rows, width = block.shape
    chips = tok_count // 2
    ahead = chips // 2
    behind = chips - 1 - ahead
    mesh_ids = pl.DeviceIdType.MESH

    def kernel(x_ref, out_ref, local_sem, send_r, send_l, send_p, recv):
        me = lax.axis_index("tok")
        grp = lax.axis_index("grp")
        z = me // 2
        core = me % 2
        right = ((z + 1) % chips) * 2 + core
        left = ((z + chips - 1) % chips) * 2 + core
        peer = z * 2 + (1 - core)
        barrier = pltpu.get_barrier_semaphore()
        for other in (right, left, peer):
            pl.semaphore_signal(barrier, 1, device_id=(grp, other), device_id_type=mesh_ids)
        pl.semaphore_wait(barrier, 3)

        def remote(src, slot, sem, target):
            return pltpu.make_async_remote_copy(
                src_ref=src,
                dst_ref=out_ref.at[slot],
                send_sem=sem,
                recv_sem=recv.at[slot],
                device_id=(grp, target),
                device_id_type=mesh_ids,
            )

        own = pltpu.make_async_copy(x_ref, out_ref.at[me], local_sem.at[0])
        own.start()
        sends = [
            remote(x_ref, me, send_p.at[0], peer),
            remote(x_ref, me, send_r.at[0], right),
            remote(x_ref, me, send_l.at[0], left),
        ]
        for c in sends:
            c.start()
        peer_count = 1
        for s in range(1, ahead + 1):
            for sign, limit, sem, target in ((-1, ahead, send_r, right), (1, behind, send_l, left)):
                if s > limit:
                    continue
                slot = ((z + chips + sign * s) % chips) * 2 + core
                remote(out_ref.at[slot], slot, sem.at[0], target).wait_recv()
                if s < limit:
                    c = remote(out_ref.at[slot], slot, sem.at[s], target)
                    c.start()
                    sends.append(c)
                c = remote(out_ref.at[slot], slot, send_p.at[peer_count], peer)
                c.start()
                sends.append(c)
                peer_count += 1
        for other_z in range(chips):
            slot = other_z * 2 + (1 - core)
            remote(out_ref.at[slot], slot, send_p.at[0], peer).wait_recv()
        own.wait()
        for c in sends:
            c.wait_send()

    block_bytes = rows * width * block.dtype.itemsize
    return pl.pallas_call(
        kernel,
        out_shape=jax.ShapeDtypeStruct((tok_count, rows, width), block.dtype),
        in_specs=[pl.BlockSpec(memory_space=pltpu.VMEM)],
        out_specs=pl.BlockSpec(memory_space=pltpu.VMEM),
        scratch_shapes=[
            pltpu.SemaphoreType.DMA((1,)),
            pltpu.SemaphoreType.DMA((ahead,)),
            pltpu.SemaphoreType.DMA((ahead,)),
            pltpu.SemaphoreType.DMA((chips,)),
            pltpu.SemaphoreType.DMA((tok_count,)),
        ],
        compiler_params=pltpu.CompilerParams(collective_id=collective_id, has_side_effects=True),
        cost_estimate=pl.CostEstimate(
            flops=0, transcendentals=0, bytes_accessed=2 * tok_count * block_bytes
        ),
    )(block)


def gather_weights(w_qkv, w_out):
    qkv_rows, out_rows = w_qkv.shape[0], w_out.shape[0]
    by_rows = lax.all_gather(
        jnp.concatenate([w_qkv, w_out], axis=0)[None], "grp", axis=0, tiled=True
    )
    grp_count, packed_rows, columns = by_rows.shape
    width = 512
    ring = ring_gather(by_rows.reshape(-1, width), 1)
    ring = ring.reshape(ring.shape[0], grp_count, packed_rows, columns)
    return ring[:, :, :qkv_rows], ring[:, :, qkv_rows:]


def expert_weight_slices(gate_up, down, after):
    grp_count = lax.axis_size("grp")
    tok_count = lax.axis_size("tok")
    per = tok_count // grp_count
    pairs = []
    for g in range(grp_count):
        for e in range(tok_count):
            pairs.append((g * tok_count + e, (e // per) * tok_count + per * g + e % per))
    block = jnp.concatenate([gate_up[0], down[0]], axis=0)
    block, _ = lax.optimization_barrier((block, after))
    return lax.ppermute(block, ("grp", "tok"), pairs)


def expert_weights_full(block, after):
    block, _ = lax.optimization_barrier((block, after))
    grp_count = lax.axis_size("grp")
    tok_count = lax.axis_size("tok")
    gathered = lax.all_gather(block, "tok", axis=0, tiled=True)
    return gathered.reshape(grp_count, tok_count // grp_count, block.shape[0], block.shape[1])


def attend(carry, grouped, keys_values, allowed):
    best, total, mixed = carry
    key_count = keys_values.shape[0]
    key_width = KV_HEADS * HEAD_DIM
    key_heads = keys_values[:, :key_width].reshape(key_count, KV_HEADS, HEAD_DIM).transpose(1, 0, 2)
    value_heads = (
        keys_values[:, key_width:].reshape(key_count, KV_HEADS, HEAD_DIM).transpose(1, 0, 2)
    )
    scores = (
        jnp.einsum("kqd,knd->kqn", grouped, key_heads, preferred_element_type=jnp.float32)
        * score_scale
    )
    if allowed is not None:
        row_count = grouped.shape[1]
        share = row_count // allowed.shape[0]
        mask = jnp.broadcast_to(allowed[:, None, :], (allowed.shape[0], share, key_count)).reshape(
            row_count, key_count
        )
        scores = jnp.where(mask[None], scores, big_negative)
    new_best = jnp.maximum(best, jnp.max(scores, axis=-1))
    factor = jnp.exp(best - new_best)
    probs = jnp.exp(scores - new_best[..., None])
    total = total * factor + jnp.sum(probs, axis=-1)
    mixed = mixed * factor[..., None] + jnp.einsum(
        "kqn,knd->kqd", probs.astype(jnp.bfloat16), value_heads, preferred_element_type=jnp.float32
    )
    return (new_best, total, mixed)


def local(
    hidden_in,
    lengths,
    prefix_cache,
    routes,
    gates,
    attn_gain,
    w_qkv,
    w_out,
    moe_gain,
    expert_gate_up,
    expert_down,
):
    tokens_here = hidden_in[0]
    tok_count = tokens_here.shape[0]
    axis_count = lax.axis_size("tok")
    device_place = lax.axis_index("tok")
    group_lengths = lengths[0]
    token_index = device_place * tok_count + jnp.arange(tok_count, dtype=jnp.int32)
    segment, offset = request_layout(group_lengths, token_index)
    position = prefix_cache.shape[1] * axis_count + offset
    query_width = HEADS * HEAD_DIM
    key_width = KV_HEADS * HEAD_DIM
    group_share = HEADS // KV_HEADS
    normed = rms_scale(tokens_here, attn_gain).astype(jnp.bfloat16)
    qkv_weight, out_weight = gather_weights(w_qkv, w_out)
    projected = jnp.einsum(
        "ngr,tgrc->ntc",
        normed.reshape(tok_count, qkv_weight.shape[1], qkv_weight.shape[2]),
        qkv_weight,
        preferred_element_type=jnp.float32,
    ).reshape(tok_count, -1)
    query = rotate(projected[:, :query_width].reshape(tok_count, HEADS, HEAD_DIM), position).astype(
        jnp.bfloat16
    )
    keys_new = rotate(
        projected[:, query_width : query_width + key_width].reshape(tok_count, KV_HEADS, HEAD_DIM),
        position,
    ).astype(jnp.bfloat16)
    values_new = projected[:, query_width + key_width :].astype(jnp.bfloat16)
    suffix_cache = jnp.concatenate([keys_new.reshape(tok_count, key_width), values_new], axis=1)
    row_count = tok_count * group_share
    grouped = (
        query.reshape(tok_count, KV_HEADS, group_share, HEAD_DIM)
        .transpose(1, 0, 2, 3)
        .reshape(KV_HEADS, row_count, HEAD_DIM)
    )
    start_carry = (
        jnp.full((KV_HEADS, row_count), big_negative, jnp.float32),
        jnp.zeros((KV_HEADS, row_count), jnp.float32),
        jnp.zeros((KV_HEADS, row_count, HEAD_DIM), jnp.float32),
    )
    both = ring_gather(jnp.concatenate([suffix_cache, prefix_cache[0]], axis=0), 0)
    piece = both[:, :tok_count].reshape(-1, both.shape[2])
    prefix_all = both[:, tok_count:].reshape(-1, both.shape[2])
    expert_weights = expert_weight_slices(expert_gate_up, expert_down, both)
    carry = attend(start_carry, grouped, prefix_all, None)
    key_index = jnp.arange(piece.shape[0], dtype=jnp.int32)
    key_segment, key_offset = request_layout(group_lengths, key_index)
    earlier = key_index[None, :] <= token_index[:, None]
    same_request = key_segment[None, :] == segment[:, None]
    carry = attend(carry, grouped, piece, earlier & same_request & (key_index[None, :] >= 0))
    best, total, mixed = carry
    attended = (mixed / total[..., None]).reshape(KV_HEADS, tok_count, group_share, HEAD_DIM)
    attended = attended.transpose(1, 0, 2, 3).reshape(tok_count, query_width).astype(jnp.bfloat16)
    projected_out = jnp.einsum(
        "ngr,tgrc->ntc",
        attended.reshape(tok_count, out_weight.shape[1], out_weight.shape[2]),
        out_weight,
        preferred_element_type=jnp.float32,
    ).reshape(tok_count, -1)
    after_attention = tokens_here.astype(jnp.float32) + projected_out
    moe_in = rms_scale(after_attention, moe_gain).astype(jnp.bfloat16)
    model_width = moe_in.shape[1]
    flat_routes = routes[0].reshape(-1)
    onehot = (flat_routes[:, None] == jnp.arange(EXPERTS, dtype=jnp.int32)[None, :]).astype(
        jnp.int32
    )
    slot_rank = jnp.sum(jnp.cumsum(onehot, axis=0) * onehot, axis=1) - 1
    slot_index = flat_routes * CAP + slot_rank
    source_token = jnp.arange(flat_routes.shape[0], dtype=jnp.int32) // TOP
    outgoing = (
        jnp.zeros((EXPERTS * CAP, model_width), jnp.bfloat16)
        .at[slot_index]
        .set(moe_in[source_token])
    )
    grp_count = lax.axis_size("grp")
    local_experts = EXPERTS // grp_count
    full = expert_weights_full(expert_weights, piece)
    gate_rows = expert_gate_up.shape[1]
    arrived = lax.all_to_all(
        outgoing.reshape(grp_count, local_experts * CAP, model_width),
        "grp",
        split_axis=0,
        concat_axis=0,
        tiled=True,
    )
    arrived = arrived.reshape(grp_count, local_experts, CAP, model_width).transpose(1, 0, 2, 3)
    arrived = arrived.reshape(local_experts, grp_count * CAP, model_width)
    gate_up_w = full[:, :, :gate_rows].transpose(1, 0, 2, 3).reshape(local_experts, -1, model_width)
    down_w = full[:, :, gate_rows:].transpose(1, 0, 2, 3).reshape(local_experts, -1, model_width)
    hidden_pair = jnp.einsum("erd,edf->erf", arrived, gate_up_w, preferred_element_type=jnp.float32)
    activated = (jax.nn.silu(hidden_pair[..., :FF]) * hidden_pair[..., FF:]).astype(jnp.bfloat16)
    expert_result = jnp.einsum(
        "erf,efd->erd", activated, down_w, preferred_element_type=jnp.float32
    ).astype(jnp.bfloat16)
    expert_result = expert_result.reshape(local_experts, grp_count, CAP, model_width).transpose(1, 0, 2, 3)
    returned = lax.all_to_all(
        expert_result.reshape(grp_count, local_experts * CAP, model_width),
        "grp",
        split_axis=0,
        concat_axis=0,
        tiled=True,
    ).reshape(EXPERTS * CAP, -1)
    weighted = returned[slot_index].astype(jnp.float32) * gates[0].reshape(-1)[:, None]
    moe_out = jnp.sum(weighted.reshape(tok_count, TOP, -1), axis=1)
    hidden_out = (after_attention + moe_out).astype(jnp.bfloat16)
    return (hidden_out[None], suffix_cache[None])


def solution(mesh):
    return jax.shard_map(
        local,
        mesh=mesh,
        in_specs=(
            P("grp", "tok", None),
            P("grp", None),
            P("grp", "tok", None),
            P("grp", "tok", None),
            P("grp", "tok", None),
            P(),
            P("grp", "tok"),
            P("grp", "tok"),
            P(),
            P("tok", "grp", None),
            P("tok", "grp", None),
        ),
        out_specs=(P("grp", "tok", None), P("grp", "tok", None)),
        check_vma=False,
    )
```

```python
import jax
import jax.numpy as jnp
from jax import lax
from jax.sharding import PartitionSpec as P
from jax.experimental import pallas as pl
from jax.experimental.pallas import tpu as pltpu

HEADS = 8
KV_HEADS = 4
HEAD_DIM = 64
FF = 512
EXPERTS = 32
TOP = 8
CAP = 40


epsilon = 1e-05
score_scale = 0.015625
rope_base = 10000.0
big_negative = -1e30


def rms_scale(values, gain):
    values = values.astype(jnp.float32)
    mean_square = jnp.mean(values * values, axis=-1, keepdims=True)
    return values * lax.rsqrt(mean_square + epsilon) * gain


def request_layout(group_lengths, token_index):
    ends = jnp.cumsum(group_lengths)
    starts = ends - group_lengths
    segment = jnp.sum((token_index[:, None] >= ends[None, :]).astype(jnp.int32), axis=1)
    match = segment[:, None] == jnp.arange(group_lengths.shape[0], dtype=jnp.int32)[None, :]
    offset = token_index - jnp.sum(jnp.where(match, starts[None, :], 0), axis=1)
    return (segment, offset)


def rotate(values, position):
    half_width = values.shape[-1] // 2
    frequency = rope_base ** (-jnp.arange(half_width, dtype=jnp.float32) * 2.0 / values.shape[-1])
    angle = position.astype(jnp.float32)[:, None] * frequency[None, :]
    cosine = jnp.cos(angle)[:, None, :]
    sine = jnp.sin(angle)[:, None, :]
    first = values[..., :half_width]
    second = values[..., half_width:]
    return jnp.concatenate(
        [first * cosine - second * sine, second * cosine + first * sine], axis=-1
    )


def ring_gather(block, collective_id):
    tok_count = lax.axis_size("tok")
    rows, width = block.shape
    chips = tok_count // 2
    ahead = chips // 2
    behind = chips - 1 - ahead
    mesh_ids = pl.DeviceIdType.MESH

    def kernel(x_ref, out_ref, local_sem, send_r, send_l, send_p, recv):
        me = lax.axis_index("tok")
        grp = lax.axis_index("grp")
        z = me // 2
        core = me % 2
        right = ((z + 1) % chips) * 2 + core
        left = ((z + chips - 1) % chips) * 2 + core
        peer = z * 2 + (1 - core)
        barrier = pltpu.get_barrier_semaphore()
        for other in (right, left, peer):
            pl.semaphore_signal(barrier, 1, device_id=(grp, other), device_id_type=mesh_ids)
        pl.semaphore_wait(barrier, 3)

        def remote(src, slot, sem, target):
            return pltpu.make_async_remote_copy(
                src_ref=src,
                dst_ref=out_ref.at[slot],
                send_sem=sem,
                recv_sem=recv.at[slot],
                device_id=(grp, target),
                device_id_type=mesh_ids,
            )

        own = pltpu.make_async_copy(x_ref, out_ref.at[me], local_sem.at[0])
        own.start()
        sends = [
            remote(x_ref, me, send_p.at[0], peer),
            remote(x_ref, me, send_r.at[0], right),
            remote(x_ref, me, send_l.at[0], left),
        ]
        for c in sends:
            c.start()
        peer_count = 1
        for s in range(1, ahead + 1):
            for sign, limit, sem, target in ((-1, ahead, send_r, right), (1, behind, send_l, left)):
                if s > limit:
                    continue
                slot = ((z + chips + sign * s) % chips) * 2 + core
                remote(out_ref.at[slot], slot, sem.at[0], target).wait_recv()
                if s < limit:
                    c = remote(out_ref.at[slot], slot, sem.at[s], target)
                    c.start()
                    sends.append(c)
                c = remote(out_ref.at[slot], slot, send_p.at[peer_count], peer)
                c.start()
                sends.append(c)
                peer_count += 1
        for other_z in range(chips):
            slot = other_z * 2 + (1 - core)
            remote(out_ref.at[slot], slot, send_p.at[0], peer).wait_recv()
        own.wait()
        for c in sends:
            c.wait_send()

    block_bytes = rows * width * block.dtype.itemsize
    return pl.pallas_call(
        kernel,
        out_shape=jax.ShapeDtypeStruct((tok_count, rows, width), block.dtype),
        in_specs=[pl.BlockSpec(memory_space=pltpu.VMEM)],
        out_specs=pl.BlockSpec(memory_space=pltpu.VMEM),
        scratch_shapes=[
            pltpu.SemaphoreType.DMA((1,)),
            pltpu.SemaphoreType.DMA((ahead,)),
            pltpu.SemaphoreType.DMA((ahead,)),
            pltpu.SemaphoreType.DMA((chips,)),
            pltpu.SemaphoreType.DMA((tok_count,)),
        ],
        compiler_params=pltpu.CompilerParams(collective_id=collective_id, has_side_effects=True),
        cost_estimate=pl.CostEstimate(
            flops=0, transcendentals=0, bytes_accessed=2 * tok_count * block_bytes
        ),
    )(block)


def gather_small(blocks):
    flat = jnp.concatenate([b.reshape(-1) for b in blocks])
    width = 512
    padded_rows = -(-flat.shape[0] // (16 * width)) * 16
    flat = jnp.pad(flat, (0, padded_rows * width - flat.shape[0]))
    gathered = ring_gather(flat.reshape(padded_rows, width), 1)
    gathered = gathered.reshape(gathered.shape[0], -1)
    pieces, start = [], 0
    for b in blocks:
        size = b.size
        pieces.append(gathered[:, start : start + size].reshape((-1,) + b.shape[1:]))
        start += size
    return pieces


def gather_rows(by_columns):
    return lax.all_gather(by_columns[None], "grp", axis=0, tiled=True)


def expert_weight_slices(gate_up, down, after):
    grp_count = lax.axis_size("grp")
    tok_count = lax.axis_size("tok")
    per = tok_count // grp_count
    pairs = []
    for g in range(grp_count):
        for e in range(tok_count):
            pairs.append((g * tok_count + e, (e // per) * tok_count + per * g + e % per))
    block = jnp.concatenate([gate_up[0], down[0]], axis=0)
    probe = after.reshape(-1)[0]
    block = jnp.where(probe != probe, jnp.zeros_like(block), block)
    return lax.ppermute(block, ("grp", "tok"), pairs)


def expert_weights_full(block, after):
    block, _ = lax.optimization_barrier((block, after))
    grp_count = lax.axis_size("grp")
    tok_count = lax.axis_size("tok")
    gathered = lax.all_gather(block, "tok", axis=0, tiled=True)
    return gathered.reshape(grp_count, tok_count // grp_count, block.shape[0], block.shape[1])


def attend(carry, grouped, keys_values, allowed):
    best, total, mixed = carry
    key_count = keys_values.shape[0]
    key_width = KV_HEADS * HEAD_DIM
    key_heads = keys_values[:, :key_width].reshape(key_count, KV_HEADS, HEAD_DIM).transpose(1, 0, 2)
    value_heads = (
        keys_values[:, key_width:].reshape(key_count, KV_HEADS, HEAD_DIM).transpose(1, 0, 2)
    )
    scores = (
        jnp.einsum("kqd,knd->kqn", grouped, key_heads, preferred_element_type=jnp.float32)
        * score_scale
    )
    if allowed is not None:
        row_count = grouped.shape[1]
        share = row_count // allowed.shape[0]
        mask = jnp.broadcast_to(allowed[:, None, :], (allowed.shape[0], share, key_count)).reshape(
            row_count, key_count
        )
        scores = jnp.where(mask[None], scores, big_negative)
    new_best = jnp.maximum(best, jnp.max(scores, axis=-1))
    factor = jnp.exp(best - new_best)
    probs = jnp.exp(scores - new_best[..., None])
    total = total * factor + jnp.sum(probs, axis=-1)
    mixed = mixed * factor[..., None] + jnp.einsum(
        "kqn,knd->kqd", probs.astype(jnp.bfloat16), value_heads, preferred_element_type=jnp.float32
    )
    return (new_best, total, mixed)


def local(
    hidden_in,
    lengths,
    prefix_cache,
    routes,
    gates,
    attn_gain,
    w_qkv,
    w_out,
    moe_gain,
    expert_gate_up,
    expert_down,
):
    tokens_here = hidden_in[0]
    tok_count = tokens_here.shape[0]
    axis_count = lax.axis_size("tok")
    device_place = lax.axis_index("tok")
    group_lengths = lengths[0]
    token_index = device_place * tok_count + jnp.arange(tok_count, dtype=jnp.int32)
    segment, offset = request_layout(group_lengths, token_index)
    position = prefix_cache.shape[1] * axis_count + offset
    query_width = HEADS * HEAD_DIM
    key_width = KV_HEADS * HEAD_DIM
    group_share = HEADS // KV_HEADS
    normed = rms_scale(tokens_here, attn_gain).astype(jnp.bfloat16)
    qkv_columns, out_columns = gather_small([w_qkv.T, w_out.T])
    qkv_weight = gather_rows(qkv_columns)
    out_columns, _ = lax.optimization_barrier((out_columns, qkv_weight))
    out_weight = gather_rows(out_columns)
    expert_weights = expert_weight_slices(expert_gate_up, expert_down, out_weight)
    projected = jnp.einsum(
        "ngr,gcr->nc",
        normed.reshape(tok_count, qkv_weight.shape[0], qkv_weight.shape[2]),
        qkv_weight,
        preferred_element_type=jnp.float32,
    )
    query = rotate(projected[:, :query_width].reshape(tok_count, HEADS, HEAD_DIM), position).astype(
        jnp.bfloat16
    )
    keys_new = rotate(
        projected[:, query_width : query_width + key_width].reshape(tok_count, KV_HEADS, HEAD_DIM),
        position,
    ).astype(jnp.bfloat16)
    values_new = projected[:, query_width + key_width :].astype(jnp.bfloat16)
    suffix_cache = jnp.concatenate([keys_new.reshape(tok_count, key_width), values_new], axis=1)
    row_count = tok_count * group_share
    grouped = (
        query.reshape(tok_count, KV_HEADS, group_share, HEAD_DIM)
        .transpose(1, 0, 2, 3)
        .reshape(KV_HEADS, row_count, HEAD_DIM)
    )
    start_carry = (
        jnp.full((KV_HEADS, row_count), big_negative, jnp.float32),
        jnp.zeros((KV_HEADS, row_count), jnp.float32),
        jnp.zeros((KV_HEADS, row_count, HEAD_DIM), jnp.float32),
    )
    both = ring_gather(jnp.concatenate([suffix_cache, prefix_cache[0]], axis=0), 0)
    piece = both[:, :tok_count].reshape(-1, both.shape[2])
    prefix_all = both[:, tok_count:].reshape(-1, both.shape[2])
    carry = attend(start_carry, grouped, prefix_all, None)
    key_index = jnp.arange(piece.shape[0], dtype=jnp.int32)
    key_segment, key_offset = request_layout(group_lengths, key_index)
    earlier = key_index[None, :] <= token_index[:, None]
    same_request = key_segment[None, :] == segment[:, None]
    carry = attend(carry, grouped, piece, earlier & same_request & (key_index[None, :] >= 0))
    best, total, mixed = carry
    attended = (mixed / total[..., None]).reshape(KV_HEADS, tok_count, group_share, HEAD_DIM)
    attended = attended.transpose(1, 0, 2, 3).reshape(tok_count, query_width).astype(jnp.bfloat16)
    projected_out = jnp.einsum(
        "ngr,gcr->nc",
        attended.reshape(tok_count, out_weight.shape[0], out_weight.shape[2]),
        out_weight,
        preferred_element_type=jnp.float32,
    )
    after_attention = tokens_here.astype(jnp.float32) + projected_out
    moe_in = rms_scale(after_attention, moe_gain).astype(jnp.bfloat16)
    model_width = moe_in.shape[1]
    flat_routes = routes[0].reshape(-1)
    onehot = (flat_routes[:, None] == jnp.arange(EXPERTS, dtype=jnp.int32)[None, :]).astype(
        jnp.int32
    )
    route_count = flat_routes.shape[0]
    lower = (
        jnp.arange(route_count, dtype=jnp.int32)[:, None]
        >= jnp.arange(route_count, dtype=jnp.int32)[None, :]
    ).astype(jnp.bfloat16)
    running = jnp.dot(lower, onehot.astype(jnp.bfloat16), preferred_element_type=jnp.float32)
    slot_rank = jnp.sum(running.astype(jnp.int32) * onehot, axis=1) - 1
    slot_index = flat_routes * CAP + slot_rank
    source_token = jnp.arange(flat_routes.shape[0], dtype=jnp.int32) // TOP
    outgoing = (
        jnp.zeros((EXPERTS * CAP, model_width), jnp.bfloat16)
        .at[slot_index]
        .set(moe_in[source_token])
    )
    grp_count = lax.axis_size("grp")
    local_experts = EXPERTS // grp_count
    full = expert_weights_full(expert_weights, piece)
    gate_rows = expert_gate_up.shape[1]
    arrived = lax.all_to_all(
        outgoing.reshape(grp_count, local_experts * CAP, model_width),
        "grp",
        split_axis=0,
        concat_axis=0,
        tiled=True,
    )
    arrived = arrived.reshape(grp_count, local_experts, CAP, model_width).transpose(1, 0, 2, 3)
    arrived = arrived.reshape(local_experts, grp_count * CAP, model_width)
    gate_up_w = full[:, :, :gate_rows].transpose(1, 0, 2, 3).reshape(local_experts, -1, model_width)
    down_w = full[:, :, gate_rows:].transpose(1, 0, 2, 3).reshape(local_experts, -1, model_width)
    hidden_pair = jnp.einsum("erd,edf->erf", arrived, gate_up_w, preferred_element_type=jnp.float32)
    activated = (jax.nn.silu(hidden_pair[..., :FF]) * hidden_pair[..., FF:]).astype(jnp.bfloat16)
    expert_result = jnp.einsum(
        "erf,efd->erd", activated, down_w, preferred_element_type=jnp.float32
    ).astype(jnp.bfloat16)
    expert_result = expert_result.reshape(local_experts, grp_count, CAP, model_width).transpose(1, 0, 2, 3)
    returned = lax.all_to_all(
        expert_result.reshape(grp_count, local_experts * CAP, model_width),
        "grp",
        split_axis=0,
        concat_axis=0,
        tiled=True,
    ).reshape(EXPERTS * CAP, -1)
    weighted = returned[slot_index].astype(jnp.float32) * gates[0].reshape(-1)[:, None]
    moe_out = jnp.sum(weighted.reshape(tok_count, TOP, -1), axis=1)
    hidden_out = (after_attention + moe_out).astype(jnp.bfloat16)
    return (hidden_out[None], suffix_cache[None])


def solution(mesh):
    return jax.shard_map(
        local,
        mesh=mesh,
        in_specs=(
            P("grp", "tok", None),
            P("grp", None),
            P("grp", "tok", None),
            P("grp", "tok", None),
            P("grp", "tok", None),
            P(),
            P("grp", "tok"),
            P("grp", "tok"),
            P(),
            P("tok", "grp", None),
            P("tok", "grp", None),
        ),
        out_specs=(P("grp", "tok", None), P("grp", "tok", None)),
        check_vma=False,
    )
```

```python
import jax
import jax.numpy as jnp
from jax import lax
from jax.sharding import PartitionSpec as P
from jax.experimental import pallas as pl
from jax.experimental.pallas import tpu as pltpu

HEADS = 8
KV_HEADS = 4
HEAD_DIM = 64
FF = 512
EXPERTS = 32
TOP = 8
CAP = 40


epsilon = 1e-05
score_scale = 0.015625
rope_base = 10000.0
big_negative = -1e30


def rms_scale(values, gain):
    values = values.astype(jnp.float32)
    mean_square = jnp.mean(values * values, axis=-1, keepdims=True)
    return values * lax.rsqrt(mean_square + epsilon) * gain


def request_layout(group_lengths, token_index):
    ends = jnp.cumsum(group_lengths)
    starts = ends - group_lengths
    segment = jnp.sum((token_index[:, None] >= ends[None, :]).astype(jnp.int32), axis=1)
    match = segment[:, None] == jnp.arange(group_lengths.shape[0], dtype=jnp.int32)[None, :]
    offset = token_index - jnp.sum(jnp.where(match, starts[None, :], 0), axis=1)
    return (segment, offset)


def rotate(values, position):
    half_width = values.shape[-1] // 2
    frequency = rope_base ** (-jnp.arange(half_width, dtype=jnp.float32) * 2.0 / values.shape[-1])
    angle = position.astype(jnp.float32)[:, None] * frequency[None, :]
    cosine = jnp.cos(angle)[:, None, :]
    sine = jnp.sin(angle)[:, None, :]
    first = values[..., :half_width]
    second = values[..., half_width:]
    return jnp.concatenate(
        [first * cosine - second * sine, second * cosine + first * sine], axis=-1
    )


def ring_gather(block, collective_id):
    tok_count = lax.axis_size("tok")
    rows, width = block.shape
    chips = tok_count // 2
    ahead = chips // 2
    behind = chips - 1 - ahead
    mesh_ids = pl.DeviceIdType.MESH

    def kernel(x_ref, out_ref, local_sem, send_r, send_l, send_p, recv):
        me = lax.axis_index("tok")
        grp = lax.axis_index("grp")
        z = me // 2
        core = me % 2
        right = ((z + 1) % chips) * 2 + core
        left = ((z + chips - 1) % chips) * 2 + core
        peer = z * 2 + (1 - core)
        barrier = pltpu.get_barrier_semaphore()
        for other in (right, left, peer):
            pl.semaphore_signal(barrier, 1, device_id=(grp, other), device_id_type=mesh_ids)
        pl.semaphore_wait(barrier, 3)

        def remote(src, slot, sem, target):
            return pltpu.make_async_remote_copy(
                src_ref=src,
                dst_ref=out_ref.at[slot],
                send_sem=sem,
                recv_sem=recv.at[slot],
                device_id=(grp, target),
                device_id_type=mesh_ids,
            )

        own = pltpu.make_async_copy(x_ref, out_ref.at[me], local_sem.at[0])
        own.start()
        sends = [
            remote(x_ref, me, send_p.at[0], peer),
            remote(x_ref, me, send_r.at[0], right),
            remote(x_ref, me, send_l.at[0], left),
        ]
        for c in sends:
            c.start()
        peer_count = 1
        for s in range(1, ahead + 1):
            for sign, limit, sem, target in ((-1, ahead, send_r, right), (1, behind, send_l, left)):
                if s > limit:
                    continue
                slot = ((z + chips + sign * s) % chips) * 2 + core
                remote(out_ref.at[slot], slot, sem.at[0], target).wait_recv()
                if s < limit:
                    c = remote(out_ref.at[slot], slot, sem.at[s], target)
                    c.start()
                    sends.append(c)
                c = remote(out_ref.at[slot], slot, send_p.at[peer_count], peer)
                c.start()
                sends.append(c)
                peer_count += 1
        for other_z in range(chips):
            slot = other_z * 2 + (1 - core)
            remote(out_ref.at[slot], slot, send_p.at[0], peer).wait_recv()
        own.wait()
        for c in sends:
            c.wait_send()

    block_bytes = rows * width * block.dtype.itemsize
    return pl.pallas_call(
        kernel,
        out_shape=jax.ShapeDtypeStruct((tok_count, rows, width), block.dtype),
        in_specs=[pl.BlockSpec(memory_space=pltpu.VMEM)],
        out_specs=pl.BlockSpec(memory_space=pltpu.VMEM),
        scratch_shapes=[
            pltpu.SemaphoreType.DMA((1,)),
            pltpu.SemaphoreType.DMA((ahead,)),
            pltpu.SemaphoreType.DMA((ahead,)),
            pltpu.SemaphoreType.DMA((chips,)),
            pltpu.SemaphoreType.DMA((tok_count,)),
        ],
        compiler_params=pltpu.CompilerParams(collective_id=collective_id, has_side_effects=True),
        cost_estimate=pl.CostEstimate(
            flops=0, transcendentals=0, bytes_accessed=2 * tok_count * block_bytes
        ),
    )(block)


def gather_small(blocks):
    flat = jnp.concatenate([b.reshape(-1) for b in blocks])
    width = 512
    padded_rows = -(-flat.shape[0] // (16 * width)) * 16
    flat = jnp.pad(flat, (0, padded_rows * width - flat.shape[0]))
    gathered = ring_gather(flat.reshape(padded_rows, width), 1)
    gathered = gathered.reshape(gathered.shape[0], -1)
    pieces, start = [], 0
    for b in blocks:
        size = b.size
        pieces.append(gathered[:, start : start + size].reshape((-1,) + b.shape[1:]))
        start += size
    return pieces


def gather_rows(by_columns):
    return lax.all_gather(by_columns[None], "grp", axis=0, tiled=True)


def expert_weight_slices(gate_up, down):
    grp_count = lax.axis_size("grp")
    tok_count = lax.axis_size("tok")
    per = tok_count // grp_count
    pairs = []
    for g in range(grp_count):
        for e in range(tok_count):
            pairs.append((g * tok_count + e, (e // per) * tok_count + per * g + e % per))
    block = jnp.concatenate([gate_up[0], down[0]], axis=0)
    return lax.ppermute(block, ("grp", "tok"), pairs)


def expert_weights_full(block, after):
    block, _ = lax.optimization_barrier((block, after))
    grp_count = lax.axis_size("grp")
    tok_count = lax.axis_size("tok")
    gathered = lax.all_gather(block, "tok", axis=0, tiled=True)
    return gathered.reshape(grp_count, tok_count // grp_count, block.shape[0], block.shape[1])


def attend(carry, grouped, keys_values, allowed):
    best, total, mixed = carry
    key_count = keys_values.shape[0]
    key_width = KV_HEADS * HEAD_DIM
    key_heads = keys_values[:, :key_width].reshape(key_count, KV_HEADS, HEAD_DIM).transpose(1, 0, 2)
    value_heads = (
        keys_values[:, key_width:].reshape(key_count, KV_HEADS, HEAD_DIM).transpose(1, 0, 2)
    )
    scores = (
        jnp.einsum("kqd,knd->kqn", grouped, key_heads, preferred_element_type=jnp.float32)
        * score_scale
    )
    if allowed is not None:
        row_count = grouped.shape[1]
        share = row_count // allowed.shape[0]
        mask = jnp.broadcast_to(allowed[:, None, :], (allowed.shape[0], share, key_count)).reshape(
            row_count, key_count
        )
        scores = jnp.where(mask[None], scores, big_negative)
    new_best = jnp.maximum(best, jnp.max(scores, axis=-1))
    factor = jnp.exp(best - new_best)
    probs = jnp.exp(scores - new_best[..., None])
    total = total * factor + jnp.sum(probs, axis=-1)
    mixed = mixed * factor[..., None] + jnp.einsum(
        "kqn,knd->kqd", probs.astype(jnp.bfloat16), value_heads, preferred_element_type=jnp.float32
    )
    return (new_best, total, mixed)


def local(
    hidden_in,
    lengths,
    prefix_cache,
    routes,
    gates,
    attn_gain,
    w_qkv,
    w_out,
    moe_gain,
    expert_gate_up,
    expert_down,
):
    tokens_here = hidden_in[0]
    tok_count = tokens_here.shape[0]
    axis_count = lax.axis_size("tok")
    device_place = lax.axis_index("tok")
    group_lengths = lengths[0]
    token_index = device_place * tok_count + jnp.arange(tok_count, dtype=jnp.int32)
    segment, offset = request_layout(group_lengths, token_index)
    position = prefix_cache.shape[1] * axis_count + offset
    query_width = HEADS * HEAD_DIM
    key_width = KV_HEADS * HEAD_DIM
    group_share = HEADS // KV_HEADS
    normed = rms_scale(tokens_here, attn_gain).astype(jnp.bfloat16)
    qkv_columns, out_columns = gather_small([w_qkv.T, w_out.T])
    packed_rows = gather_rows(jnp.concatenate([qkv_columns, out_columns], axis=1))
    qkv_width = qkv_columns.shape[1]
    qkv_weight = packed_rows[:, :, :qkv_width]
    out_weight = packed_rows[:, :, qkv_width:]
    expert_weights = expert_weight_slices(expert_gate_up, expert_down)
    projected = jnp.einsum(
        "ngr,gcr->nc",
        normed.reshape(tok_count, qkv_weight.shape[0], qkv_weight.shape[2]),
        qkv_weight,
        preferred_element_type=jnp.float32,
    )
    query = rotate(projected[:, :query_width].reshape(tok_count, HEADS, HEAD_DIM), position).astype(
        jnp.bfloat16
    )
    keys_new = rotate(
        projected[:, query_width : query_width + key_width].reshape(tok_count, KV_HEADS, HEAD_DIM),
        position,
    ).astype(jnp.bfloat16)
    values_new = projected[:, query_width + key_width :].astype(jnp.bfloat16)
    suffix_cache = jnp.concatenate([keys_new.reshape(tok_count, key_width), values_new], axis=1)
    row_count = tok_count * group_share
    grouped = (
        query.reshape(tok_count, KV_HEADS, group_share, HEAD_DIM)
        .transpose(1, 0, 2, 3)
        .reshape(KV_HEADS, row_count, HEAD_DIM)
    )
    start_carry = (
        jnp.full((KV_HEADS, row_count), big_negative, jnp.float32),
        jnp.zeros((KV_HEADS, row_count), jnp.float32),
        jnp.zeros((KV_HEADS, row_count, HEAD_DIM), jnp.float32),
    )
    both = ring_gather(jnp.concatenate([suffix_cache, prefix_cache[0]], axis=0), 0)
    piece = both[:, :tok_count].reshape(-1, both.shape[2])
    prefix_all = both[:, tok_count:].reshape(-1, both.shape[2])
    carry = attend(start_carry, grouped, prefix_all, None)
    key_index = jnp.arange(piece.shape[0], dtype=jnp.int32)
    key_segment, key_offset = request_layout(group_lengths, key_index)
    earlier = key_index[None, :] <= token_index[:, None]
    same_request = key_segment[None, :] == segment[:, None]
    carry = attend(carry, grouped, piece, earlier & same_request & (key_index[None, :] >= 0))
    best, total, mixed = carry
    attended = (mixed / total[..., None]).reshape(KV_HEADS, tok_count, group_share, HEAD_DIM)
    attended = attended.transpose(1, 0, 2, 3).reshape(tok_count, query_width).astype(jnp.bfloat16)
    projected_out = jnp.einsum(
        "ngr,gcr->nc",
        attended.reshape(tok_count, out_weight.shape[0], out_weight.shape[2]),
        out_weight,
        preferred_element_type=jnp.float32,
    )
    after_attention = tokens_here.astype(jnp.float32) + projected_out
    moe_in = rms_scale(after_attention, moe_gain).astype(jnp.bfloat16)
    model_width = moe_in.shape[1]
    flat_routes = routes[0].reshape(-1)
    onehot = (flat_routes[:, None] == jnp.arange(EXPERTS, dtype=jnp.int32)[None, :]).astype(
        jnp.int32
    )
    route_count = flat_routes.shape[0]
    lower = (
        jnp.arange(route_count, dtype=jnp.int32)[:, None]
        >= jnp.arange(route_count, dtype=jnp.int32)[None, :]
    ).astype(jnp.bfloat16)
    running = jnp.dot(lower, onehot.astype(jnp.bfloat16), preferred_element_type=jnp.float32)
    slot_rank = jnp.sum(running.astype(jnp.int32) * onehot, axis=1) - 1
    slot_index = flat_routes * CAP + slot_rank
    source_token = jnp.arange(flat_routes.shape[0], dtype=jnp.int32) // TOP
    outgoing = (
        jnp.zeros((EXPERTS * CAP, model_width), jnp.bfloat16)
        .at[slot_index]
        .set(moe_in[source_token])
    )
    grp_count = lax.axis_size("grp")
    local_experts = EXPERTS // grp_count
    full = expert_weights_full(expert_weights, piece)
    gate_rows = expert_gate_up.shape[1]
    arrived = lax.all_to_all(
        outgoing.reshape(grp_count, local_experts * CAP, model_width),
        "grp",
        split_axis=0,
        concat_axis=0,
        tiled=True,
    )
    arrived = arrived.reshape(grp_count, local_experts, CAP, model_width).transpose(1, 0, 2, 3)
    arrived = arrived.reshape(local_experts, grp_count * CAP, model_width)
    gate_up_w = full[:, :, :gate_rows].transpose(1, 0, 2, 3).reshape(local_experts, -1, model_width)
    down_w = full[:, :, gate_rows:].transpose(1, 0, 2, 3).reshape(local_experts, -1, model_width)
    hidden_pair = jnp.einsum("erd,edf->erf", arrived, gate_up_w, preferred_element_type=jnp.float32)
    activated = (jax.nn.silu(hidden_pair[..., :FF]) * hidden_pair[..., FF:]).astype(jnp.bfloat16)
    expert_result = jnp.einsum(
        "erf,efd->erd", activated, down_w, preferred_element_type=jnp.float32
    ).astype(jnp.bfloat16)
    expert_result = expert_result.reshape(local_experts, grp_count, CAP, model_width).transpose(1, 0, 2, 3)
    returned = lax.all_to_all(
        expert_result.reshape(grp_count, local_experts * CAP, model_width),
        "grp",
        split_axis=0,
        concat_axis=0,
        tiled=True,
    ).reshape(EXPERTS * CAP, -1)
    weighted = returned[slot_index].astype(jnp.float32) * gates[0].reshape(-1)[:, None]
    moe_out = jnp.sum(weighted.reshape(tok_count, TOP, -1), axis=1)
    hidden_out = (after_attention + moe_out).astype(jnp.bfloat16)
    return (hidden_out[None], suffix_cache[None])


def solution(mesh):
    return jax.shard_map(
        local,
        mesh=mesh,
        in_specs=(
            P("grp", "tok", None),
            P("grp", None),
            P("grp", "tok", None),
            P("grp", "tok", None),
            P("grp", "tok", None),
            P(),
            P("grp", "tok"),
            P("grp", "tok"),
            P(),
            P("tok", "grp", None),
            P("tok", "grp", None),
        ),
        out_specs=(P("grp", "tok", None), P("grp", "tok", None)),
        check_vma=False,
    )
```

```python
import jax
import jax.numpy as jnp
from jax import lax
from jax.sharding import PartitionSpec as P
from jax.experimental import pallas as pl
from jax.experimental.pallas import tpu as pltpu

HEADS = 8
KV_HEADS = 4
HEAD_DIM = 64
FF = 512
EXPERTS = 32
TOP = 8
CAP = 40


epsilon = 1e-05
score_scale = 0.015625
rope_base = 10000.0
big_negative = -1e30


def rms_scale(values, gain):
    values = values.astype(jnp.float32)
    mean_square = jnp.mean(values * values, axis=-1, keepdims=True)
    return values * lax.rsqrt(mean_square + epsilon) * gain


def request_layout(group_lengths, token_index):
    ends = jnp.cumsum(group_lengths)
    starts = ends - group_lengths
    segment = jnp.sum((token_index[:, None] >= ends[None, :]).astype(jnp.int32), axis=1)
    match = segment[:, None] == jnp.arange(group_lengths.shape[0], dtype=jnp.int32)[None, :]
    offset = token_index - jnp.sum(jnp.where(match, starts[None, :], 0), axis=1)
    return (segment, offset)


def rotate(values, position):
    half_width = values.shape[-1] // 2
    frequency = rope_base ** (-jnp.arange(half_width, dtype=jnp.float32) * 2.0 / values.shape[-1])
    angle = position.astype(jnp.float32)[:, None] * frequency[None, :]
    cosine = jnp.cos(angle)[:, None, :]
    sine = jnp.sin(angle)[:, None, :]
    first = values[..., :half_width]
    second = values[..., half_width:]
    return jnp.concatenate(
        [first * cosine - second * sine, second * cosine + first * sine], axis=-1
    )


def ring_gather(block, collective_id):
    tok_count = lax.axis_size("tok")
    rows, width = block.shape
    chips = tok_count // 2
    ahead = chips // 2
    behind = chips - 1 - ahead
    mesh_ids = pl.DeviceIdType.MESH

    def kernel(x_ref, out_ref, local_sem, send_r, send_l, send_p, recv):
        me = lax.axis_index("tok")
        grp = lax.axis_index("grp")
        z = me // 2
        core = me % 2
        right = ((z + 1) % chips) * 2 + core
        left = ((z + chips - 1) % chips) * 2 + core
        peer = z * 2 + (1 - core)
        barrier = pltpu.get_barrier_semaphore()
        for other in (right, left, peer):
            pl.semaphore_signal(barrier, 1, device_id=(grp, other), device_id_type=mesh_ids)
        pl.semaphore_wait(barrier, 3)

        def remote(src, slot, sem, target):
            return pltpu.make_async_remote_copy(
                src_ref=src,
                dst_ref=out_ref.at[slot],
                send_sem=sem,
                recv_sem=recv.at[slot],
                device_id=(grp, target),
                device_id_type=mesh_ids,
            )

        own = pltpu.make_async_copy(x_ref, out_ref.at[me], local_sem.at[0])
        own.start()
        sends = [
            remote(x_ref, me, send_p.at[0], peer),
            remote(x_ref, me, send_r.at[0], right),
            remote(x_ref, me, send_l.at[0], left),
        ]
        for c in sends:
            c.start()
        peer_count = 1
        for s in range(1, ahead + 1):
            for sign, limit, sem, target in ((-1, ahead, send_r, right), (1, behind, send_l, left)):
                if s > limit:
                    continue
                slot = ((z + chips + sign * s) % chips) * 2 + core
                remote(out_ref.at[slot], slot, sem.at[0], target).wait_recv()
                if s < limit:
                    c = remote(out_ref.at[slot], slot, sem.at[s], target)
                    c.start()
                    sends.append(c)
                c = remote(out_ref.at[slot], slot, send_p.at[peer_count], peer)
                c.start()
                sends.append(c)
                peer_count += 1
        for other_z in range(chips):
            slot = other_z * 2 + (1 - core)
            remote(out_ref.at[slot], slot, send_p.at[0], peer).wait_recv()
        own.wait()
        for c in sends:
            c.wait_send()

    block_bytes = rows * width * block.dtype.itemsize
    return pl.pallas_call(
        kernel,
        out_shape=jax.ShapeDtypeStruct((tok_count, rows, width), block.dtype),
        in_specs=[pl.BlockSpec(memory_space=pltpu.VMEM)],
        out_specs=pl.BlockSpec(memory_space=pltpu.VMEM),
        scratch_shapes=[
            pltpu.SemaphoreType.DMA((1,)),
            pltpu.SemaphoreType.DMA((ahead,)),
            pltpu.SemaphoreType.DMA((ahead,)),
            pltpu.SemaphoreType.DMA((chips,)),
            pltpu.SemaphoreType.DMA((tok_count,)),
        ],
        compiler_params=pltpu.CompilerParams(collective_id=collective_id, has_side_effects=True),
        cost_estimate=pl.CostEstimate(
            flops=0, transcendentals=0, bytes_accessed=2 * tok_count * block_bytes
        ),
    )(block)


def gather_small(blocks):
    flat = jnp.concatenate([b.reshape(-1) for b in blocks])
    width = 512
    padded_rows = -(-flat.shape[0] // (16 * width)) * 16
    flat = jnp.pad(flat, (0, padded_rows * width - flat.shape[0]))
    gathered = ring_gather(flat.reshape(padded_rows, width), 1)
    gathered = gathered.reshape(gathered.shape[0], -1)
    pieces, start = [], 0
    for b in blocks:
        size = b.size
        pieces.append(gathered[:, start : start + size].reshape((-1,) + b.shape[1:]))
        start += size
    return pieces


def gather_rows(by_columns):
    return lax.all_gather(by_columns[None], "grp", axis=0, tiled=True)


def expert_weight_slices(gate_up, down):
    grp_count = lax.axis_size("grp")
    tok_count = lax.axis_size("tok")
    per = tok_count // grp_count
    pairs = []
    for g in range(grp_count):
        for e in range(tok_count):
            pairs.append((g * tok_count + e, (e // per) * tok_count + per * g + e % per))
    block = jnp.concatenate([gate_up[0], down[0]], axis=0)
    return lax.ppermute(block, ("grp", "tok"), pairs)


def expert_weights_full(block, after):
    block, _ = lax.optimization_barrier((block, after))
    grp_count = lax.axis_size("grp")
    tok_count = lax.axis_size("tok")
    gathered = lax.all_gather(block, "tok", axis=0, tiled=True)
    return gathered.reshape(grp_count, tok_count // grp_count, block.shape[0], block.shape[1])


def attend(carry, grouped, keys_values, allowed):
    best, total, mixed = carry
    key_count = keys_values.shape[0]
    key_width = KV_HEADS * HEAD_DIM
    key_heads = keys_values[:, :key_width].reshape(key_count, KV_HEADS, HEAD_DIM).transpose(1, 0, 2)
    value_heads = (
        keys_values[:, key_width:].reshape(key_count, KV_HEADS, HEAD_DIM).transpose(1, 0, 2)
    )
    scores = (
        jnp.einsum("kqd,knd->kqn", grouped, key_heads, preferred_element_type=jnp.float32)
        * score_scale
    )
    if allowed is not None:
        row_count = grouped.shape[1]
        share = row_count // allowed.shape[0]
        mask = jnp.broadcast_to(allowed[:, None, :], (allowed.shape[0], share, key_count)).reshape(
            row_count, key_count
        )
        scores = jnp.where(mask[None], scores, big_negative)
    new_best = jnp.maximum(best, jnp.max(scores, axis=-1))
    factor = jnp.exp(best - new_best)
    probs = jnp.exp(scores - new_best[..., None])
    total = total * factor + jnp.sum(probs, axis=-1)
    mixed = mixed * factor[..., None] + jnp.einsum(
        "kqn,knd->kqd", probs.astype(jnp.bfloat16), value_heads, preferred_element_type=jnp.float32
    )
    return (new_best, total, mixed)


def local(
    hidden_in,
    lengths,
    prefix_cache,
    routes,
    gates,
    attn_gain,
    w_qkv,
    w_out,
    moe_gain,
    expert_gate_up,
    expert_down,
):
    tokens_here = hidden_in[0]
    tok_count = tokens_here.shape[0]
    axis_count = lax.axis_size("tok")
    device_place = lax.axis_index("tok")
    group_lengths = lengths[0]
    token_index = device_place * tok_count + jnp.arange(tok_count, dtype=jnp.int32)
    segment, offset = request_layout(group_lengths, token_index)
    position = prefix_cache.shape[1] * axis_count + offset
    query_width = HEADS * HEAD_DIM
    key_width = KV_HEADS * HEAD_DIM
    group_share = HEADS // KV_HEADS
    normed = rms_scale(tokens_here, attn_gain).astype(jnp.bfloat16)
    qkv_columns, out_columns = gather_small([w_qkv.T, w_out.T])
    expert_weights = expert_weight_slices(expert_gate_up, expert_down)
    both_columns = jnp.concatenate([qkv_columns, out_columns], axis=1)
    probe = expert_weights[0, 0]
    both_columns = jnp.where(probe != probe, jnp.zeros_like(both_columns), both_columns)
    packed_rows = gather_rows(both_columns)
    qkv_width = qkv_columns.shape[1]
    qkv_weight = packed_rows[:, :, :qkv_width]
    out_weight = packed_rows[:, :, qkv_width:]
    projected = jnp.einsum(
        "ngr,gcr->nc",
        normed.reshape(tok_count, qkv_weight.shape[0], qkv_weight.shape[2]),
        qkv_weight,
        preferred_element_type=jnp.float32,
    )
    query = rotate(projected[:, :query_width].reshape(tok_count, HEADS, HEAD_DIM), position).astype(
        jnp.bfloat16
    )
    keys_new = rotate(
        projected[:, query_width : query_width + key_width].reshape(tok_count, KV_HEADS, HEAD_DIM),
        position,
    ).astype(jnp.bfloat16)
    values_new = projected[:, query_width + key_width :].astype(jnp.bfloat16)
    suffix_cache = jnp.concatenate([keys_new.reshape(tok_count, key_width), values_new], axis=1)
    row_count = tok_count * group_share
    grouped = (
        query.reshape(tok_count, KV_HEADS, group_share, HEAD_DIM)
        .transpose(1, 0, 2, 3)
        .reshape(KV_HEADS, row_count, HEAD_DIM)
    )
    start_carry = (
        jnp.full((KV_HEADS, row_count), big_negative, jnp.float32),
        jnp.zeros((KV_HEADS, row_count), jnp.float32),
        jnp.zeros((KV_HEADS, row_count, HEAD_DIM), jnp.float32),
    )
    both = ring_gather(jnp.concatenate([suffix_cache, prefix_cache[0]], axis=0), 0)
    piece = both[:, :tok_count].reshape(-1, both.shape[2])
    prefix_all = both[:, tok_count:].reshape(-1, both.shape[2])
    carry = attend(start_carry, grouped, prefix_all, None)
    key_index = jnp.arange(piece.shape[0], dtype=jnp.int32)
    key_segment, key_offset = request_layout(group_lengths, key_index)
    earlier = key_index[None, :] <= token_index[:, None]
    same_request = key_segment[None, :] == segment[:, None]
    carry = attend(carry, grouped, piece, earlier & same_request & (key_index[None, :] >= 0))
    best, total, mixed = carry
    attended = (mixed / total[..., None]).reshape(KV_HEADS, tok_count, group_share, HEAD_DIM)
    attended = attended.transpose(1, 0, 2, 3).reshape(tok_count, query_width).astype(jnp.bfloat16)
    projected_out = jnp.einsum(
        "ngr,gcr->nc",
        attended.reshape(tok_count, out_weight.shape[0], out_weight.shape[2]),
        out_weight,
        preferred_element_type=jnp.float32,
    )
    after_attention = tokens_here.astype(jnp.float32) + projected_out
    moe_in = rms_scale(after_attention, moe_gain).astype(jnp.bfloat16)
    model_width = moe_in.shape[1]
    flat_routes = routes[0].reshape(-1)
    onehot = (flat_routes[:, None] == jnp.arange(EXPERTS, dtype=jnp.int32)[None, :]).astype(
        jnp.int32
    )
    route_count = flat_routes.shape[0]
    lower = (
        jnp.arange(route_count, dtype=jnp.int32)[:, None]
        >= jnp.arange(route_count, dtype=jnp.int32)[None, :]
    ).astype(jnp.bfloat16)
    running = jnp.dot(lower, onehot.astype(jnp.bfloat16), preferred_element_type=jnp.float32)
    slot_rank = jnp.sum(running.astype(jnp.int32) * onehot, axis=1) - 1
    slot_index = flat_routes * CAP + slot_rank
    source_token = jnp.arange(flat_routes.shape[0], dtype=jnp.int32) // TOP
    outgoing = (
        jnp.zeros((EXPERTS * CAP, model_width), jnp.bfloat16)
        .at[slot_index]
        .set(moe_in[source_token])
    )
    grp_count = lax.axis_size("grp")
    local_experts = EXPERTS // grp_count
    full = expert_weights_full(expert_weights, piece)
    gate_rows = expert_gate_up.shape[1]
    arrived = lax.all_to_all(
        outgoing.reshape(grp_count, local_experts * CAP, model_width),
        "grp",
        split_axis=0,
        concat_axis=0,
        tiled=True,
    )
    arrived = arrived.reshape(grp_count, local_experts, CAP, model_width).transpose(1, 0, 2, 3)
    arrived = arrived.reshape(local_experts, grp_count * CAP, model_width)
    gate_up_w = full[:, :, :gate_rows].transpose(1, 0, 2, 3).reshape(local_experts, -1, model_width)
    down_w = full[:, :, gate_rows:].transpose(1, 0, 2, 3).reshape(local_experts, -1, model_width)
    hidden_pair = jnp.einsum("erd,edf->erf", arrived, gate_up_w, preferred_element_type=jnp.float32)
    activated = (jax.nn.silu(hidden_pair[..., :FF]) * hidden_pair[..., FF:]).astype(jnp.bfloat16)
    expert_result = jnp.einsum(
        "erf,efd->erd", activated, down_w, preferred_element_type=jnp.float32
    ).astype(jnp.bfloat16)
    expert_result = expert_result.reshape(local_experts, grp_count, CAP, model_width).transpose(1, 0, 2, 3)
    returned = lax.all_to_all(
        expert_result.reshape(grp_count, local_experts * CAP, model_width),
        "grp",
        split_axis=0,
        concat_axis=0,
        tiled=True,
    ).reshape(EXPERTS * CAP, -1)
    weighted = returned[slot_index].astype(jnp.float32) * gates[0].reshape(-1)[:, None]
    moe_out = jnp.sum(weighted.reshape(tok_count, TOP, -1), axis=1)
    hidden_out = (after_attention + moe_out).astype(jnp.bfloat16)
    return (hidden_out[None], suffix_cache[None])


def solution(mesh):
    return jax.shard_map(
        local,
        mesh=mesh,
        in_specs=(
            P("grp", "tok", None),
            P("grp", None),
            P("grp", "tok", None),
            P("grp", "tok", None),
            P("grp", "tok", None),
            P(),
            P("grp", "tok"),
            P("grp", "tok"),
            P(),
            P("tok", "grp", None),
            P("tok", "grp", None),
        ),
        out_specs=(P("grp", "tok", None), P("grp", "tok", None)),
        check_vma=False,
    )
```

```python
import jax
import jax.numpy as jnp
from jax import lax
from jax.sharding import PartitionSpec as P
from jax.experimental import pallas as pl
from jax.experimental.pallas import tpu as pltpu

HEADS = 8
KV_HEADS = 4
HEAD_DIM = 64
FF = 512
EXPERTS = 32
TOP = 8
CAP = 40


epsilon = 1e-05
score_scale = 0.015625
rope_base = 10000.0
big_negative = -1e30


def rms_scale(values, gain):
    values = values.astype(jnp.float32)
    mean_square = jnp.mean(values * values, axis=-1, keepdims=True)
    return values * lax.rsqrt(mean_square + epsilon) * gain


def request_layout(group_lengths, token_index):
    ends = jnp.cumsum(group_lengths)
    starts = ends - group_lengths
    segment = jnp.sum((token_index[:, None] >= ends[None, :]).astype(jnp.int32), axis=1)
    match = segment[:, None] == jnp.arange(group_lengths.shape[0], dtype=jnp.int32)[None, :]
    offset = token_index - jnp.sum(jnp.where(match, starts[None, :], 0), axis=1)
    return (segment, offset)


def rotate(values, position):
    half_width = values.shape[-1] // 2
    frequency = rope_base ** (-jnp.arange(half_width, dtype=jnp.float32) * 2.0 / values.shape[-1])
    angle = position.astype(jnp.float32)[:, None] * frequency[None, :]
    cosine = jnp.cos(angle)[:, None, :]
    sine = jnp.sin(angle)[:, None, :]
    first = values[..., :half_width]
    second = values[..., half_width:]
    return jnp.concatenate(
        [first * cosine - second * sine, second * cosine + first * sine], axis=-1
    )


def ring_gather(block, collective_id):
    tok_count = lax.axis_size("tok")
    rows, width = block.shape
    chips = tok_count // 2
    ahead = chips // 2
    behind = chips - 1 - ahead
    mesh_ids = pl.DeviceIdType.MESH

    def kernel(x_ref, out_ref, local_sem, send_r, send_l, send_p, recv):
        me = lax.axis_index("tok")
        grp = lax.axis_index("grp")
        z = me // 2
        core = me % 2
        right = ((z + 1) % chips) * 2 + core
        left = ((z + chips - 1) % chips) * 2 + core
        peer = z * 2 + (1 - core)
        barrier = pltpu.get_barrier_semaphore()
        for other in (right, left, peer):
            pl.semaphore_signal(barrier, 1, device_id=(grp, other), device_id_type=mesh_ids)
        pl.semaphore_wait(barrier, 3)

        def remote(src, slot, sem, target):
            return pltpu.make_async_remote_copy(
                src_ref=src,
                dst_ref=out_ref.at[slot],
                send_sem=sem,
                recv_sem=recv.at[slot],
                device_id=(grp, target),
                device_id_type=mesh_ids,
            )

        own = pltpu.make_async_copy(x_ref, out_ref.at[me], local_sem.at[0])
        own.start()
        sends = [
            remote(x_ref, me, send_p.at[0], peer),
            remote(x_ref, me, send_r.at[0], right),
            remote(x_ref, me, send_l.at[0], left),
        ]
        for c in sends:
            c.start()
        peer_count = 1
        for s in range(1, ahead + 1):
            for sign, limit, sem, target in ((-1, ahead, send_r, right), (1, behind, send_l, left)):
                if s > limit:
                    continue
                slot = ((z + chips + sign * s) % chips) * 2 + core
                remote(out_ref.at[slot], slot, sem.at[0], target).wait_recv()
                if s < limit:
                    c = remote(out_ref.at[slot], slot, sem.at[s], target)
                    c.start()
                    sends.append(c)
                c = remote(out_ref.at[slot], slot, send_p.at[peer_count], peer)
                c.start()
                sends.append(c)
                peer_count += 1
        for other_z in range(chips):
            slot = other_z * 2 + (1 - core)
            remote(out_ref.at[slot], slot, send_p.at[0], peer).wait_recv()
        own.wait()
        for c in sends:
            c.wait_send()

    block_bytes = rows * width * block.dtype.itemsize
    return pl.pallas_call(
        kernel,
        out_shape=jax.ShapeDtypeStruct((tok_count, rows, width), block.dtype),
        in_specs=[pl.BlockSpec(memory_space=pltpu.VMEM)],
        out_specs=pl.BlockSpec(memory_space=pltpu.VMEM),
        scratch_shapes=[
            pltpu.SemaphoreType.DMA((1,)),
            pltpu.SemaphoreType.DMA((ahead,)),
            pltpu.SemaphoreType.DMA((ahead,)),
            pltpu.SemaphoreType.DMA((chips,)),
            pltpu.SemaphoreType.DMA((tok_count,)),
        ],
        compiler_params=pltpu.CompilerParams(collective_id=collective_id, has_side_effects=True),
        cost_estimate=pl.CostEstimate(
            flops=0, transcendentals=0, bytes_accessed=2 * tok_count * block_bytes
        ),
    )(block)


def gather_small(blocks):
    flat = jnp.concatenate([b.reshape(-1) for b in blocks])
    width = 512
    padded_rows = -(-flat.shape[0] // (16 * width)) * 16
    flat = jnp.pad(flat, (0, padded_rows * width - flat.shape[0]))
    gathered = ring_gather(flat.reshape(padded_rows, width), 1)
    gathered = gathered.reshape(gathered.shape[0], -1)
    pieces, start = [], 0
    for b in blocks:
        size = b.size
        pieces.append(gathered[:, start : start + size].reshape((-1,) + b.shape[1:]))
        start += size
    return pieces


def gather_rows(by_columns):
    return lax.all_gather(by_columns[None], "grp", axis=0, tiled=True)


def expert_weight_slices(gate_up, down):
    grp_count = lax.axis_size("grp")
    tok_count = lax.axis_size("tok")
    per = tok_count // grp_count
    pairs = []
    for g in range(grp_count):
        for e in range(tok_count):
            pairs.append((g * tok_count + e, (e // per) * tok_count + per * g + e % per))
    block = jnp.concatenate([gate_up[0], down[0]], axis=0)
    return lax.ppermute(block, ("grp", "tok"), pairs)


def expert_weights_full(block, after):
    block, _ = lax.optimization_barrier((block, after))
    grp_count = lax.axis_size("grp")
    tok_count = lax.axis_size("tok")
    gathered = lax.all_gather(block, "tok", axis=0, tiled=True)
    return gathered.reshape(grp_count, tok_count // grp_count, block.shape[0], block.shape[1])


def attend(carry, grouped, keys_values, allowed):
    best, total, mixed = carry
    key_count = keys_values.shape[0]
    key_width = KV_HEADS * HEAD_DIM
    key_heads = keys_values[:, :key_width].reshape(key_count, KV_HEADS, HEAD_DIM).transpose(1, 0, 2)
    value_heads = (
        keys_values[:, key_width:].reshape(key_count, KV_HEADS, HEAD_DIM).transpose(1, 0, 2)
    )
    scores = (
        jnp.einsum("kqd,knd->kqn", grouped, key_heads, preferred_element_type=jnp.float32)
        * score_scale
    )
    if allowed is not None:
        mask = allowed
        scores = jnp.where(mask[None], scores, big_negative)
    new_best = jnp.maximum(best, jnp.max(scores, axis=-1))
    factor = jnp.exp(best - new_best)
    probs = jnp.exp(scores - new_best[..., None])
    total = total * factor + jnp.sum(probs, axis=-1)
    mixed = mixed * factor[..., None] + jnp.einsum(
        "kqn,knd->kqd", probs.astype(jnp.bfloat16), value_heads, preferred_element_type=jnp.float32
    )
    return (new_best, total, mixed)


def local(
    hidden_in,
    lengths,
    prefix_cache,
    routes,
    gates,
    attn_gain,
    w_qkv,
    w_out,
    moe_gain,
    expert_gate_up,
    expert_down,
):
    tokens_here = hidden_in[0]
    tok_count = tokens_here.shape[0]
    axis_count = lax.axis_size("tok")
    device_place = lax.axis_index("tok")
    group_lengths = lengths[0]
    token_index = device_place * tok_count + jnp.arange(tok_count, dtype=jnp.int32)
    segment, offset = request_layout(group_lengths, token_index)
    position = prefix_cache.shape[1] * axis_count + offset
    query_width = HEADS * HEAD_DIM
    key_width = KV_HEADS * HEAD_DIM
    group_share = HEADS // KV_HEADS
    normed = rms_scale(tokens_here, attn_gain).astype(jnp.bfloat16)
    qkv_columns, out_columns = gather_small([w_qkv.T, w_out.T])
    packed_rows = gather_rows(jnp.concatenate([qkv_columns, out_columns], axis=1))
    qkv_width = qkv_columns.shape[1]
    qkv_weight = packed_rows[:, :, :qkv_width]
    out_weight = packed_rows[:, :, qkv_width:]
    expert_weights = expert_weight_slices(expert_gate_up, expert_down)
    projected = jnp.einsum(
        "ngr,gcr->nc",
        normed.reshape(tok_count, qkv_weight.shape[0], qkv_weight.shape[2]),
        qkv_weight,
        preferred_element_type=jnp.float32,
    )
    query = rotate(projected[:, :query_width].reshape(tok_count, HEADS, HEAD_DIM), position).astype(
        jnp.bfloat16
    )
    keys_new = rotate(
        projected[:, query_width : query_width + key_width].reshape(tok_count, KV_HEADS, HEAD_DIM),
        position,
    ).astype(jnp.bfloat16)
    values_new = projected[:, query_width + key_width :].astype(jnp.bfloat16)
    suffix_cache = jnp.concatenate([keys_new.reshape(tok_count, key_width), values_new], axis=1)
    row_count = tok_count * group_share
    grouped = (
        query.reshape(tok_count, KV_HEADS, group_share, HEAD_DIM)
        .transpose(1, 0, 2, 3)
        .reshape(KV_HEADS, row_count, HEAD_DIM)
    )
    start_carry = (
        jnp.full((KV_HEADS, row_count), big_negative, jnp.float32),
        jnp.zeros((KV_HEADS, row_count), jnp.float32),
        jnp.zeros((KV_HEADS, row_count, HEAD_DIM), jnp.float32),
    )
    both = ring_gather(jnp.concatenate([suffix_cache, prefix_cache[0]], axis=0), 0)
    piece = both[:, :tok_count].reshape(-1, both.shape[2])
    prefix_all = both[:, tok_count:].reshape(-1, both.shape[2])
    carry = attend(start_carry, grouped, prefix_all, None)
    key_index = jnp.arange(piece.shape[0], dtype=jnp.int32)
    key_segment, key_offset = request_layout(group_lengths, key_index)
    row_token = jnp.repeat(token_index, group_share)
    row_segment = jnp.repeat(segment, group_share)
    earlier = key_index[None, :] <= row_token[:, None]
    same_request = key_segment[None, :] == row_segment[:, None]
    carry = attend(carry, grouped, piece, earlier & same_request & (key_index[None, :] >= 0))
    best, total, mixed = carry
    attended = (mixed / total[..., None]).reshape(KV_HEADS, tok_count, group_share, HEAD_DIM)
    attended = attended.transpose(1, 0, 2, 3).reshape(tok_count, query_width).astype(jnp.bfloat16)
    projected_out = jnp.einsum(
        "ngr,gcr->nc",
        attended.reshape(tok_count, out_weight.shape[0], out_weight.shape[2]),
        out_weight,
        preferred_element_type=jnp.float32,
    )
    after_attention = tokens_here.astype(jnp.float32) + projected_out
    moe_in = rms_scale(after_attention, moe_gain).astype(jnp.bfloat16)
    model_width = moe_in.shape[1]
    flat_routes = routes[0].reshape(-1)
    onehot = (flat_routes[:, None] == jnp.arange(EXPERTS, dtype=jnp.int32)[None, :]).astype(
        jnp.int32
    )
    route_count = flat_routes.shape[0]
    lower = (
        jnp.arange(route_count, dtype=jnp.int32)[:, None]
        >= jnp.arange(route_count, dtype=jnp.int32)[None, :]
    ).astype(jnp.bfloat16)
    running = jnp.dot(lower, onehot.astype(jnp.bfloat16), preferred_element_type=jnp.float32)
    slot_rank = jnp.sum(running.astype(jnp.int32) * onehot, axis=1) - 1
    slot_index = flat_routes * CAP + slot_rank
    source_token = jnp.arange(flat_routes.shape[0], dtype=jnp.int32) // TOP
    outgoing = (
        jnp.zeros((EXPERTS * CAP, model_width), jnp.bfloat16)
        .at[slot_index]
        .set(moe_in[source_token])
    )
    grp_count = lax.axis_size("grp")
    local_experts = EXPERTS // grp_count
    full = expert_weights_full(expert_weights, piece)
    gate_rows = expert_gate_up.shape[1]
    arrived = lax.all_to_all(
        outgoing.reshape(grp_count, local_experts * CAP, model_width),
        "grp",
        split_axis=0,
        concat_axis=0,
        tiled=True,
    )
    arrived = arrived.reshape(grp_count, local_experts, CAP, model_width).transpose(1, 0, 2, 3)
    arrived = arrived.reshape(local_experts, grp_count * CAP, model_width)
    gate_up_w = full[:, :, :gate_rows].transpose(1, 0, 2, 3).reshape(local_experts, -1, model_width)
    down_w = full[:, :, gate_rows:].transpose(1, 0, 2, 3).reshape(local_experts, -1, model_width)
    hidden_pair = jnp.einsum("erd,edf->erf", arrived, gate_up_w, preferred_element_type=jnp.float32)
    activated = (jax.nn.silu(hidden_pair[..., :FF]) * hidden_pair[..., FF:]).astype(jnp.bfloat16)
    expert_result = jnp.einsum(
        "erf,efd->erd", activated, down_w, preferred_element_type=jnp.float32
    ).astype(jnp.bfloat16)
    expert_result = expert_result.reshape(local_experts, grp_count, CAP, model_width).transpose(1, 0, 2, 3)
    returned = lax.all_to_all(
        expert_result.reshape(grp_count, local_experts * CAP, model_width),
        "grp",
        split_axis=0,
        concat_axis=0,
        tiled=True,
    ).reshape(EXPERTS * CAP, -1)
    weighted = returned[slot_index].astype(jnp.float32) * gates[0].reshape(-1)[:, None]
    moe_out = jnp.sum(weighted.reshape(tok_count, TOP, -1), axis=1)
    hidden_out = (after_attention + moe_out).astype(jnp.bfloat16)
    return (hidden_out[None], suffix_cache[None])


def solution(mesh):
    return jax.shard_map(
        local,
        mesh=mesh,
        in_specs=(
            P("grp", "tok", None),
            P("grp", None),
            P("grp", "tok", None),
            P("grp", "tok", None),
            P("grp", "tok", None),
            P(),
            P("grp", "tok"),
            P("grp", "tok"),
            P(),
            P("tok", "grp", None),
            P("tok", "grp", None),
        ),
        out_specs=(P("grp", "tok", None), P("grp", "tok", None)),
        check_vma=False,
    )
```

```python
import jax
import jax.numpy as jnp
from jax import lax
from jax.sharding import PartitionSpec as P
from jax.experimental import pallas as pl
from jax.experimental.pallas import tpu as pltpu

HEADS = 8
KV_HEADS = 4
HEAD_DIM = 64
FF = 512
EXPERTS = 32
TOP = 8
CAP = 40


epsilon = 1e-05
score_scale = 0.015625
rope_base = 10000.0
big_negative = -1e30


def rms_scale(values, gain):
    values = values.astype(jnp.float32)
    mean_square = jnp.mean(values * values, axis=-1, keepdims=True)
    return values * lax.rsqrt(mean_square + epsilon) * gain


def request_layout(group_lengths, token_index):
    ends = jnp.cumsum(group_lengths)
    starts = ends - group_lengths
    segment = jnp.sum((token_index[:, None] >= ends[None, :]).astype(jnp.int32), axis=1)
    match = segment[:, None] == jnp.arange(group_lengths.shape[0], dtype=jnp.int32)[None, :]
    offset = token_index - jnp.sum(jnp.where(match, starts[None, :], 0), axis=1)
    return (segment, offset)


def rotate(values, position):
    half_width = values.shape[-1] // 2
    frequency = rope_base ** (-jnp.arange(half_width, dtype=jnp.float32) * 2.0 / values.shape[-1])
    angle = position.astype(jnp.float32)[:, None] * frequency[None, :]
    cosine = jnp.cos(angle)[:, None, :]
    sine = jnp.sin(angle)[:, None, :]
    first = values[..., :half_width]
    second = values[..., half_width:]
    return jnp.concatenate(
        [first * cosine - second * sine, second * cosine + first * sine], axis=-1
    )


def ring_gather(block, collective_id):
    tok_count = lax.axis_size("tok")
    rows, width = block.shape
    chips = tok_count // 2
    ahead = chips // 2
    behind = chips - 1 - ahead
    mesh_ids = pl.DeviceIdType.MESH

    def kernel(x_ref, out_ref, local_sem, send_r, send_l, send_p, recv):
        me = lax.axis_index("tok")
        grp = lax.axis_index("grp")
        z = me // 2
        core = me % 2
        right = ((z + 1) % chips) * 2 + core
        left = ((z + chips - 1) % chips) * 2 + core
        peer = z * 2 + (1 - core)
        barrier = pltpu.get_barrier_semaphore()
        for other in (right, left, peer):
            pl.semaphore_signal(barrier, 1, device_id=(grp, other), device_id_type=mesh_ids)
        pl.semaphore_wait(barrier, 3)

        def remote(src, slot, sem, target):
            return pltpu.make_async_remote_copy(
                src_ref=src,
                dst_ref=out_ref.at[slot],
                send_sem=sem,
                recv_sem=recv.at[slot],
                device_id=(grp, target),
                device_id_type=mesh_ids,
            )

        own = pltpu.make_async_copy(x_ref, out_ref.at[me], local_sem.at[0])
        own.start()
        sends = [
            remote(x_ref, me, send_p.at[0], peer),
            remote(x_ref, me, send_r.at[0], right),
            remote(x_ref, me, send_l.at[0], left),
        ]
        for c in sends:
            c.start()
        peer_count = 1
        for s in range(1, ahead + 1):
            for sign, limit, sem, target in ((-1, ahead, send_r, right), (1, behind, send_l, left)):
                if s > limit:
                    continue
                slot = ((z + chips + sign * s) % chips) * 2 + core
                remote(out_ref.at[slot], slot, sem.at[0], target).wait_recv()
                if s < limit:
                    c = remote(out_ref.at[slot], slot, sem.at[s], target)
                    c.start()
                    sends.append(c)
                c = remote(out_ref.at[slot], slot, send_p.at[peer_count], peer)
                c.start()
                sends.append(c)
                peer_count += 1
        for other_z in range(chips):
            slot = other_z * 2 + (1 - core)
            remote(out_ref.at[slot], slot, send_p.at[0], peer).wait_recv()
        own.wait()
        for c in sends:
            c.wait_send()

    block_bytes = rows * width * block.dtype.itemsize
    return pl.pallas_call(
        kernel,
        out_shape=jax.ShapeDtypeStruct((tok_count, rows, width), block.dtype),
        in_specs=[pl.BlockSpec(memory_space=pltpu.VMEM)],
        out_specs=pl.BlockSpec(memory_space=pltpu.VMEM),
        scratch_shapes=[
            pltpu.SemaphoreType.DMA((1,)),
            pltpu.SemaphoreType.DMA((ahead,)),
            pltpu.SemaphoreType.DMA((ahead,)),
            pltpu.SemaphoreType.DMA((chips,)),
            pltpu.SemaphoreType.DMA((tok_count,)),
        ],
        compiler_params=pltpu.CompilerParams(collective_id=collective_id, has_side_effects=True),
        cost_estimate=pl.CostEstimate(
            flops=0, transcendentals=0, bytes_accessed=2 * tok_count * block_bytes
        ),
    )(block)


def gather_small(blocks):
    flat = jnp.concatenate([b.reshape(-1) for b in blocks])
    width = 512
    padded_rows = -(-flat.shape[0] // (16 * width)) * 16
    flat = jnp.pad(flat, (0, padded_rows * width - flat.shape[0]))
    gathered = ring_gather(flat.reshape(padded_rows, width), 1)
    gathered = gathered.reshape(gathered.shape[0], -1)
    pieces, start = [], 0
    for b in blocks:
        size = b.size
        pieces.append(gathered[:, start : start + size].reshape((-1,) + b.shape[1:]))
        start += size
    return pieces


def gather_rows(by_columns):
    return lax.all_gather(by_columns[None], "grp", axis=0, tiled=True)


def expert_weight_slices(gate_up, down):
    grp_count = lax.axis_size("grp")
    tok_count = lax.axis_size("tok")
    per = tok_count // grp_count
    pairs = []
    for g in range(grp_count):
        for e in range(tok_count):
            pairs.append((g * tok_count + e, (e // per) * tok_count + per * g + e % per))
    block = jnp.concatenate([gate_up[0], down[0]], axis=0)
    return lax.ppermute(block, ("grp", "tok"), pairs)


def expert_weights_full(block, after):
    block, _ = lax.optimization_barrier((block, after))
    grp_count = lax.axis_size("grp")
    tok_count = lax.axis_size("tok")
    gathered = lax.all_gather(block, "tok", axis=0, tiled=True)
    return gathered.reshape(grp_count, tok_count // grp_count, block.shape[0], block.shape[1])


def attend(carry, grouped, keys_values, allowed):
    best, total, mixed = carry
    key_count = keys_values.shape[0]
    key_width = KV_HEADS * HEAD_DIM
    key_heads = keys_values[:, :key_width].reshape(key_count, KV_HEADS, HEAD_DIM).transpose(1, 0, 2)
    value_heads = (
        keys_values[:, key_width:].reshape(key_count, KV_HEADS, HEAD_DIM).transpose(1, 0, 2)
    )
    scores = (
        jnp.einsum("kqd,knd->kqn", grouped, key_heads, preferred_element_type=jnp.float32)
        * score_scale
    )
    if allowed is not None:
        mask = allowed
        scores = jnp.where(mask[None], scores, big_negative)
    new_best = jnp.maximum(best, jnp.max(scores, axis=-1))
    factor = jnp.exp(best - new_best)
    probs = jnp.exp(scores - new_best[..., None])
    total = total * factor + jnp.sum(probs, axis=-1)
    mixed = mixed * factor[..., None] + jnp.einsum(
        "kqn,knd->kqd", probs.astype(jnp.bfloat16), value_heads, preferred_element_type=jnp.float32
    )
    return (new_best, total, mixed)


def local(
    hidden_in,
    lengths,
    prefix_cache,
    routes,
    gates,
    attn_gain,
    w_qkv,
    w_out,
    moe_gain,
    expert_gate_up,
    expert_down,
):
    tokens_here = hidden_in[0]
    tok_count = tokens_here.shape[0]
    axis_count = lax.axis_size("tok")
    device_place = lax.axis_index("tok")
    group_lengths = lengths[0]
    token_index = device_place * tok_count + jnp.arange(tok_count, dtype=jnp.int32)
    segment, offset = request_layout(group_lengths, token_index)
    position = prefix_cache.shape[1] * axis_count + offset
    query_width = HEADS * HEAD_DIM
    key_width = KV_HEADS * HEAD_DIM
    group_share = HEADS // KV_HEADS
    normed = rms_scale(tokens_here, attn_gain).astype(jnp.bfloat16)
    qkv_columns, out_columns = gather_small([w_qkv.T, w_out.T])
    packed_rows = gather_rows(jnp.concatenate([qkv_columns, out_columns], axis=1))
    qkv_width = qkv_columns.shape[1]
    qkv_weight = packed_rows[:, :, :qkv_width]
    out_weight = packed_rows[:, :, qkv_width:]
    expert_weights = expert_weight_slices(expert_gate_up, expert_down)
    projected = jnp.einsum(
        "ngr,gcr->nc",
        normed.reshape(tok_count, qkv_weight.shape[0], qkv_weight.shape[2]),
        qkv_weight,
        preferred_element_type=jnp.float32,
    )
    query = rotate(projected[:, :query_width].reshape(tok_count, HEADS, HEAD_DIM), position).astype(
        jnp.bfloat16
    )
    keys_new = rotate(
        projected[:, query_width : query_width + key_width].reshape(tok_count, KV_HEADS, HEAD_DIM),
        position,
    ).astype(jnp.bfloat16)
    values_new = projected[:, query_width + key_width :].astype(jnp.bfloat16)
    suffix_cache = jnp.concatenate([keys_new.reshape(tok_count, key_width), values_new], axis=1)
    row_count = tok_count * group_share
    grouped = (
        query.reshape(tok_count, KV_HEADS, group_share, HEAD_DIM)
        .transpose(1, 0, 2, 3)
        .reshape(KV_HEADS, row_count, HEAD_DIM)
    )
    start_carry = (
        jnp.full((KV_HEADS, row_count), big_negative, jnp.float32),
        jnp.zeros((KV_HEADS, row_count), jnp.float32),
        jnp.zeros((KV_HEADS, row_count, HEAD_DIM), jnp.float32),
    )
    both = ring_gather(jnp.concatenate([suffix_cache, prefix_cache[0]], axis=0), 0)
    piece = both[:, :tok_count].reshape(-1, both.shape[2])
    prefix_all = both[:, tok_count:].reshape(-1, both.shape[2])
    carry = attend(start_carry, grouped, prefix_all, None)
    key_index = jnp.arange(piece.shape[0], dtype=jnp.int32)
    key_segment, key_offset = request_layout(group_lengths, key_index)
    row_token = jnp.repeat(token_index, group_share)
    row_segment = jnp.repeat(segment, group_share)
    earlier = key_index[None, :] <= row_token[:, None]
    same_request = key_segment[None, :] == row_segment[:, None]
    carry = attend(carry, grouped, piece, earlier & same_request & (key_index[None, :] >= 0))
    best, total, mixed = carry
    attended = (mixed / total[..., None]).reshape(KV_HEADS, tok_count, group_share, HEAD_DIM)
    attended = attended.transpose(1, 0, 2, 3).reshape(tok_count, query_width).astype(jnp.bfloat16)
    projected_out = jnp.einsum(
        "ngr,gcr->nc",
        attended.reshape(tok_count, out_weight.shape[0], out_weight.shape[2]),
        out_weight,
        preferred_element_type=jnp.float32,
    )
    after_attention = tokens_here.astype(jnp.float32) + projected_out
    moe_in = rms_scale(after_attention, moe_gain).astype(jnp.bfloat16)
    model_width = moe_in.shape[1]
    flat_routes = routes[0].reshape(-1)
    onehot = (flat_routes[:, None] == jnp.arange(EXPERTS, dtype=jnp.int32)[None, :]).astype(
        jnp.int32
    )
    route_count = flat_routes.shape[0]
    lower = (
        jnp.arange(route_count, dtype=jnp.int32)[:, None]
        >= jnp.arange(route_count, dtype=jnp.int32)[None, :]
    ).astype(jnp.bfloat16)
    running = jnp.dot(lower, onehot.astype(jnp.bfloat16), preferred_element_type=jnp.float32)
    slot_rank = jnp.sum(running.astype(jnp.int32) * onehot, axis=1) - 1
    slot_index = flat_routes * CAP + slot_rank
    source_token = jnp.arange(flat_routes.shape[0], dtype=jnp.int32) // TOP
    slot_of_route = (
        slot_index[None, :] == jnp.arange(EXPERTS * CAP, dtype=jnp.int32)[:, None]
    ).astype(jnp.bfloat16)
    token_of_route = (
        source_token[:, None] == jnp.arange(tok_count, dtype=jnp.int32)[None, :]
    ).astype(jnp.bfloat16)
    slot_token = jnp.dot(slot_of_route, token_of_route, preferred_element_type=jnp.float32)
    outgoing = jnp.dot(
        slot_token.astype(jnp.bfloat16), moe_in, preferred_element_type=jnp.float32
    ).astype(jnp.bfloat16)
    grp_count = lax.axis_size("grp")
    local_experts = EXPERTS // grp_count
    full = expert_weights_full(expert_weights, piece)
    gate_rows = expert_gate_up.shape[1]
    arrived = lax.all_to_all(
        outgoing.reshape(grp_count, local_experts * CAP, model_width),
        "grp",
        split_axis=0,
        concat_axis=0,
        tiled=True,
    )
    arrived = arrived.reshape(grp_count, local_experts, CAP, model_width).transpose(1, 0, 2, 3)
    arrived = arrived.reshape(local_experts, grp_count * CAP, model_width)
    gate_up_w = full[:, :, :gate_rows].transpose(1, 0, 2, 3).reshape(local_experts, -1, model_width)
    down_w = full[:, :, gate_rows:].transpose(1, 0, 2, 3).reshape(local_experts, -1, model_width)
    hidden_pair = jnp.einsum("erd,edf->erf", arrived, gate_up_w, preferred_element_type=jnp.float32)
    activated = (jax.nn.silu(hidden_pair[..., :FF]) * hidden_pair[..., FF:]).astype(jnp.bfloat16)
    expert_result = jnp.einsum(
        "erf,efd->erd", activated, down_w, preferred_element_type=jnp.float32
    ).astype(jnp.bfloat16)
    expert_result = expert_result.reshape(local_experts, grp_count, CAP, model_width).transpose(1, 0, 2, 3)
    returned = lax.all_to_all(
        expert_result.reshape(grp_count, local_experts * CAP, model_width),
        "grp",
        split_axis=0,
        concat_axis=0,
        tiled=True,
    ).reshape(EXPERTS * CAP, -1)
    weighted = returned[slot_index].astype(jnp.float32) * gates[0].reshape(-1)[:, None]
    moe_out = jnp.sum(weighted.reshape(tok_count, TOP, -1), axis=1)
    hidden_out = (after_attention + moe_out).astype(jnp.bfloat16)
    return (hidden_out[None], suffix_cache[None])


def solution(mesh):
    return jax.shard_map(
        local,
        mesh=mesh,
        in_specs=(
            P("grp", "tok", None),
            P("grp", None),
            P("grp", "tok", None),
            P("grp", "tok", None),
            P("grp", "tok", None),
            P(),
            P("grp", "tok"),
            P("grp", "tok"),
            P(),
            P("tok", "grp", None),
            P("tok", "grp", None),
        ),
        out_specs=(P("grp", "tok", None), P("grp", "tok", None)),
        check_vma=False,
    )
```

```python
import jax
import jax.numpy as jnp
from jax import lax
from jax.sharding import PartitionSpec as P
from jax.experimental import pallas as pl
from jax.experimental.pallas import tpu as pltpu

HEADS = 8
KV_HEADS = 4
HEAD_DIM = 64
FF = 512
EXPERTS = 32
TOP = 8
CAP = 40


epsilon = 1e-05
score_scale = 0.015625
rope_base = 10000.0
big_negative = -1e30


def rms_scale(values, gain):
    values = values.astype(jnp.float32)
    mean_square = jnp.mean(values * values, axis=-1, keepdims=True)
    return values * lax.rsqrt(mean_square + epsilon) * gain


def request_layout(group_lengths, token_index):
    ends = jnp.cumsum(group_lengths)
    starts = ends - group_lengths
    segment = jnp.sum((token_index[:, None] >= ends[None, :]).astype(jnp.int32), axis=1)
    match = segment[:, None] == jnp.arange(group_lengths.shape[0], dtype=jnp.int32)[None, :]
    offset = token_index - jnp.sum(jnp.where(match, starts[None, :], 0), axis=1)
    return (segment, offset)


def rotate(values, position):
    half_width = values.shape[-1] // 2
    frequency = rope_base ** (-jnp.arange(half_width, dtype=jnp.float32) * 2.0 / values.shape[-1])
    angle = position.astype(jnp.float32)[:, None] * frequency[None, :]
    cosine = jnp.cos(angle)[:, None, :]
    sine = jnp.sin(angle)[:, None, :]
    first = values[..., :half_width]
    second = values[..., half_width:]
    return jnp.concatenate(
        [first * cosine - second * sine, second * cosine + first * sine], axis=-1
    )


def ring_gather(block, collective_id):
    tok_count = lax.axis_size("tok")
    rows, width = block.shape
    chips = tok_count // 2
    ahead = chips // 2
    behind = chips - 1 - ahead
    mesh_ids = pl.DeviceIdType.MESH

    def kernel(x_ref, out_ref, local_sem, send_r, send_l, send_p, recv):
        me = lax.axis_index("tok")
        grp = lax.axis_index("grp")
        z = me // 2
        core = me % 2
        right = ((z + 1) % chips) * 2 + core
        left = ((z + chips - 1) % chips) * 2 + core
        peer = z * 2 + (1 - core)
        barrier = pltpu.get_barrier_semaphore()
        for other in (right, left, peer):
            pl.semaphore_signal(barrier, 1, device_id=(grp, other), device_id_type=mesh_ids)
        pl.semaphore_wait(barrier, 3)

        def remote(src, slot, sem, target):
            return pltpu.make_async_remote_copy(
                src_ref=src,
                dst_ref=out_ref.at[slot],
                send_sem=sem,
                recv_sem=recv.at[slot],
                device_id=(grp, target),
                device_id_type=mesh_ids,
            )

        own = pltpu.make_async_copy(x_ref, out_ref.at[me], local_sem.at[0])
        own.start()
        sends = [
            remote(x_ref, me, send_p.at[0], peer),
            remote(x_ref, me, send_r.at[0], right),
            remote(x_ref, me, send_l.at[0], left),
        ]
        for c in sends:
            c.start()
        peer_count = 1
        for s in range(1, ahead + 1):
            for sign, limit, sem, target in ((-1, ahead, send_r, right), (1, behind, send_l, left)):
                if s > limit:
                    continue
                slot = ((z + chips + sign * s) % chips) * 2 + core
                remote(out_ref.at[slot], slot, sem.at[0], target).wait_recv()
                if s < limit:
                    c = remote(out_ref.at[slot], slot, sem.at[s], target)
                    c.start()
                    sends.append(c)
                c = remote(out_ref.at[slot], slot, send_p.at[peer_count], peer)
                c.start()
                sends.append(c)
                peer_count += 1
        for other_z in range(chips):
            slot = other_z * 2 + (1 - core)
            remote(out_ref.at[slot], slot, send_p.at[0], peer).wait_recv()
        own.wait()
        for c in sends:
            c.wait_send()

    block_bytes = rows * width * block.dtype.itemsize
    return pl.pallas_call(
        kernel,
        out_shape=jax.ShapeDtypeStruct((tok_count, rows, width), block.dtype),
        in_specs=[pl.BlockSpec(memory_space=pltpu.VMEM)],
        out_specs=pl.BlockSpec(memory_space=pltpu.VMEM),
        scratch_shapes=[
            pltpu.SemaphoreType.DMA((1,)),
            pltpu.SemaphoreType.DMA((ahead,)),
            pltpu.SemaphoreType.DMA((ahead,)),
            pltpu.SemaphoreType.DMA((chips,)),
            pltpu.SemaphoreType.DMA((tok_count,)),
        ],
        compiler_params=pltpu.CompilerParams(collective_id=collective_id, has_side_effects=True),
        cost_estimate=pl.CostEstimate(
            flops=0, transcendentals=0, bytes_accessed=2 * tok_count * block_bytes
        ),
    )(block)


def gather_small(blocks):
    flat = jnp.concatenate([b.reshape(-1) for b in blocks])
    width = 512
    padded_rows = -(-flat.shape[0] // (16 * width)) * 16
    flat = jnp.pad(flat, (0, padded_rows * width - flat.shape[0]))
    gathered = ring_gather(flat.reshape(padded_rows, width), 1)
    gathered = gathered.reshape(gathered.shape[0], -1)
    pieces, start = [], 0
    for b in blocks:
        size = b.size
        pieces.append(gathered[:, start : start + size].reshape((-1,) + b.shape[1:]))
        start += size
    return pieces


def gather_rows(by_columns):
    return lax.all_gather(by_columns[None], "grp", axis=0, tiled=True)


def expert_weight_slices(gate_up, down):
    grp_count = lax.axis_size("grp")
    tok_count = lax.axis_size("tok")
    per = tok_count // grp_count
    pairs = []
    for g in range(grp_count):
        for e in range(tok_count):
            pairs.append((g * tok_count + e, (e // per) * tok_count + per * g + e % per))
    block = jnp.concatenate([gate_up[0], down[0]], axis=0)
    return lax.ppermute(block, ("grp", "tok"), pairs)


def expert_weights_full(block, after):
    block, _ = lax.optimization_barrier((block, after))
    grp_count = lax.axis_size("grp")
    tok_count = lax.axis_size("tok")
    gathered = lax.all_gather(block, "tok", axis=0, tiled=True)
    return gathered.reshape(grp_count, tok_count // grp_count, block.shape[0], block.shape[1])


def attend(carry, grouped, keys_values, allowed):
    best, total, mixed = carry
    key_count = keys_values.shape[0]
    key_width = KV_HEADS * HEAD_DIM
    key_heads = keys_values[:, :key_width].reshape(key_count, KV_HEADS, HEAD_DIM).transpose(1, 0, 2)
    value_heads = (
        keys_values[:, key_width:].reshape(key_count, KV_HEADS, HEAD_DIM).transpose(1, 0, 2)
    )
    scores = (
        jnp.einsum("kqd,knd->kqn", grouped, key_heads, preferred_element_type=jnp.float32)
        * score_scale
    )
    if allowed is not None:
        mask = allowed
        scores = jnp.where(mask[None], scores, big_negative)
    new_best = jnp.maximum(best, jnp.max(scores, axis=-1))
    factor = jnp.exp(best - new_best)
    probs = jnp.exp(scores - new_best[..., None])
    total = total * factor + jnp.sum(probs, axis=-1)
    mixed = mixed * factor[..., None] + jnp.einsum(
        "kqn,knd->kqd", probs.astype(jnp.bfloat16), value_heads, preferred_element_type=jnp.float32
    )
    return (new_best, total, mixed)


def local(
    hidden_in,
    lengths,
    prefix_cache,
    routes,
    gates,
    attn_gain,
    w_qkv,
    w_out,
    moe_gain,
    expert_gate_up,
    expert_down,
):
    tokens_here = hidden_in[0]
    tok_count = tokens_here.shape[0]
    axis_count = lax.axis_size("tok")
    device_place = lax.axis_index("tok")
    group_lengths = lengths[0]
    token_index = device_place * tok_count + jnp.arange(tok_count, dtype=jnp.int32)
    segment, offset = request_layout(group_lengths, token_index)
    position = prefix_cache.shape[1] * axis_count + offset
    query_width = HEADS * HEAD_DIM
    key_width = KV_HEADS * HEAD_DIM
    group_share = HEADS // KV_HEADS
    normed = rms_scale(tokens_here, attn_gain).astype(jnp.bfloat16)
    qkv_columns, out_columns = gather_small([w_qkv.T, w_out.T])
    packed_rows = gather_rows(jnp.concatenate([qkv_columns, out_columns], axis=1))
    qkv_width = qkv_columns.shape[1]
    qkv_weight = packed_rows[:, :, :qkv_width]
    out_weight = packed_rows[:, :, qkv_width:]
    expert_weights = expert_weight_slices(expert_gate_up, expert_down)
    projected = jnp.einsum(
        "ngr,gcr->nc",
        normed.reshape(tok_count, qkv_weight.shape[0], qkv_weight.shape[2]),
        qkv_weight,
        preferred_element_type=jnp.float32,
    )
    query = rotate(projected[:, :query_width].reshape(tok_count, HEADS, HEAD_DIM), position).astype(
        jnp.bfloat16
    )
    keys_new = rotate(
        projected[:, query_width : query_width + key_width].reshape(tok_count, KV_HEADS, HEAD_DIM),
        position,
    ).astype(jnp.bfloat16)
    values_new = projected[:, query_width + key_width :].astype(jnp.bfloat16)
    suffix_cache = jnp.concatenate([keys_new.reshape(tok_count, key_width), values_new], axis=1)
    row_count = tok_count * group_share
    grouped = (
        query.reshape(tok_count, KV_HEADS, group_share, HEAD_DIM)
        .transpose(1, 0, 2, 3)
        .reshape(KV_HEADS, row_count, HEAD_DIM)
    )
    start_carry = (
        jnp.full((KV_HEADS, row_count), big_negative, jnp.float32),
        jnp.zeros((KV_HEADS, row_count), jnp.float32),
        jnp.zeros((KV_HEADS, row_count, HEAD_DIM), jnp.float32),
    )
    both = ring_gather(jnp.concatenate([suffix_cache, prefix_cache[0]], axis=0), 0)
    piece = both[:, :tok_count].reshape(-1, both.shape[2])
    prefix_all = both[:, tok_count:].reshape(-1, both.shape[2])
    carry = attend(start_carry, grouped, prefix_all, None)
    key_index = jnp.arange(piece.shape[0], dtype=jnp.int32)
    key_segment, key_offset = request_layout(group_lengths, key_index)
    row_token = jnp.repeat(token_index, group_share)
    row_segment = jnp.repeat(segment, group_share)
    earlier = key_index[None, :] <= row_token[:, None]
    same_request = key_segment[None, :] == row_segment[:, None]
    carry = attend(carry, grouped, piece, earlier & same_request & (key_index[None, :] >= 0))
    best, total, mixed = carry
    attended = (mixed / total[..., None]).reshape(KV_HEADS, tok_count, group_share, HEAD_DIM)
    attended = attended.transpose(1, 0, 2, 3).reshape(tok_count, query_width).astype(jnp.bfloat16)
    projected_out = jnp.einsum(
        "ngr,gcr->nc",
        attended.reshape(tok_count, out_weight.shape[0], out_weight.shape[2]),
        out_weight,
        preferred_element_type=jnp.float32,
    )
    after_attention = tokens_here.astype(jnp.float32) + projected_out
    moe_in = rms_scale(after_attention, moe_gain).astype(jnp.bfloat16)
    model_width = moe_in.shape[1]
    flat_routes = routes[0].reshape(-1)
    onehot = (flat_routes[:, None] == jnp.arange(EXPERTS, dtype=jnp.int32)[None, :]).astype(
        jnp.int32
    )
    route_count = flat_routes.shape[0]
    lower = (
        jnp.arange(route_count, dtype=jnp.int32)[:, None]
        >= jnp.arange(route_count, dtype=jnp.int32)[None, :]
    ).astype(jnp.bfloat16)
    running = jnp.dot(lower, onehot.astype(jnp.bfloat16), preferred_element_type=jnp.float32)
    slot_rank = jnp.sum(running.astype(jnp.int32) * onehot, axis=1) - 1
    slot_index = flat_routes * CAP + slot_rank
    source_token = jnp.arange(flat_routes.shape[0], dtype=jnp.int32) // TOP
    slot_of_route = (
        slot_index[None, :] == jnp.arange(EXPERTS * CAP, dtype=jnp.int32)[:, None]
    ).astype(jnp.bfloat16)
    token_of_route = (
        source_token[:, None] == jnp.arange(tok_count, dtype=jnp.int32)[None, :]
    ).astype(jnp.bfloat16)
    slot_token = jnp.dot(slot_of_route, token_of_route, preferred_element_type=jnp.float32)
    outgoing = jnp.dot(
        slot_token.astype(jnp.bfloat16), moe_in, preferred_element_type=jnp.float32
    ).astype(jnp.bfloat16)
    grp_count = lax.axis_size("grp")
    local_experts = EXPERTS // grp_count
    full = expert_weights_full(expert_weights, piece)
    gate_rows = expert_gate_up.shape[1]
    arrived = lax.all_to_all(
        outgoing.reshape(grp_count, local_experts * CAP, model_width),
        "grp",
        split_axis=0,
        concat_axis=0,
        tiled=True,
    )
    arrived = arrived.reshape(grp_count, local_experts, CAP, model_width).transpose(1, 0, 2, 3)
    arrived = arrived.reshape(local_experts, grp_count * CAP, model_width)
    gate_up_w = full[:, :, :gate_rows].transpose(1, 0, 2, 3).reshape(local_experts, -1, model_width)
    down_w = full[:, :, gate_rows:].transpose(1, 0, 2, 3).reshape(local_experts, -1, model_width)
    hidden_pair = jnp.einsum("erd,edf->erf", arrived, gate_up_w, preferred_element_type=jnp.float32)
    activated = (jax.nn.silu(hidden_pair[..., :FF]) * hidden_pair[..., FF:]).astype(jnp.bfloat16)
    expert_result = jnp.einsum(
        "erf,efd->erd", activated, down_w, preferred_element_type=jnp.float32
    ).astype(jnp.bfloat16)
    expert_result = expert_result.reshape(local_experts, grp_count, CAP, model_width).transpose(1, 0, 2, 3)
    returned = lax.all_to_all(
        expert_result.reshape(grp_count, local_experts * CAP, model_width),
        "grp",
        split_axis=0,
        concat_axis=0,
        tiled=True,
    ).reshape(EXPERTS * CAP, -1)
    gate_of_route = token_of_route.astype(jnp.float32).T * gates[0].reshape(-1)[None, :]
    combine = jnp.dot(
        gate_of_route,
        slot_of_route.astype(jnp.float32).T,
        precision=lax.Precision.HIGHEST,
        preferred_element_type=jnp.float32,
    )
    moe_out = jnp.dot(
        combine,
        returned.astype(jnp.float32),
        precision=lax.Precision.HIGHEST,
        preferred_element_type=jnp.float32,
    )
    hidden_out = (after_attention + moe_out).astype(jnp.bfloat16)
    return (hidden_out[None], suffix_cache[None])


def solution(mesh):
    return jax.shard_map(
        local,
        mesh=mesh,
        in_specs=(
            P("grp", "tok", None),
            P("grp", None),
            P("grp", "tok", None),
            P("grp", "tok", None),
            P("grp", "tok", None),
            P(),
            P("grp", "tok"),
            P("grp", "tok"),
            P(),
            P("tok", "grp", None),
            P("tok", "grp", None),
        ),
        out_specs=(P("grp", "tok", None), P("grp", "tok", None)),
        check_vma=False,
    )
```

```python
import jax
import jax.numpy as jnp
from jax import lax
from jax.sharding import PartitionSpec as P
from jax.experimental import pallas as pl
from jax.experimental.pallas import tpu as pltpu

HEADS = 8
KV_HEADS = 4
HEAD_DIM = 64
FF = 512
EXPERTS = 32
TOP = 8
CAP = 40


epsilon = 1e-05
score_scale = 0.015625
rope_base = 10000.0
big_negative = -1e30


def rms_scale(values, gain):
    values = values.astype(jnp.float32)
    mean_square = jnp.mean(values * values, axis=-1, keepdims=True)
    return values * lax.rsqrt(mean_square + epsilon) * gain


def request_layout(group_lengths, token_index):
    ends = jnp.cumsum(group_lengths)
    starts = ends - group_lengths
    segment = jnp.sum((token_index[:, None] >= ends[None, :]).astype(jnp.int32), axis=1)
    match = segment[:, None] == jnp.arange(group_lengths.shape[0], dtype=jnp.int32)[None, :]
    offset = token_index - jnp.sum(jnp.where(match, starts[None, :], 0), axis=1)
    return (segment, offset)


def rotate(values, position):
    half_width = values.shape[-1] // 2
    frequency = rope_base ** (-jnp.arange(half_width, dtype=jnp.float32) * 2.0 / values.shape[-1])
    angle = position.astype(jnp.float32)[:, None] * frequency[None, :]
    cosine = jnp.cos(angle)[:, None, :]
    sine = jnp.sin(angle)[:, None, :]
    first = values[..., :half_width]
    second = values[..., half_width:]
    return jnp.concatenate(
        [first * cosine - second * sine, second * cosine + first * sine], axis=-1
    )


def ring_gather(block, collective_id):
    tok_count = lax.axis_size("tok")
    rows, width = block.shape
    chips = tok_count // 2
    ahead = chips // 2
    behind = chips - 1 - ahead
    mesh_ids = pl.DeviceIdType.MESH

    def kernel(x_ref, out_ref, local_sem, send_r, send_l, send_p, recv):
        me = lax.axis_index("tok")
        grp = lax.axis_index("grp")
        z = me // 2
        core = me % 2
        right = ((z + 1) % chips) * 2 + core
        left = ((z + chips - 1) % chips) * 2 + core
        peer = z * 2 + (1 - core)
        barrier = pltpu.get_barrier_semaphore()
        for other in (right, left, peer):
            pl.semaphore_signal(barrier, 1, device_id=(grp, other), device_id_type=mesh_ids)
        pl.semaphore_wait(barrier, 3)

        def remote(src, slot, sem, target):
            return pltpu.make_async_remote_copy(
                src_ref=src,
                dst_ref=out_ref.at[slot],
                send_sem=sem,
                recv_sem=recv.at[slot],
                device_id=(grp, target),
                device_id_type=mesh_ids,
            )

        own = pltpu.make_async_copy(x_ref, out_ref.at[me], local_sem.at[0])
        own.start()
        sends = [
            remote(x_ref, me, send_p.at[0], peer),
            remote(x_ref, me, send_r.at[0], right),
            remote(x_ref, me, send_l.at[0], left),
        ]
        for c in sends:
            c.start()
        peer_count = 1
        for s in range(1, ahead + 1):
            for sign, limit, sem, target in ((-1, ahead, send_r, right), (1, behind, send_l, left)):
                if s > limit:
                    continue
                slot = ((z + chips + sign * s) % chips) * 2 + core
                remote(out_ref.at[slot], slot, sem.at[0], target).wait_recv()
                if s < limit:
                    c = remote(out_ref.at[slot], slot, sem.at[s], target)
                    c.start()
                    sends.append(c)
                c = remote(out_ref.at[slot], slot, send_p.at[peer_count], peer)
                c.start()
                sends.append(c)
                peer_count += 1
        for other_z in range(chips):
            slot = other_z * 2 + (1 - core)
            remote(out_ref.at[slot], slot, send_p.at[0], peer).wait_recv()
        own.wait()
        for c in sends:
            c.wait_send()

    block_bytes = rows * width * block.dtype.itemsize
    return pl.pallas_call(
        kernel,
        out_shape=jax.ShapeDtypeStruct((tok_count, rows, width), block.dtype),
        in_specs=[pl.BlockSpec(memory_space=pltpu.VMEM)],
        out_specs=pl.BlockSpec(memory_space=pltpu.VMEM),
        scratch_shapes=[
            pltpu.SemaphoreType.DMA((1,)),
            pltpu.SemaphoreType.DMA((ahead,)),
            pltpu.SemaphoreType.DMA((ahead,)),
            pltpu.SemaphoreType.DMA((chips,)),
            pltpu.SemaphoreType.DMA((tok_count,)),
        ],
        compiler_params=pltpu.CompilerParams(collective_id=collective_id, has_side_effects=True),
        cost_estimate=pl.CostEstimate(
            flops=0, transcendentals=0, bytes_accessed=2 * tok_count * block_bytes
        ),
    )(block)


def direct_gather(block, collective_id):
    tok_count = lax.axis_size("tok")
    rows, width = block.shape
    mesh_ids = pl.DeviceIdType.MESH

    def kernel(x_ref, out_ref, local_sem, send_sems, recv):
        me = lax.axis_index("tok")
        grp = lax.axis_index("grp")
        barrier = pltpu.get_barrier_semaphore()

        def other_of(i):
            return (me + 1 + i) % tok_count

        def remote(src, slot, sem, target):
            return pltpu.make_async_remote_copy(
                src_ref=src,
                dst_ref=out_ref.at[slot],
                send_sem=sem,
                recv_sem=recv.at[slot],
                device_id=(grp, target),
                device_id_type=mesh_ids,
            )

        def greet(i, c):
            pl.semaphore_signal(barrier, 1, device_id=(grp, other_of(i)), device_id_type=mesh_ids)
            return c

        lax.fori_loop(0, tok_count - 1, greet, 0)
        pl.semaphore_wait(barrier, tok_count - 1)
        own = pltpu.make_async_copy(x_ref, out_ref.at[me], local_sem.at[0])
        own.start()

        def send(i, c):
            remote(x_ref, me, send_sems.at[i], other_of(i)).start()
            return c

        lax.fori_loop(0, tok_count - 1, send, 0)

        def arrive(i, c):
            source = other_of(i)
            remote(out_ref.at[source], source, send_sems.at[0], source).wait_recv()
            return c

        lax.fori_loop(0, tok_count - 1, arrive, 0)
        own.wait()

        def sent(i, c):
            remote(x_ref, me, send_sems.at[i], other_of(i)).wait_send()
            return c

        lax.fori_loop(0, tok_count - 1, sent, 0)

    block_bytes = rows * width * block.dtype.itemsize
    return pl.pallas_call(
        kernel,
        out_shape=jax.ShapeDtypeStruct((tok_count, rows, width), block.dtype),
        in_specs=[pl.BlockSpec(memory_space=pltpu.VMEM)],
        out_specs=pl.BlockSpec(memory_space=pltpu.VMEM),
        scratch_shapes=[
            pltpu.SemaphoreType.DMA((1,)),
            pltpu.SemaphoreType.DMA((tok_count,)),
            pltpu.SemaphoreType.DMA((tok_count,)),
        ],
        compiler_params=pltpu.CompilerParams(collective_id=collective_id, has_side_effects=True),
        cost_estimate=pl.CostEstimate(
            flops=0, transcendentals=0, bytes_accessed=2 * tok_count * block_bytes
        ),
    )(block)


def gather_small(blocks):
    flat = jnp.concatenate([b.reshape(-1) for b in blocks])
    width = 512
    padded_rows = -(-flat.shape[0] // (16 * width)) * 16
    flat = jnp.pad(flat, (0, padded_rows * width - flat.shape[0]))
    gathered = direct_gather(flat.reshape(padded_rows, width), 1)
    gathered = gathered.reshape(gathered.shape[0], -1)
    pieces, start = [], 0
    for b in blocks:
        size = b.size
        pieces.append(gathered[:, start : start + size].reshape((-1,) + b.shape[1:]))
        start += size
    return pieces


def gather_rows(by_columns):
    return lax.all_gather(by_columns[None], "grp", axis=0, tiled=True)


def expert_weight_slices(gate_up, down):
    grp_count = lax.axis_size("grp")
    tok_count = lax.axis_size("tok")
    per = tok_count // grp_count
    pairs = []
    for g in range(grp_count):
        for e in range(tok_count):
            pairs.append((g * tok_count + e, (e // per) * tok_count + per * g + e % per))
    block = jnp.concatenate([gate_up[0], down[0]], axis=0)
    return lax.ppermute(block, ("grp", "tok"), pairs)


def expert_weights_full(block, after):
    block, _ = lax.optimization_barrier((block, after))
    grp_count = lax.axis_size("grp")
    tok_count = lax.axis_size("tok")
    gathered = lax.all_gather(block, "tok", axis=0, tiled=True)
    return gathered.reshape(grp_count, tok_count // grp_count, block.shape[0], block.shape[1])


def attend(carry, grouped, keys_values, allowed):
    best, total, mixed = carry
    key_count = keys_values.shape[0]
    key_width = KV_HEADS * HEAD_DIM
    key_heads = keys_values[:, :key_width].reshape(key_count, KV_HEADS, HEAD_DIM).transpose(1, 0, 2)
    value_heads = (
        keys_values[:, key_width:].reshape(key_count, KV_HEADS, HEAD_DIM).transpose(1, 0, 2)
    )
    scores = (
        jnp.einsum("kqd,knd->kqn", grouped, key_heads, preferred_element_type=jnp.float32)
        * score_scale
    )
    if allowed is not None:
        mask = allowed
        scores = jnp.where(mask[None], scores, big_negative)
    new_best = jnp.maximum(best, jnp.max(scores, axis=-1))
    factor = jnp.exp(best - new_best)
    probs = jnp.exp(scores - new_best[..., None])
    total = total * factor + jnp.sum(probs, axis=-1)
    mixed = mixed * factor[..., None] + jnp.einsum(
        "kqn,knd->kqd", probs.astype(jnp.bfloat16), value_heads, preferred_element_type=jnp.float32
    )
    return (new_best, total, mixed)


def local(
    hidden_in,
    lengths,
    prefix_cache,
    routes,
    gates,
    attn_gain,
    w_qkv,
    w_out,
    moe_gain,
    expert_gate_up,
    expert_down,
):
    tokens_here = hidden_in[0]
    tok_count = tokens_here.shape[0]
    axis_count = lax.axis_size("tok")
    device_place = lax.axis_index("tok")
    group_lengths = lengths[0]
    token_index = device_place * tok_count + jnp.arange(tok_count, dtype=jnp.int32)
    segment, offset = request_layout(group_lengths, token_index)
    position = prefix_cache.shape[1] * axis_count + offset
    query_width = HEADS * HEAD_DIM
    key_width = KV_HEADS * HEAD_DIM
    group_share = HEADS // KV_HEADS
    normed = rms_scale(tokens_here, attn_gain).astype(jnp.bfloat16)
    qkv_columns, out_columns = gather_small([w_qkv.T, w_out.T])
    packed_rows = gather_rows(jnp.concatenate([qkv_columns, out_columns], axis=1))
    qkv_width = qkv_columns.shape[1]
    qkv_weight = packed_rows[:, :, :qkv_width]
    out_weight = packed_rows[:, :, qkv_width:]
    expert_weights = expert_weight_slices(expert_gate_up, expert_down)
    projected = jnp.einsum(
        "ngr,gcr->nc",
        normed.reshape(tok_count, qkv_weight.shape[0], qkv_weight.shape[2]),
        qkv_weight,
        preferred_element_type=jnp.float32,
    )
    query = rotate(projected[:, :query_width].reshape(tok_count, HEADS, HEAD_DIM), position).astype(
        jnp.bfloat16
    )
    keys_new = rotate(
        projected[:, query_width : query_width + key_width].reshape(tok_count, KV_HEADS, HEAD_DIM),
        position,
    ).astype(jnp.bfloat16)
    values_new = projected[:, query_width + key_width :].astype(jnp.bfloat16)
    suffix_cache = jnp.concatenate([keys_new.reshape(tok_count, key_width), values_new], axis=1)
    row_count = tok_count * group_share
    grouped = (
        query.reshape(tok_count, KV_HEADS, group_share, HEAD_DIM)
        .transpose(1, 0, 2, 3)
        .reshape(KV_HEADS, row_count, HEAD_DIM)
    )
    start_carry = (
        jnp.full((KV_HEADS, row_count), big_negative, jnp.float32),
        jnp.zeros((KV_HEADS, row_count), jnp.float32),
        jnp.zeros((KV_HEADS, row_count, HEAD_DIM), jnp.float32),
    )
    both = ring_gather(jnp.concatenate([suffix_cache, prefix_cache[0]], axis=0), 0)
    piece = both[:, :tok_count].reshape(-1, both.shape[2])
    prefix_all = both[:, tok_count:].reshape(-1, both.shape[2])
    carry = attend(start_carry, grouped, prefix_all, None)
    key_index = jnp.arange(piece.shape[0], dtype=jnp.int32)
    key_segment, key_offset = request_layout(group_lengths, key_index)
    row_token = jnp.repeat(token_index, group_share)
    row_segment = jnp.repeat(segment, group_share)
    earlier = key_index[None, :] <= row_token[:, None]
    same_request = key_segment[None, :] == row_segment[:, None]
    carry = attend(carry, grouped, piece, earlier & same_request & (key_index[None, :] >= 0))
    best, total, mixed = carry
    attended = (mixed / total[..., None]).reshape(KV_HEADS, tok_count, group_share, HEAD_DIM)
    attended = attended.transpose(1, 0, 2, 3).reshape(tok_count, query_width).astype(jnp.bfloat16)
    projected_out = jnp.einsum(
        "ngr,gcr->nc",
        attended.reshape(tok_count, out_weight.shape[0], out_weight.shape[2]),
        out_weight,
        preferred_element_type=jnp.float32,
    )
    after_attention = tokens_here.astype(jnp.float32) + projected_out
    moe_in = rms_scale(after_attention, moe_gain).astype(jnp.bfloat16)
    model_width = moe_in.shape[1]
    flat_routes = routes[0].reshape(-1)
    onehot = (flat_routes[:, None] == jnp.arange(EXPERTS, dtype=jnp.int32)[None, :]).astype(
        jnp.int32
    )
    route_count = flat_routes.shape[0]
    lower = (
        jnp.arange(route_count, dtype=jnp.int32)[:, None]
        >= jnp.arange(route_count, dtype=jnp.int32)[None, :]
    ).astype(jnp.bfloat16)
    running = jnp.dot(lower, onehot.astype(jnp.bfloat16), preferred_element_type=jnp.float32)
    slot_rank = jnp.sum(running.astype(jnp.int32) * onehot, axis=1) - 1
    slot_index = flat_routes * CAP + slot_rank
    source_token = jnp.arange(flat_routes.shape[0], dtype=jnp.int32) // TOP
    slot_of_route = (
        slot_index[None, :] == jnp.arange(EXPERTS * CAP, dtype=jnp.int32)[:, None]
    ).astype(jnp.bfloat16)
    token_of_route = (
        source_token[:, None] == jnp.arange(tok_count, dtype=jnp.int32)[None, :]
    ).astype(jnp.bfloat16)
    slot_token = jnp.dot(slot_of_route, token_of_route, preferred_element_type=jnp.float32)
    outgoing = jnp.dot(
        slot_token.astype(jnp.bfloat16), moe_in, preferred_element_type=jnp.float32
    ).astype(jnp.bfloat16)
    grp_count = lax.axis_size("grp")
    local_experts = EXPERTS // grp_count
    full = expert_weights_full(expert_weights, piece)
    gate_rows = expert_gate_up.shape[1]
    arrived = lax.all_to_all(
        outgoing.reshape(grp_count, local_experts * CAP, model_width),
        "grp",
        split_axis=0,
        concat_axis=0,
        tiled=True,
    )
    arrived = arrived.reshape(grp_count, local_experts, CAP, model_width).transpose(1, 0, 2, 3)
    arrived = arrived.reshape(local_experts, grp_count * CAP, model_width)
    gate_up_w = full[:, :, :gate_rows].transpose(1, 0, 2, 3).reshape(local_experts, -1, model_width)
    down_w = full[:, :, gate_rows:].transpose(1, 0, 2, 3).reshape(local_experts, -1, model_width)
    hidden_pair = jnp.einsum("erd,edf->erf", arrived, gate_up_w, preferred_element_type=jnp.float32)
    activated = (jax.nn.silu(hidden_pair[..., :FF]) * hidden_pair[..., FF:]).astype(jnp.bfloat16)
    expert_result = jnp.einsum(
        "erf,efd->erd", activated, down_w, preferred_element_type=jnp.float32
    ).astype(jnp.bfloat16)
    expert_result = expert_result.reshape(local_experts, grp_count, CAP, model_width).transpose(1, 0, 2, 3)
    returned = lax.all_to_all(
        expert_result.reshape(grp_count, local_experts * CAP, model_width),
        "grp",
        split_axis=0,
        concat_axis=0,
        tiled=True,
    ).reshape(EXPERTS * CAP, -1)
    gate_of_route = token_of_route.astype(jnp.float32).T * gates[0].reshape(-1)[None, :]
    combine = jnp.dot(
        gate_of_route,
        slot_of_route.astype(jnp.float32).T,
        precision=lax.Precision.HIGHEST,
        preferred_element_type=jnp.float32,
    )
    moe_out = jnp.dot(
        combine,
        returned.astype(jnp.float32),
        precision=lax.Precision.HIGHEST,
        preferred_element_type=jnp.float32,
    )
    hidden_out = (after_attention + moe_out).astype(jnp.bfloat16)
    return (hidden_out[None], suffix_cache[None])


def solution(mesh):
    return jax.shard_map(
        local,
        mesh=mesh,
        in_specs=(
            P("grp", "tok", None),
            P("grp", None),
            P("grp", "tok", None),
            P("grp", "tok", None),
            P("grp", "tok", None),
            P(),
            P("grp", "tok"),
            P("grp", "tok"),
            P(),
            P("tok", "grp", None),
            P("tok", "grp", None),
        ),
        out_specs=(P("grp", "tok", None), P("grp", "tok", None)),
        check_vma=False,
    )
```

```python
import jax
import jax.numpy as jnp
from jax import lax
from jax.sharding import PartitionSpec as P
from jax.experimental import pallas as pl
from jax.experimental.pallas import tpu as pltpu

HEADS = 8
KV_HEADS = 4
HEAD_DIM = 64
FF = 512
EXPERTS = 32
TOP = 8
CAP = 40


epsilon = 1e-05
score_scale = 0.015625
rope_base = 10000.0
big_negative = -1e30


def rms_scale(values, gain):
    values = values.astype(jnp.float32)
    mean_square = jnp.mean(values * values, axis=-1, keepdims=True)
    return values * lax.rsqrt(mean_square + epsilon) * gain


def request_layout(group_lengths, token_index):
    ends = jnp.cumsum(group_lengths)
    starts = ends - group_lengths
    segment = jnp.sum((token_index[:, None] >= ends[None, :]).astype(jnp.int32), axis=1)
    match = segment[:, None] == jnp.arange(group_lengths.shape[0], dtype=jnp.int32)[None, :]
    offset = token_index - jnp.sum(jnp.where(match, starts[None, :], 0), axis=1)
    return (segment, offset)


def rotate(values, position):
    half_width = values.shape[-1] // 2
    frequency = rope_base ** (-jnp.arange(half_width, dtype=jnp.float32) * 2.0 / values.shape[-1])
    angle = position.astype(jnp.float32)[:, None] * frequency[None, :]
    cosine = jnp.cos(angle)[:, None, :]
    sine = jnp.sin(angle)[:, None, :]
    first = values[..., :half_width]
    second = values[..., half_width:]
    return jnp.concatenate(
        [first * cosine - second * sine, second * cosine + first * sine], axis=-1
    )


def ring_gather(block, collective_id):
    tok_count = lax.axis_size("tok")
    rows, width = block.shape
    chips = tok_count // 2
    ahead = chips // 2
    behind = chips - 1 - ahead
    mesh_ids = pl.DeviceIdType.MESH

    def kernel(x_ref, out_ref, local_sem, send_r, send_l, send_p, recv):
        me = lax.axis_index("tok")
        grp = lax.axis_index("grp")
        z = me // 2
        core = me % 2
        right = ((z + 1) % chips) * 2 + core
        left = ((z + chips - 1) % chips) * 2 + core
        peer = z * 2 + (1 - core)
        barrier = pltpu.get_barrier_semaphore()
        for other in (right, left, peer):
            pl.semaphore_signal(barrier, 1, device_id=(grp, other), device_id_type=mesh_ids)
        pl.semaphore_wait(barrier, 3)

        def remote(src, slot, sem, target):
            return pltpu.make_async_remote_copy(
                src_ref=src,
                dst_ref=out_ref.at[slot],
                send_sem=sem,
                recv_sem=recv.at[slot],
                device_id=(grp, target),
                device_id_type=mesh_ids,
            )

        own = pltpu.make_async_copy(x_ref, out_ref.at[me], local_sem.at[0])
        own.start()
        sends = [
            remote(x_ref, me, send_p.at[0], peer),
            remote(x_ref, me, send_r.at[0], right),
            remote(x_ref, me, send_l.at[0], left),
        ]
        for c in sends:
            c.start()
        peer_count = 1
        for s in range(1, ahead + 1):
            for sign, limit, sem, target in ((-1, ahead, send_r, right), (1, behind, send_l, left)):
                if s > limit:
                    continue
                slot = ((z + chips + sign * s) % chips) * 2 + core
                remote(out_ref.at[slot], slot, sem.at[0], target).wait_recv()
                if s < limit:
                    c = remote(out_ref.at[slot], slot, sem.at[s], target)
                    c.start()
                    sends.append(c)
                c = remote(out_ref.at[slot], slot, send_p.at[peer_count], peer)
                c.start()
                sends.append(c)
                peer_count += 1
        for other_z in range(chips):
            slot = other_z * 2 + (1 - core)
            remote(out_ref.at[slot], slot, send_p.at[0], peer).wait_recv()
        own.wait()
        for c in sends:
            c.wait_send()

    block_bytes = rows * width * block.dtype.itemsize
    return pl.pallas_call(
        kernel,
        out_shape=jax.ShapeDtypeStruct((tok_count, rows, width), block.dtype),
        in_specs=[pl.BlockSpec(memory_space=pltpu.VMEM)],
        out_specs=pl.BlockSpec(memory_space=pltpu.VMEM),
        scratch_shapes=[
            pltpu.SemaphoreType.DMA((1,)),
            pltpu.SemaphoreType.DMA((ahead,)),
            pltpu.SemaphoreType.DMA((ahead,)),
            pltpu.SemaphoreType.DMA((chips,)),
            pltpu.SemaphoreType.DMA((tok_count,)),
        ],
        compiler_params=pltpu.CompilerParams(collective_id=collective_id, has_side_effects=True),
        cost_estimate=pl.CostEstimate(
            flops=0, transcendentals=0, bytes_accessed=2 * tok_count * block_bytes
        ),
    )(block)


def gather_small(blocks):
    flat = jnp.concatenate([b.reshape(-1) for b in blocks])
    width = 512
    padded_rows = -(-flat.shape[0] // (16 * width)) * 16
    flat = jnp.pad(flat, (0, padded_rows * width - flat.shape[0]))
    gathered = ring_gather(flat.reshape(padded_rows, width), 1)
    gathered = gathered.reshape(gathered.shape[0], -1)
    pieces, start = [], 0
    for b in blocks:
        size = b.size
        pieces.append(gathered[:, start : start + size].reshape((-1,) + b.shape[1:]))
        start += size
    return pieces


def gather_rows(by_columns):
    return lax.all_gather(by_columns[None], "grp", axis=0, tiled=True)


def expert_weight_slices(gate_up, down, after):
    grp_count = lax.axis_size("grp")
    tok_count = lax.axis_size("tok")
    per = tok_count // grp_count
    pairs = []
    for g in range(grp_count):
        for e in range(tok_count):
            pairs.append((g * tok_count + e, (e // per) * tok_count + per * g + e % per))
    block = jnp.concatenate([gate_up[0], down[0]], axis=0)
    probe = after.reshape(-1)[0]
    block = jnp.where(probe != probe, jnp.zeros_like(block), block)
    return lax.ppermute(block, ("grp", "tok"), pairs)


def expert_weights_full(block, after):
    block, _ = lax.optimization_barrier((block, after))
    grp_count = lax.axis_size("grp")
    tok_count = lax.axis_size("tok")
    gathered = lax.all_gather(block, "tok", axis=0, tiled=True)
    return gathered.reshape(grp_count, tok_count // grp_count, block.shape[0], block.shape[1])


def attend(carry, grouped, keys_values, allowed):
    best, total, mixed = carry
    key_count = keys_values.shape[0]
    key_width = KV_HEADS * HEAD_DIM
    key_heads = keys_values[:, :key_width].reshape(key_count, KV_HEADS, HEAD_DIM).transpose(1, 0, 2)
    value_heads = (
        keys_values[:, key_width:].reshape(key_count, KV_HEADS, HEAD_DIM).transpose(1, 0, 2)
    )
    scores = (
        jnp.einsum("kqd,knd->kqn", grouped, key_heads, preferred_element_type=jnp.float32)
        * score_scale
    )
    if allowed is not None:
        mask = allowed
        scores = jnp.where(mask[None], scores, big_negative)
    new_best = jnp.maximum(best, jnp.max(scores, axis=-1))
    factor = jnp.exp(best - new_best)
    probs = jnp.exp(scores - new_best[..., None])
    total = total * factor + jnp.sum(probs, axis=-1)
    mixed = mixed * factor[..., None] + jnp.einsum(
        "kqn,knd->kqd", probs.astype(jnp.bfloat16), value_heads, preferred_element_type=jnp.float32
    )
    return (new_best, total, mixed)


def local(
    hidden_in,
    lengths,
    prefix_cache,
    routes,
    gates,
    attn_gain,
    w_qkv,
    w_out,
    moe_gain,
    expert_gate_up,
    expert_down,
):
    tokens_here = hidden_in[0]
    tok_count = tokens_here.shape[0]
    axis_count = lax.axis_size("tok")
    device_place = lax.axis_index("tok")
    group_lengths = lengths[0]
    token_index = device_place * tok_count + jnp.arange(tok_count, dtype=jnp.int32)
    segment, offset = request_layout(group_lengths, token_index)
    position = prefix_cache.shape[1] * axis_count + offset
    query_width = HEADS * HEAD_DIM
    key_width = KV_HEADS * HEAD_DIM
    group_share = HEADS // KV_HEADS
    normed = rms_scale(tokens_here, attn_gain).astype(jnp.bfloat16)
    qkv_columns, out_columns = gather_small([w_qkv.T, w_out.T])
    packed_rows = gather_rows(jnp.concatenate([qkv_columns, out_columns], axis=1))
    qkv_width = qkv_columns.shape[1]
    qkv_weight = packed_rows[:, :, :qkv_width]
    out_weight = packed_rows[:, :, qkv_width:]
    projected = jnp.einsum(
        "ngr,gcr->nc",
        normed.reshape(tok_count, qkv_weight.shape[0], qkv_weight.shape[2]),
        qkv_weight,
        preferred_element_type=jnp.float32,
    )
    query = rotate(projected[:, :query_width].reshape(tok_count, HEADS, HEAD_DIM), position).astype(
        jnp.bfloat16
    )
    keys_new = rotate(
        projected[:, query_width : query_width + key_width].reshape(tok_count, KV_HEADS, HEAD_DIM),
        position,
    ).astype(jnp.bfloat16)
    values_new = projected[:, query_width + key_width :].astype(jnp.bfloat16)
    suffix_cache = jnp.concatenate([keys_new.reshape(tok_count, key_width), values_new], axis=1)
    row_count = tok_count * group_share
    grouped = (
        query.reshape(tok_count, KV_HEADS, group_share, HEAD_DIM)
        .transpose(1, 0, 2, 3)
        .reshape(KV_HEADS, row_count, HEAD_DIM)
    )
    start_carry = (
        jnp.full((KV_HEADS, row_count), big_negative, jnp.float32),
        jnp.zeros((KV_HEADS, row_count), jnp.float32),
        jnp.zeros((KV_HEADS, row_count, HEAD_DIM), jnp.float32),
    )
    both = ring_gather(jnp.concatenate([suffix_cache, prefix_cache[0]], axis=0), 0)
    piece = both[:, :tok_count].reshape(-1, both.shape[2])
    prefix_all = both[:, tok_count:].reshape(-1, both.shape[2])
    expert_weights = expert_weight_slices(expert_gate_up, expert_down, both)
    carry = attend(start_carry, grouped, prefix_all, None)
    key_index = jnp.arange(piece.shape[0], dtype=jnp.int32)
    key_segment, key_offset = request_layout(group_lengths, key_index)
    row_token = jnp.repeat(token_index, group_share)
    row_segment = jnp.repeat(segment, group_share)
    earlier = key_index[None, :] <= row_token[:, None]
    same_request = key_segment[None, :] == row_segment[:, None]
    carry = attend(carry, grouped, piece, earlier & same_request & (key_index[None, :] >= 0))
    best, total, mixed = carry
    attended = (mixed / total[..., None]).reshape(KV_HEADS, tok_count, group_share, HEAD_DIM)
    attended = attended.transpose(1, 0, 2, 3).reshape(tok_count, query_width).astype(jnp.bfloat16)
    projected_out = jnp.einsum(
        "ngr,gcr->nc",
        attended.reshape(tok_count, out_weight.shape[0], out_weight.shape[2]),
        out_weight,
        preferred_element_type=jnp.float32,
    )
    after_attention = tokens_here.astype(jnp.float32) + projected_out
    moe_in = rms_scale(after_attention, moe_gain).astype(jnp.bfloat16)
    model_width = moe_in.shape[1]
    flat_routes = routes[0].reshape(-1)
    onehot = (flat_routes[:, None] == jnp.arange(EXPERTS, dtype=jnp.int32)[None, :]).astype(
        jnp.int32
    )
    route_count = flat_routes.shape[0]
    lower = (
        jnp.arange(route_count, dtype=jnp.int32)[:, None]
        >= jnp.arange(route_count, dtype=jnp.int32)[None, :]
    ).astype(jnp.bfloat16)
    running = jnp.dot(lower, onehot.astype(jnp.bfloat16), preferred_element_type=jnp.float32)
    slot_rank = jnp.sum(running.astype(jnp.int32) * onehot, axis=1) - 1
    slot_index = flat_routes * CAP + slot_rank
    source_token = jnp.arange(flat_routes.shape[0], dtype=jnp.int32) // TOP
    slot_of_route = (
        slot_index[None, :] == jnp.arange(EXPERTS * CAP, dtype=jnp.int32)[:, None]
    ).astype(jnp.bfloat16)
    token_of_route = (
        source_token[:, None] == jnp.arange(tok_count, dtype=jnp.int32)[None, :]
    ).astype(jnp.bfloat16)
    slot_token = jnp.dot(slot_of_route, token_of_route, preferred_element_type=jnp.float32)
    outgoing = jnp.dot(
        slot_token.astype(jnp.bfloat16), moe_in, preferred_element_type=jnp.float32
    ).astype(jnp.bfloat16)
    grp_count = lax.axis_size("grp")
    local_experts = EXPERTS // grp_count
    full = expert_weights_full(expert_weights, piece)
    gate_rows = expert_gate_up.shape[1]
    arrived = lax.all_to_all(
        outgoing.reshape(grp_count, local_experts * CAP, model_width),
        "grp",
        split_axis=0,
        concat_axis=0,
        tiled=True,
    )
    arrived = arrived.reshape(grp_count, local_experts, CAP, model_width).transpose(1, 0, 2, 3)
    arrived = arrived.reshape(local_experts, grp_count * CAP, model_width)
    gate_up_w = full[:, :, :gate_rows].transpose(1, 0, 2, 3).reshape(local_experts, -1, model_width)
    down_w = full[:, :, gate_rows:].transpose(1, 0, 2, 3).reshape(local_experts, -1, model_width)
    hidden_pair = jnp.einsum("erd,edf->erf", arrived, gate_up_w, preferred_element_type=jnp.float32)
    activated = (jax.nn.silu(hidden_pair[..., :FF]) * hidden_pair[..., FF:]).astype(jnp.bfloat16)
    expert_result = jnp.einsum(
        "erf,efd->erd", activated, down_w, preferred_element_type=jnp.float32
    ).astype(jnp.bfloat16)
    expert_result = expert_result.reshape(local_experts, grp_count, CAP, model_width).transpose(1, 0, 2, 3)
    returned = lax.all_to_all(
        expert_result.reshape(grp_count, local_experts * CAP, model_width),
        "grp",
        split_axis=0,
        concat_axis=0,
        tiled=True,
    ).reshape(EXPERTS * CAP, -1)
    gate_of_route = token_of_route.astype(jnp.float32).T * gates[0].reshape(-1)[None, :]
    combine = jnp.dot(
        gate_of_route,
        slot_of_route.astype(jnp.float32).T,
        precision=lax.Precision.HIGHEST,
        preferred_element_type=jnp.float32,
    )
    moe_out = jnp.dot(
        combine,
        returned.astype(jnp.float32),
        precision=lax.Precision.HIGHEST,
        preferred_element_type=jnp.float32,
    )
    hidden_out = (after_attention + moe_out).astype(jnp.bfloat16)
    return (hidden_out[None], suffix_cache[None])


def solution(mesh):
    return jax.shard_map(
        local,
        mesh=mesh,
        in_specs=(
            P("grp", "tok", None),
            P("grp", None),
            P("grp", "tok", None),
            P("grp", "tok", None),
            P("grp", "tok", None),
            P(),
            P("grp", "tok"),
            P("grp", "tok"),
            P(),
            P("tok", "grp", None),
            P("tok", "grp", None),
        ),
        out_specs=(P("grp", "tok", None), P("grp", "tok", None)),
        check_vma=False,
    )
```

```python
import jax
import jax.numpy as jnp
from jax import lax
from jax.sharding import PartitionSpec as P
from jax.experimental import pallas as pl
from jax.experimental.pallas import tpu as pltpu

HEADS = 8
KV_HEADS = 4
HEAD_DIM = 64
FF = 512
EXPERTS = 32
TOP = 8
CAP = 40


epsilon = 1e-05
score_scale = 0.015625
rope_base = 10000.0
big_negative = -1e30


def rms_scale(values, gain):
    values = values.astype(jnp.float32)
    mean_square = jnp.mean(values * values, axis=-1, keepdims=True)
    return values * lax.rsqrt(mean_square + epsilon) * gain


def request_layout(group_lengths, token_index):
    ends = jnp.cumsum(group_lengths)
    starts = ends - group_lengths
    segment = jnp.sum((token_index[:, None] >= ends[None, :]).astype(jnp.int32), axis=1)
    match = segment[:, None] == jnp.arange(group_lengths.shape[0], dtype=jnp.int32)[None, :]
    offset = token_index - jnp.sum(jnp.where(match, starts[None, :], 0), axis=1)
    return (segment, offset)


def rotate(values, position):
    half_width = values.shape[-1] // 2
    frequency = rope_base ** (-jnp.arange(half_width, dtype=jnp.float32) * 2.0 / values.shape[-1])
    angle = position.astype(jnp.float32)[:, None] * frequency[None, :]
    cosine = jnp.cos(angle)[:, None, :]
    sine = jnp.sin(angle)[:, None, :]
    first = values[..., :half_width]
    second = values[..., half_width:]
    return jnp.concatenate(
        [first * cosine - second * sine, second * cosine + first * sine], axis=-1
    )


def ring_gather(block, collective_id):
    tok_count = lax.axis_size("tok")
    rows, width = block.shape
    chips = tok_count // 2
    ahead = chips // 2
    behind = chips - 1 - ahead
    mesh_ids = pl.DeviceIdType.MESH

    def kernel(x_ref, out_ref, local_sem, send_r, send_l, send_p, recv):
        me = lax.axis_index("tok")
        grp = lax.axis_index("grp")
        z = me // 2
        core = me % 2
        right = ((z + 1) % chips) * 2 + core
        left = ((z + chips - 1) % chips) * 2 + core
        peer = z * 2 + (1 - core)
        barrier = pltpu.get_barrier_semaphore()
        for other in (right, left, peer):
            pl.semaphore_signal(barrier, 1, device_id=(grp, other), device_id_type=mesh_ids)
        pl.semaphore_wait(barrier, 3)

        def remote(src, slot, sem, target):
            return pltpu.make_async_remote_copy(
                src_ref=src,
                dst_ref=out_ref.at[slot],
                send_sem=sem,
                recv_sem=recv.at[slot],
                device_id=(grp, target),
                device_id_type=mesh_ids,
            )

        own = pltpu.make_async_copy(x_ref, out_ref.at[me], local_sem.at[0])
        own.start()
        sends = [
            remote(x_ref, me, send_p.at[0], peer),
            remote(x_ref, me, send_r.at[0], right),
            remote(x_ref, me, send_l.at[0], left),
        ]
        for c in sends:
            c.start()
        peer_count = 1
        for s in range(1, ahead + 1):
            for sign, limit, sem, target in ((-1, ahead, send_r, right), (1, behind, send_l, left)):
                if s > limit:
                    continue
                slot = ((z + chips + sign * s) % chips) * 2 + core
                remote(out_ref.at[slot], slot, sem.at[0], target).wait_recv()
                if s < limit:
                    c = remote(out_ref.at[slot], slot, sem.at[s], target)
                    c.start()
                    sends.append(c)
                c = remote(out_ref.at[slot], slot, send_p.at[peer_count], peer)
                c.start()
                sends.append(c)
                peer_count += 1
        for other_z in range(chips):
            slot = other_z * 2 + (1 - core)
            remote(out_ref.at[slot], slot, send_p.at[0], peer).wait_recv()
        own.wait()
        for c in sends:
            c.wait_send()

    block_bytes = rows * width * block.dtype.itemsize
    return pl.pallas_call(
        kernel,
        out_shape=jax.ShapeDtypeStruct((tok_count, rows, width), block.dtype),
        in_specs=[pl.BlockSpec(memory_space=pltpu.VMEM)],
        out_specs=pl.BlockSpec(memory_space=pltpu.VMEM),
        scratch_shapes=[
            pltpu.SemaphoreType.DMA((1,)),
            pltpu.SemaphoreType.DMA((ahead,)),
            pltpu.SemaphoreType.DMA((ahead,)),
            pltpu.SemaphoreType.DMA((chips,)),
            pltpu.SemaphoreType.DMA((tok_count,)),
        ],
        compiler_params=pltpu.CompilerParams(collective_id=collective_id, has_side_effects=True),
        cost_estimate=pl.CostEstimate(
            flops=0, transcendentals=0, bytes_accessed=2 * tok_count * block_bytes
        ),
    )(block)


def gather_small(blocks):
    flat = jnp.concatenate([b.reshape(-1) for b in blocks])
    width = 512
    padded_rows = -(-flat.shape[0] // (16 * width)) * 16
    flat = jnp.pad(flat, (0, padded_rows * width - flat.shape[0]))
    gathered = ring_gather(flat.reshape(padded_rows, width), 1)
    gathered = gathered.reshape(gathered.shape[0], -1)
    pieces, start = [], 0
    for b in blocks:
        size = b.size
        pieces.append(gathered[:, start : start + size].reshape((-1,) + b.shape[1:]))
        start += size
    return pieces


def gather_rows(by_columns):
    return lax.all_gather(by_columns[None], "grp", axis=0, tiled=True)


def expert_weight_slices(gate_up, down):
    grp_count = lax.axis_size("grp")
    tok_count = lax.axis_size("tok")
    per = tok_count // grp_count
    pairs = []
    for g in range(grp_count):
        for e in range(tok_count):
            pairs.append((g * tok_count + e, (e // per) * tok_count + per * g + e % per))
    block = jnp.concatenate([gate_up[0], down[0]], axis=0)
    return lax.ppermute(block, ("grp", "tok"), pairs)


def expert_weights_full(block, after):
    block, _ = lax.optimization_barrier((block, after))
    grp_count = lax.axis_size("grp")
    tok_count = lax.axis_size("tok")
    gathered = lax.all_gather(block, "tok", axis=0, tiled=True)
    return gathered.reshape(grp_count, tok_count // grp_count, block.shape[0], block.shape[1])


def attend(carry, grouped, keys_values, allowed):
    best, total, mixed = carry
    key_count = keys_values.shape[0]
    key_width = KV_HEADS * HEAD_DIM
    key_heads = keys_values[:, :key_width].reshape(key_count, KV_HEADS, HEAD_DIM).transpose(1, 0, 2)
    value_heads = (
        keys_values[:, key_width:].reshape(key_count, KV_HEADS, HEAD_DIM).transpose(1, 0, 2)
    )
    scores = (
        jnp.einsum("kqd,knd->kqn", grouped, key_heads, preferred_element_type=jnp.float32)
        * score_scale
    )
    if allowed is not None:
        mask = allowed
        scores = jnp.where(mask[None], scores, big_negative)
    new_best = jnp.maximum(best, jnp.max(scores, axis=-1))
    factor = jnp.exp(best - new_best)
    probs = jnp.exp(scores - new_best[..., None])
    total = total * factor + jnp.sum(probs, axis=-1)
    mixed = mixed * factor[..., None] + jnp.einsum(
        "kqn,knd->kqd", probs.astype(jnp.bfloat16), value_heads, preferred_element_type=jnp.float32
    )
    return (new_best, total, mixed)


def local(
    hidden_in,
    lengths,
    prefix_cache,
    routes,
    gates,
    attn_gain,
    w_qkv,
    w_out,
    moe_gain,
    expert_gate_up,
    expert_down,
):
    tokens_here = hidden_in[0]
    tok_count = tokens_here.shape[0]
    axis_count = lax.axis_size("tok")
    device_place = lax.axis_index("tok")
    group_lengths = lengths[0]
    token_index = device_place * tok_count + jnp.arange(tok_count, dtype=jnp.int32)
    segment, offset = request_layout(group_lengths, token_index)
    position = prefix_cache.shape[1] * axis_count + offset
    query_width = HEADS * HEAD_DIM
    key_width = KV_HEADS * HEAD_DIM
    group_share = HEADS // KV_HEADS
    normed = rms_scale(tokens_here, attn_gain).astype(jnp.bfloat16)
    qkv_columns, out_columns = gather_small([w_qkv.T, w_out.T])
    packed_rows = gather_rows(jnp.concatenate([qkv_columns, out_columns], axis=1))
    qkv_width = qkv_columns.shape[1]
    qkv_weight = packed_rows[:, :, :qkv_width]
    out_weight = packed_rows[:, :, qkv_width:]
    expert_weights = expert_weight_slices(expert_gate_up, expert_down)
    projected = jnp.einsum(
        "ngr,gcr->nc",
        normed.reshape(tok_count, qkv_weight.shape[0], qkv_weight.shape[2]),
        qkv_weight,
        preferred_element_type=jnp.float32,
    )
    query = rotate(projected[:, :query_width].reshape(tok_count, HEADS, HEAD_DIM), position).astype(
        jnp.bfloat16
    )
    keys_new = rotate(
        projected[:, query_width : query_width + key_width].reshape(tok_count, KV_HEADS, HEAD_DIM),
        position,
    ).astype(jnp.bfloat16)
    values_new = projected[:, query_width + key_width :].astype(jnp.bfloat16)
    suffix_cache = jnp.concatenate([keys_new.reshape(tok_count, key_width), values_new], axis=1)
    row_count = tok_count * group_share
    grouped = (
        query.reshape(tok_count, KV_HEADS, group_share, HEAD_DIM)
        .transpose(1, 0, 2, 3)
        .reshape(KV_HEADS, row_count, HEAD_DIM)
    )
    start_carry = (
        jnp.full((KV_HEADS, row_count), big_negative, jnp.float32),
        jnp.zeros((KV_HEADS, row_count), jnp.float32),
        jnp.zeros((KV_HEADS, row_count, HEAD_DIM), jnp.float32),
    )
    both = ring_gather(jnp.concatenate([suffix_cache, prefix_cache[0]], axis=0), 0)
    piece = both[:, :tok_count].reshape(-1, both.shape[2])
    prefix_all = both[:, tok_count:].reshape(-1, both.shape[2])
    carry = attend(start_carry, grouped, prefix_all, None)
    key_index = jnp.arange(piece.shape[0], dtype=jnp.int32)
    key_segment, key_offset = request_layout(group_lengths, key_index)
    row_token = jnp.repeat(token_index, group_share)
    row_segment = jnp.repeat(segment, group_share)
    earlier = key_index[None, :] <= row_token[:, None]
    same_request = key_segment[None, :] == row_segment[:, None]
    carry = attend(carry, grouped, piece, earlier & same_request & (key_index[None, :] >= 0))
    best, total, mixed = carry
    attended = (mixed / total[..., None]).reshape(KV_HEADS, tok_count, group_share, HEAD_DIM)
    attended = attended.transpose(1, 0, 2, 3).reshape(tok_count, query_width).astype(jnp.bfloat16)
    projected_out = jnp.einsum(
        "ngr,gcr->nc",
        attended.reshape(tok_count, out_weight.shape[0], out_weight.shape[2]),
        out_weight,
        preferred_element_type=jnp.float32,
    )
    after_attention = tokens_here.astype(jnp.float32) + projected_out
    moe_in = rms_scale(after_attention, moe_gain).astype(jnp.bfloat16)
    model_width = moe_in.shape[1]
    flat_routes = routes[0].reshape(-1)
    onehot = (flat_routes[:, None] == jnp.arange(EXPERTS, dtype=jnp.int32)[None, :]).astype(
        jnp.int32
    )
    route_count = flat_routes.shape[0]
    lower = (
        jnp.arange(route_count, dtype=jnp.int32)[:, None]
        >= jnp.arange(route_count, dtype=jnp.int32)[None, :]
    ).astype(jnp.bfloat16)
    running = jnp.dot(lower, onehot.astype(jnp.bfloat16), preferred_element_type=jnp.float32)
    slot_rank = jnp.sum(running.astype(jnp.int32) * onehot, axis=1) - 1
    slot_index = flat_routes * CAP + slot_rank
    source_token = jnp.arange(flat_routes.shape[0], dtype=jnp.int32) // TOP
    slot_of_route = (
        slot_index[None, :] == jnp.arange(EXPERTS * CAP, dtype=jnp.int32)[:, None]
    ).astype(jnp.bfloat16)
    token_of_route = (
        source_token[:, None] == jnp.arange(tok_count, dtype=jnp.int32)[None, :]
    ).astype(jnp.bfloat16)
    slot_token = jnp.dot(slot_of_route, token_of_route, preferred_element_type=jnp.float32)
    outgoing = jnp.dot(
        slot_token.astype(jnp.bfloat16), moe_in, preferred_element_type=jnp.float32
    ).astype(jnp.bfloat16)
    grp_count = lax.axis_size("grp")
    local_experts = EXPERTS // grp_count
    full = expert_weights_full(expert_weights, both)
    gate_rows = expert_gate_up.shape[1]
    arrived = lax.all_to_all(
        outgoing.reshape(grp_count, local_experts * CAP, model_width),
        "grp",
        split_axis=0,
        concat_axis=0,
        tiled=True,
    )
    arrived = arrived.reshape(grp_count, local_experts, CAP, model_width).transpose(1, 0, 2, 3)
    arrived = arrived.reshape(local_experts, grp_count * CAP, model_width)
    gate_up_w = full[:, :, :gate_rows].transpose(1, 0, 2, 3).reshape(local_experts, -1, model_width)
    down_w = full[:, :, gate_rows:].transpose(1, 0, 2, 3).reshape(local_experts, -1, model_width)
    hidden_pair = jnp.einsum("erd,edf->erf", arrived, gate_up_w, preferred_element_type=jnp.float32)
    activated = (jax.nn.silu(hidden_pair[..., :FF]) * hidden_pair[..., FF:]).astype(jnp.bfloat16)
    expert_result = jnp.einsum(
        "erf,efd->erd", activated, down_w, preferred_element_type=jnp.float32
    ).astype(jnp.bfloat16)
    expert_result = expert_result.reshape(local_experts, grp_count, CAP, model_width).transpose(1, 0, 2, 3)
    returned = lax.all_to_all(
        expert_result.reshape(grp_count, local_experts * CAP, model_width),
        "grp",
        split_axis=0,
        concat_axis=0,
        tiled=True,
    ).reshape(EXPERTS * CAP, -1)
    gate_of_route = token_of_route.astype(jnp.float32).T * gates[0].reshape(-1)[None, :]
    combine = jnp.dot(
        gate_of_route,
        slot_of_route.astype(jnp.float32).T,
        precision=lax.Precision.HIGHEST,
        preferred_element_type=jnp.float32,
    )
    moe_out = jnp.dot(
        combine,
        returned.astype(jnp.float32),
        precision=lax.Precision.HIGHEST,
        preferred_element_type=jnp.float32,
    )
    hidden_out = (after_attention + moe_out).astype(jnp.bfloat16)
    return (hidden_out[None], suffix_cache[None])


def solution(mesh):
    return jax.shard_map(
        local,
        mesh=mesh,
        in_specs=(
            P("grp", "tok", None),
            P("grp", None),
            P("grp", "tok", None),
            P("grp", "tok", None),
            P("grp", "tok", None),
            P(),
            P("grp", "tok"),
            P("grp", "tok"),
            P(),
            P("tok", "grp", None),
            P("tok", "grp", None),
        ),
        out_specs=(P("grp", "tok", None), P("grp", "tok", None)),
        check_vma=False,
    )
```
